256 devices in a mesh: img: 32 (over z_lo, y, core), slab: 8 (over x, z_hi).
Axes of the slice: x: 4, y: 4, z: 8 (z_hi: 2, z_lo: 4; z = z_hi * 4 + z_lo), core: 2. Of those that a mesh axis runs over, the one named last changes fastest.
Arguments:
- images: bfloat16 [256, 2, 384, 384], P('img'), may hold values from -6 to 6
- volume: float32 [2, 384, 384, 384], P(None, 'slab', 'img'), may hold values from -6 to 6
- orient: int32 [256], P('img'), may hold values from 1 to 4095
- prior_shift: int32 [256], P('img'), may hold values from 0 to 63
- noise_var: float32 [256], P('img'), may hold values from 1.5 to 2000
Outputs:
- density: float32 [384, 384, 384], P('img', 'slab')
The draws below stay inside these ranges and needn't reach their ends.
All inputs are finite; a program needn't handle non-finite values.
Results may differ from the reference program's by a relative error of at most 0.0003.
The reference program's roundings to bfloat16 on the way (of `slices` and `weighted`) count: a program that leaves them out, or rounds other values in their place, can miss the bound.
Values may be sent and summed in bfloat16 or wider, within the bound.
A program may use at most 128 MiB of HBM per device.

```python
import math
import jax
import jax.numpy as jnp
from jax import lax

L = 384
GRID = 16
PRIOR = 8
NORIENT = 4096
NIMG = 256


def draw_noise_var(key, part):
    lowest = 150.0
    highest = 2000.0
    uniform_draw = jax.random.uniform(key, (NIMG,), jnp.float32)
    return jnp.exp(math.log(lowest) + uniform_draw * (math.log(highest) - math.log(lowest)))


def set_ends(array, own_key, smallest, high):
    longest = array.shape.index(max(array.shape))
    spots = []
    for shift in (0, 1):
        where = [jax.random.randint(jax.random.fold_in(own_key, axis), (), 0, length) for axis, length in enumerate(array.shape)]
        where[longest] = (where[longest] + shift) % array.shape[longest]
        spots.append(tuple(where))
    return array.at[spots[0]].set(smallest).at[spots[1]].set(high)


def block_levels(own_key, shape, shards, least, top_value):
    gain, own = 1.0, jax.random.fold_in(own_key, 6)
    for position, blocks in shards:
        heights = jnp.exp(jax.random.uniform(jax.random.fold_in(own, position), (blocks,), jnp.float32, least / len(shards), top_value / len(shards)))
        gain = gain * jnp.repeat(heights, shape[position] // blocks).reshape([-1 if axis == position else 1 for axis in range(len(shape))])
    return gain


def bell_draw(key, dims, deviation, bound, cuts=(), kind=jnp.bfloat16):
    values = jax.random.normal(key, dims, jnp.float32) * deviation
    if len(cuts) > 0:
        values = block_levels(key, dims, cuts, -0.22, 0.18) * values
    return jnp.clip(values, min=-bound, max=bound).astype(kind)


def setup_inputs(seed: int = 0) -> dict:
    keys = jax.random.split(jax.random.key(seed), 6)
    return {
        "images": bell_draw(keys[0], (NIMG, 2, L, L), 1.0, 6.0, ((0, 32),)),
        "volume": bell_draw(keys[1], (2, L, L, L), 1.0, 6.0, ((1, 8), (2, 32)), jnp.float32),
        "orient": set_ends(jax.random.randint(keys[2], (NIMG,), 1, NORIENT), jax.random.fold_in(keys[2], 1), 1, NORIENT - 1).astype(jnp.int32),
        "prior_shift": set_ends(jax.random.randint(keys[3], (NIMG,), 0, PRIOR * PRIOR), jax.random.fold_in(keys[3], 1), 0, (PRIOR * PRIOR) - 1).astype(jnp.int32),
        "noise_var": draw_noise_var(jax.random.fold_in(keys[5], 71), 0),
    }


precise = lax.Precision.HIGHEST


def plane_index(orients, first_row, row_count, extent):
    centre = extent // 2
    half_grid = NORIENT // 2
    row_ids = first_row + jnp.arange(row_count, dtype=jnp.int32)
    return centre + jnp.floor_divide((row_ids[None, :] - centre) * (orients[:, None] - half_grid), half_grid)


def phase_angles(offsets, first_row, row_count, extent):
    row_ids = first_row + jnp.arange(row_count, dtype=jnp.int32)
    shifted = offsets[:, None] + jnp.arange(GRID, dtype=jnp.int32)[None, :] - GRID // 2
    phase_turns = jnp.mod((row_ids[None, :, None] - extent // 2) * shifted[:, None, :], extent)
    return phase_turns.astype(jnp.float32) * (2.0 * math.pi / extent)


def tables(offsets_rows, offsets_cols, first_row, row_count, extent):
    rows_angle = phase_angles(offsets_rows, first_row, row_count, extent)
    cols_angle = phase_angles(offsets_cols, 0, extent, extent)
    return jnp.cos(rows_angle), jnp.sin(rows_angle), jnp.cos(cols_angle), jnp.sin(cols_angle)


def partial_scores(slices, images, phase_waves):
    cos_rows, sin_rows, cos_cols, sin_cols = phase_waves
    slice_real = slices[:, 0].astype(jnp.float32)
    slice_imag = slices[:, 1].astype(jnp.float32)
    image_real = images[:, 0].astype(jnp.float32)
    image_imag = images[:, 1].astype(jnp.float32)
    prod_real = slice_real * image_real + slice_imag * image_imag
    prod_imag = slice_real * image_imag - slice_imag * image_real
    line_real = jnp.einsum("njx,nxb->njb", prod_real, cos_cols, precision=precise) - jnp.einsum("njx,nxb->njb", prod_imag, sin_cols, precision=precise)
    line_imag = jnp.einsum("njx,nxb->njb", prod_real, sin_cols, precision=precise) + jnp.einsum("njx,nxb->njb", prod_imag, cos_cols, precision=precise)
    return jnp.einsum("nja,njb->nab", cos_rows, line_real, precision=precise) - jnp.einsum("nja,njb->nab", sin_rows, line_imag, precision=precise)


def posterior(scores, noise_var):
    logits = scores / (2.0 * noise_var[:, None, None])
    highest = jnp.max(logits, axis=(1, 2), keepdims=True)
    expo = jnp.exp(logits - highest)
    return expo / jnp.sum(expo, axis=(1, 2), keepdims=True)


def weight_images(images, weights, phase_waves):
    cos_rows, sin_rows, cos_cols, sin_cols = phase_waves
    rows_real = jnp.einsum("nja,nab->njb", cos_rows, weights, precision=precise)
    rows_imag = -jnp.einsum("nja,nab->njb", sin_rows, weights, precision=precise)
    filt_real = jnp.einsum("njb,nxb->njx", rows_real, cos_cols, precision=precise) + jnp.einsum("njb,nxb->njx", rows_imag, sin_cols, precision=precise)
    filt_imag = jnp.einsum("njb,nxb->njx", rows_imag, cos_cols, precision=precise) - jnp.einsum("njb,nxb->njx", rows_real, sin_cols, precision=precise)
    image_real = images[:, 0].astype(jnp.float32)
    image_imag = images[:, 1].astype(jnp.float32)
    out_real = image_real * filt_real - image_imag * filt_imag
    out_imag = image_real * filt_imag + image_imag * filt_real
    return jnp.stack([out_real, out_imag], axis=1).astype(jnp.bfloat16)


def reference(images, volume, orient, prior_shift, noise_var):
    extent = L
    row_ids = jnp.arange(extent, dtype=jnp.int32)
    planes = plane_index(orient, 0, extent, extent)

    def per_image(packed):
        picture, plane_row, shift_one, noise_level = packed
        slices = volume[:, plane_row, row_ids, :].astype(jnp.bfloat16)[None]
        offsets = shift_one[None]
        phase_waves = tables(offsets // PRIOR - PRIOR // 2, offsets % PRIOR - PRIOR // 2, 0, extent, extent)
        scores = partial_scores(slices, picture[None], phase_waves)
        return weight_images(picture[None], posterior(scores, noise_level[None]), phase_waves)[0]

    weighted = lax.map(per_image, (images, planes, prior_shift, noise_var))
    row_grid = jnp.broadcast_to(row_ids[None, :], planes.shape)
    backproj = jnp.zeros(volume.shape, jnp.float32).at[:, planes, row_grid, :].add(jnp.moveaxis(weighted, 1, 0).astype(jnp.float32))
    hit_count = jnp.zeros((extent, extent), jnp.float32).at[planes, row_grid].add(1.0)
    merged = (backproj + volume) / (hit_count + 1.0)[None, :, :, None]
    spectrum = lax.complex(merged[0], merged[1])
    inverse = jnp.fft.ifftn(spectrum)
    parity = (row_ids[:, None, None] + row_ids[None, :, None] + row_ids[None, None, :]) % 2
    sign_flip = (1 - 2 * parity).astype(jnp.float32)
    density = jnp.real(inverse) * sign_flip * (extent ** 3 * extent ** -1.5)
    return jnp.transpose(density, (2, 1, 0))
```

```python
import math

import jax
import jax.numpy as jnp
import numpy as np
from jax import lax
from jax.experimental import pallas as pl
from jax.experimental.pallas import tpu as pltpu
from jax.sharding import PartitionSpec as P

GRID = 16
PRIOR = 8
NORIENT = 4096
L = 384
HALF = L // 2
PRECISE = lax.Precision.HIGHEST
F32 = jnp.float32
BF16 = jnp.bfloat16
VLIM = 60 * 1024 * 1024

NT = (((1,), (1,)), ((), ()))
NN = (((1,), (0,)), ((), ()))


def wave(product):
    angle = 2.0 * math.pi * np.mod(product, L) / L
    return np.cos(angle), np.sin(angle)


def make_tables():
    ids = np.arange(L)
    lane = np.arange(GRID * GRID)
    col_c, col_s = wave((ids[:, None] - HALF) * (lane % GRID)[None, :])
    prior = np.arange(PRIOR)
    pr_c, pr_s = wave((prior[:, None] - PRIOR // 2 - GRID // 2) * (ids[None, :] - HALF))
    prior_cols = np.concatenate([pr_c, pr_s], axis=1)
    ct, st = wave(ids[:, None] * (ids[None, :] - HALF))
    ex = np.concatenate(
        [np.concatenate([ct, -st], axis=1), np.concatenate([st, ct], axis=1)], axis=0
    )
    local = np.arange(192)
    real_rows, imag_rows = [], []
    for zh in range(2):
        kz = 96 * (local // 48) + 48 * zh + local % 48
        c, s = ct[:, kz], st[:, kz]
        real_rows += [c[:, :128], c[:, 128:], -s[:, 128:], -s[:, :128]]
        imag_rows += [s[:, :128], s[:, 128:], c[:, 128:], c[:, :128]]
    ez = np.concatenate(
        [np.concatenate(real_rows, axis=1), np.concatenate(imag_rows, axis=1)], axis=0
    )
    ey = []
    for core in range(2):
        ky = 24 * (local // 12) + 12 * core + local % 12
        ey.append(np.concatenate([ct[:, ky], -st[:, ky]], axis=1) * L ** (-1.5))
    as_f32 = lambda a: np.asarray(a, np.float32)
    return tuple(map(as_f32, (col_c, col_s, prior_cols, ex, ez, np.stack(ey))))


def place():
    img = lax.axis_index("img")
    slab = lax.axis_index("slab")
    return img, slab, img // 8, slab // 2, slab % 2


def remote(src, dst, send, recv, img, slab):
    return pltpu.make_async_remote_copy(
        src_ref=src,
        dst_ref=dst,
        send_sem=send,
        recv_sem=recv,
        device_id={"img": img, "slab": slab},
        device_id_type=pl.DeviceIdType.MESH,
    )


def spread_kernel(a_ref, v_ref, m_ref, xd_ref, vd_ref, md_ref, send, recv, local):
    img, slab, zl, x, zh = place()
    z = zh * 4 + zl
    yc = img % 8
    for k in range(1, 4):
        to = (x + k) % 4
        remote(
            v_ref.at[:, pl.ds(3 * to, 3)], vd_ref.at[x], send.at[1], recv.at[1], img, 2 * to + zh
        ).start()

    def meta_step(k, carry):
        to = (img + k) % 32
        remote(m_ref, md_ref.at[img], send.at[2], recv.at[2], to, slab).start()
        return carry

    lax.fori_loop(1, 32, meta_step, 0)
    for d in (2, 6, 1, 7, 0):
        to_z = (z + d) % 8

        def step(k, carry, d=d, to_z=to_z):
            to = (to_z % 4) * 8 + (yc + k) % 8
            to_slab = 2 * x + to_z // 4
            if d in (2, 6):
                c = 0 if d == 2 else 1
                remote(
                    a_ref.at[to, :, c], xd_ref.at[img, :, c], send.at[0], recv.at[0], to, to_slab
                ).start()
            else:
                remote(
                    a_ref.at[to], xd_ref.at[img], send.at[0], recv.at[0], to, to_slab
                ).start()
            return carry

        lax.fori_loop(1 if d == 0 else 0, 8, step, 0)
    own = (
        pltpu.make_async_copy(a_ref.at[img], xd_ref.at[img], local.at[0]),
        pltpu.make_async_copy(v_ref.at[:, pl.ds(3 * x, 3)], vd_ref.at[x], local.at[1]),
        pltpu.make_async_copy(m_ref, md_ref.at[img], local.at[2]),
    )
    for copy in own:
        copy.start()
    for copy in own:
        copy.wait()
    first = (a_ref.at[pl.ds(0, 31)], vd_ref.at[pl.ds(0, 3)], md_ref.at[pl.ds(0, 31)])
    into = (xd_ref.at[pl.ds(0, 31)], vd_ref.at[pl.ds(0, 3)], md_ref.at[pl.ds(0, 31)])
    for n in range(3):
        pltpu.make_async_copy(first[n], first[n], send.at[n]).wait()
        pltpu.make_async_copy(into[n], into[n], recv.at[n]).wait()


def image_values(md_ref):
    meta = md_ref[...].reshape(256, 128)
    orient = meta[:, 0:1].astype(jnp.int32)
    prior = meta[:, 1:2].astype(jnp.int32)
    return meta, orient, prior


def rotations(prior, pr_ref, rr_ref):
    ids = lax.broadcasted_iota(jnp.int32, (256, PRIOR), 1)
    in_cols = jnp.where((prior & 7) == ids, 1.0, 0.0).astype(F32)
    in_rows = jnp.where((prior >> 3) == ids, 1.0, 0.0).astype(F32)
    cols = lax.dot_general(in_cols, pr_ref[...], NN, precision=PRECISE, preferred_element_type=F32)
    rows = lax.dot_general(in_rows, rr_ref[...], NN, precision=PRECISE, preferred_element_type=F32)
    return cols, rows


def turned(cols, rows, j):
    cr, ci = cols[:, :L], cols[:, L:]
    ar, ai = rows[:, j : j + 1], rows[:, 3 + j : 4 + j]
    return cr * ar - ci * ai, cr * ai + ci * ar


def cell_waves(cc_ref, cs_ref, rt_ref, j):
    rc, rs = rt_ref[j : j + 1, :], rt_ref[3 + j : 4 + j, :]
    cc, cs = cc_ref[...], cs_ref[...]
    return cc * rc - cs * rs, cs * rc + cc * rs


def plane_ids(index, zh):
    block = (
        (index >= 48).astype(jnp.int32)
        + (index >= 96).astype(jnp.int32)
        + (index >= 144).astype(jnp.int32)
    )
    return index + 48 * block + 48 * zh


def planes_of(orient, row):
    return (((row - HALF) * (orient - NORIENT // 2)) >> 11) + HALF


def picture(xd_ref, j, c):
    return xd_ref[:, j, c].astype(F32).reshape(256, L)


def map_rows(vd_ref, j, c):
    return jnp.concatenate([vd_ref[b, c, j] for b in range(4)], axis=0)


def score_kernel(xd_ref, vd_ref, md_ref, cc_ref, cs_ref, pr_ref, rt_ref, rr_ref, out_ref):
    img, slab, zl, x, zh = place()
    meta, orient, prior = image_values(md_ref)
    cols, rows = rotations(prior, pr_ref, rr_ref)
    zid = plane_ids(lax.broadcasted_iota(jnp.int32, (1, 192), 1), zh)
    total = jnp.zeros((256, 256), F32)
    for j in range(3):
        row = 12 * img + 3 * x + j
        pick = jnp.where(planes_of(orient, row) == zid, 1.0, 0.0).astype(BF16)
        sr, si = (
            lax.dot_general(
                pick, map_rows(vd_ref, j, c).astype(BF16), NN, preferred_element_type=F32
            )
            for c in range(2)
        )
        xr, xi = picture(xd_ref, j, 0), picture(xd_ref, j, 1)
        pr = sr * xr + si * xi
        pi = sr * xi - si * xr
        tr, ti = turned(cols, rows, j)
        wr, wi = cell_waves(cc_ref, cs_ref, rt_ref, j)
        lhs = jnp.concatenate([pr * tr - pi * ti, pr * ti + pi * tr], axis=1)
        rhs = jnp.concatenate([wr, -wi], axis=0)
        total += lax.dot_general(lhs, rhs, NN, precision=PRECISE, preferred_element_type=F32)
    out_ref[...] = total.reshape(32, 8, 256)


def posterior_kernel(sc_ref, m_ref, w_ref, parts, sums, send, recv, local):
    img, slab, zl, x, zh = place()

    def step_a(k, carry):
        to = (img + k) % 32
        remote(sc_ref.at[to], parts.at[img], send.at[0], recv.at[0], to, slab).start()
        return carry

    lax.fori_loop(1, 32, step_a, 0)
    own = pltpu.make_async_copy(sc_ref.at[img], parts.at[img], local.at[0])
    own.start()
    own.wait()
    pltpu.make_async_copy(parts.at[pl.ds(0, 31)], parts.at[pl.ds(0, 31)], recv.at[0]).wait()
    sums[slab] = jnp.sum(parts[...], axis=0)

    def step_b(k, carry):
        to = (slab + k) % 8
        remote(sums.at[slab], sums.at[slab], send.at[1], recv.at[1], img, to).start()
        return carry

    lax.fori_loop(1, 8, step_b, 0)
    pltpu.make_async_copy(sums.at[pl.ds(0, 7)], sums.at[pl.ds(0, 7)], recv.at[1]).wait()
    logits = jnp.sum(sums[...], axis=0) / (2.0 * m_ref[:, 2:3])
    expo = jnp.exp(logits - jnp.max(logits, axis=1, keepdims=True))
    w_ref[img] = expo / jnp.sum(expo, axis=1, keepdims=True)

    def step_c(k, carry):
        to = (img + k) % 32
        remote(w_ref.at[img], w_ref.at[img], send.at[2], recv.at[2], to, slab).start()
        return carry

    lax.fori_loop(1, 32, step_c, 0)
    pltpu.make_async_copy(w_ref.at[pl.ds(0, 31)], w_ref.at[pl.ds(0, 31)], recv.at[2]).wait()
    pltpu.make_async_copy(parts.at[pl.ds(0, 31)], parts.at[pl.ds(0, 31)], send.at[0]).wait()
    pltpu.make_async_copy(sums.at[pl.ds(0, 7)], sums.at[pl.ds(0, 7)], send.at[1]).wait()
    pltpu.make_async_copy(w_ref.at[pl.ds(0, 31)], w_ref.at[pl.ds(0, 31)], send.at[2]).wait()


def merge_kernel(
    w_ref, xd_ref, vd_ref, md_ref, cc_ref, cs_ref, pr_ref, rt_ref, rr_ref, ex_ref, out_ref
):
    img, slab, zl, x, zh = place()
    meta, orient, prior = image_values(md_ref)
    orient_row = meta.T[0:1, :].astype(jnp.int32)
    cols, rows = rotations(prior, pr_ref, rr_ref)
    zid = plane_ids(lax.broadcasted_iota(jnp.int32, (192, 1), 0), zh)
    weights = w_ref[...].reshape(256, 256)
    for j in range(3):
        row = 12 * img + 3 * x + j
        wr, wi = cell_waves(cc_ref, cs_ref, rt_ref, j)
        rhs = jnp.concatenate([wr, wi], axis=0)
        f = lax.dot_general(weights, rhs, NT, precision=PRECISE, preferred_element_type=F32)
        fr, fi = f[:, :L], f[:, L:]
        tr, ti = turned(cols, rows, j)
        gr = tr * fr - ti * fi
        gi = tr * fi + ti * fr
        xr, xi = picture(xd_ref, j, 0), picture(xd_ref, j, 1)
        hit = jnp.where(planes_of(orient_row, row) == zid, 1.0, 0.0).astype(F32)
        scale = jnp.sum(hit, axis=1, keepdims=True) + 1.0
        put = hit.astype(BF16)
        merged = []
        for c, part in enumerate((xr * gr + xi * gi, xi * gr - xr * gi)):
            back = lax.dot_general(put, part.astype(BF16), NN, preferred_element_type=F32)
            merged.append((back + map_rows(vd_ref, j, c)) / scale)
        lhs = jnp.concatenate(merged, axis=1)
        g = lax.dot_general(ex_ref[...], lhs, NT, precision=PRECISE, preferred_element_type=F32)
        g_re, g_im = g[:L], g[L:]
        tiles = (
            g_re[:, :128],
            jnp.concatenate([g_re[:, 128:], g_im[:, 128:]], axis=1),
            g_im[:, :128],
        )
        for t in range(3):
            out_ref[t, pl.ds(j, L, stride=3), :] = tiles[t]


def planes_kernel(g_ref, r_ref, send, recv, local):
    img, slab, zl, x, zh = place()
    q, core = img // 2, img % 2
    me = q * 8 + slab
    mine = r_ref.at[pl.ds(3 * zh, 3), :, 4 * q + x]

    def step(k, carry):
        to = (me + k) % 128
        remote(
            g_ref.at[:, pl.ds(3 * to, 3)], mine, send.at[0], recv.at[0], 2 * (to // 8) + core, to % 8
        ).start()
        return carry

    lax.fori_loop(1, 128, step, 0)
    own = pltpu.make_async_copy(g_ref.at[:, pl.ds(3 * me, 3)], mine, local.at[0])
    own.start()
    own.wait()
    most = g_ref.at[:, pl.ds(0, 381)]
    pltpu.make_async_copy(most, most, recv.at[0]).wait()
    pltpu.make_async_copy(most, most, send.at[0]).wait()


def transform_kernel(r_ref, ez_ref, ey_ref, out_ref):
    core = lax.axis_index("img") % 2
    for k in range(3):
        t = jnp.concatenate([r_ref[n, k] for n in range(6)], axis=1)
        u = lax.dot_general(t, ez_ref[...], NT, precision=PRECISE, preferred_element_type=F32)
        rhs = jnp.concatenate([u[:, :L], u[:, L:]], axis=0)
        d = lax.dot_general(ey_ref[core], rhs, NN, precision=PRECISE, preferred_element_type=F32)
        for h in range(2):
            out_ref[h, :, k] = d[192 * h : 192 * h + 192].reshape(4, 48, L)


def deliver_kernel(d_ref, out_ref, other, total, send, recv, send_x, recv_x):
    img, slab, zl, x, zh = place()
    q, core = img // 2, img % 2
    swap = remote(d_ref.at[1 - core], other, send_x, recv_x, 2 * q + 1 - core, slab)
    swap.start()
    swap.wait()
    to = 2 * q + slab // 4
    spot = out_ref.at[pl.ds(3 * (slab % 4), 3)]
    total[...] = d_ref[core] + other[...]
    for n in range(4):
        to_slab = 4 * core + n
        here = jnp.logical_and(to == img, to_slab == slab)

        @pl.when(here)
        def _():
            pltpu.make_async_copy(total.at[n], spot, recv).start()

        @pl.when(jnp.logical_not(here))
        def _():
            remote(total.at[n], spot, send.at[n], recv, to, to_slab).start()

    for n in range(4):
        here = jnp.logical_and(to == img, 4 * core + n == slab)

        @pl.when(jnp.logical_not(here))
        def _():
            pltpu.make_async_copy(total.at[n], total.at[n], send.at[n]).wait()

    pltpu.make_async_copy(out_ref, out_ref, recv).wait()


ANY = pl.BlockSpec(memory_space=pl.ANY)
VMEM = pl.BlockSpec(memory_space=pltpu.VMEM)
DMA = pltpu.SemaphoreType.DMA


def call(kernel, out_shape, args, in_specs, out_specs, scratch=(), side=False, name=None):
    return pl.pallas_call(
        kernel,
        out_shape=out_shape,
        in_specs=in_specs,
        out_specs=out_specs,
        scratch_shapes=list(scratch),
        compiler_params=pltpu.CompilerParams(vmem_limit_bytes=VLIM, has_side_effects=side),
        name=name,
    )(*args)


def shaped(shape, dtype=F32):
    return jax.ShapeDtypeStruct(shape, dtype)


def per_device(images, volume, orient, prior_shift, noise_var):
    col_c, col_s, prior_cols, ex, ez, ey = make_tables()
    img = lax.axis_index("img")
    x = lax.axis_index("slab") // 2
    strips = images.reshape(8, 2, 32, 4, 3, L)
    strips = lax.dynamic_index_in_dim(strips, x, axis=3, keepdims=False)
    strips = jnp.transpose(strips, (2, 3, 1, 0, 4))
    vol = jnp.transpose(volume, (0, 2, 1, 3))
    meta = jnp.stack([orient.astype(F32), prior_shift.astype(F32), noise_var], axis=1)
    meta = jnp.pad(meta, ((0, 0), (0, 125)))
    rows = 12 * img + 3 * x + jnp.arange(3, dtype=jnp.int32) - HALF
    cell = jnp.arange(GRID * GRID, dtype=jnp.int32) // GRID
    shift = jnp.arange(PRIOR, dtype=jnp.int32) - PRIOR // 2 - GRID // 2
    step = 2.0 * math.pi / L
    row_angle = jnp.mod(rows[:, None] * cell[None, :], L).astype(F32) * step
    row_waves = jnp.concatenate([jnp.cos(row_angle), jnp.sin(row_angle)], axis=0)
    turn_angle = jnp.mod(shift[:, None] * rows[None, :], L).astype(F32) * step
    row_turns = jnp.concatenate([jnp.cos(turn_angle), jnp.sin(turn_angle)], axis=1)
    row_waves = jnp.pad(row_waves, ((0, 2), (0, 0)))
    row_turns = jnp.pad(row_turns, ((0, 0), (0, 122)))

    xd, vd, md = call(
        spread_kernel,
        (shaped((32, 3, 2, 8, L), BF16), shaped((4, 2, 3, 48, L)), shaped((32, 8, 128))),
        (strips, vol, meta),
        [ANY] * 3,
        [ANY] * 3,
        [DMA((3,)), DMA((3,)), DMA((3,))],
        True,
        "spread",
    )
    shared = (md, col_c, col_s, prior_cols, row_waves, row_turns)
    partial = call(
        score_kernel, shaped((32, 8, 256)), (xd, vd) + shared, [VMEM] * 8, VMEM, name="score"
    )
    weights = call(
        posterior_kernel,
        shaped((32, 8, 256)),
        (partial, meta),
        [VMEM] * 2,
        VMEM,
        [
            pltpu.VMEM((32, 8, 256), F32),
            pltpu.VMEM((8, 8, 256), F32),
            DMA((3,)),
            DMA((3,)),
            DMA((1,)),
        ],
        True,
        "posterior",
    )
    g = call(
        merge_kernel,
        shaped((3, 1152, 128)),
        (weights, xd, vd) + shared + (ex,),
        [VMEM] * 10,
        VMEM,
        name="merge",
    )
    r = call(
        planes_kernel,
        shaped((6, 3, 64, 3, 1, 128)),
        (g.reshape(3, L, 3, 1, 128),),
        [ANY],
        ANY,
        [DMA((1,)), DMA((1,)), DMA((1,))],
        True,
        "planes",
    )
    d = call(
        transform_kernel,
        shaped((2, 4, 3, 48, L)),
        (r.reshape(6, 3, 192, 128), ez, ey),
        [VMEM] * 3,
        VMEM,
        name="transform",
    )
    return call(
        deliver_kernel,
        shaped((12, 48, L)),
        (d,),
        [VMEM],
        VMEM,
        [
            pltpu.VMEM((4, 3, 48, L), F32),
            pltpu.VMEM((4, 3, 48, L), F32),
            DMA((4,)),
            DMA(()),
            DMA(()),
            DMA(()),
        ],
        True,
        "deliver",
    )


def solution(mesh):
    return jax.shard_map(
        per_device,
        mesh=mesh,
        in_specs=(
            P("img", None, None, None),
            P(None, "slab", "img", None),
            P("img"),
            P("img"),
            P("img"),
        ),
        out_specs=P("img", "slab", None),
        check_vma=False,
    )
```

```python
import math

import jax
import jax.numpy as jnp
import numpy as np
from jax import lax
from jax.experimental import pallas as pl
from jax.experimental.pallas import tpu as pltpu
from jax.sharding import PartitionSpec as P

GRID = 16
PRIOR = 8
NORIENT = 4096
L = 384
HALF = L // 2
SCALE = L ** (-1.5)
PRECISE = lax.Precision.HIGHEST
F32 = jnp.float32
BF16 = jnp.bfloat16
I32 = jnp.int32
VLIM = 62 * 1024 * 1024

NT = (((1,), (1,)), ((), ()))
NN = (((1,), (0,)), ((), ()))


def wave(product):
    angle = 2.0 * math.pi * np.mod(product, L) / L
    return np.cos(angle).astype(np.float32), np.sin(angle).astype(np.float32)


def make_tables():
    ids = np.arange(L)
    ct, st = wave(ids[:, None] * (ids[None, :] - HALF))
    shift = np.arange(PRIOR) - PRIOR // 2 - GRID // 2
    pr = np.concatenate(wave(shift[:, None] * (ids[None, :] - HALF)), axis=1)
    tiles = lambda a: np.ascontiguousarray(a.reshape(L, 3, 128).transpose(1, 0, 2))
    return np.stack([tiles(ct), tiles(st)]), pr


def remote(src, dst, send, recv, img, slab):
    return pltpu.make_async_remote_copy(
        src_ref=src,
        dst_ref=dst,
        send_sem=send,
        recv_sem=recv,
        device_id={"img": img, "slab": slab},
        device_id_type=pl.DeviceIdType.MESH,
    )


def drain(ref, sem):
    pltpu.make_async_copy(ref, ref, sem).wait()


def dot(a, b, dims=NN):
    return lax.dot_general(a, b, dims, preferred_element_type=F32)


def dot_full(a, b, dims=NN):
    return lax.dot_general(a, b, dims, precision=PRECISE, preferred_element_type=F32)


def halves(a):
    high = a.astype(BF16)
    return high, (a - high.astype(F32)).astype(BF16)


def dot_split(ah, al, bh, bl, dims):
    return dot(ah, bh, dims) + (dot(ah, bl, dims) + dot(al, bh, dims))


def iota(shape, axis):
    return lax.broadcasted_iota(I32, shape, axis)


def count(index, step, top):
    total = jnp.zeros_like(index)
    for edge in range(step, top, step):
        total += (index >= edge).astype(I32)
    return total


def plane_ids(index, zh):
    return index + 48 * count(index, 48, 192) + 48 * zh


def planes_of(orient, row):
    return (((row - HALF) * (orient - NORIENT // 2)) >> 11) + HALF


def whole(tab, part):
    return jnp.concatenate([tab[part, n] for n in range(3)], axis=1)


def kernel(
    img_in, vol_in, meta, tab_in, pr,
    out,
    pics, vol, tab, strip, strips, a, volb, xd, vbd, vd, md, tt, wt,
    exh, exl, ezh, ezl, eyh, eyl, sc, parts, sums, w, mh, ml, g, r, d, other, total,
    load, spread_send, spread_recv, own, post_send, post_recv,
    plane_send, plane_recv, swap_send, swap_recv, out_send, out_recv,
):
    img = lax.axis_index("img")
    slab = lax.axis_index("slab")
    zl, x, zh = img // 8, slab // 2, slab % 2
    q, core, yc = img // 2, img % 2, img % 8
    z = zh * 4 + zl
    me = q * 8 + slab

    loads = [
        pltpu.make_async_copy(src, dst, load.at[n])
        for n, (src, dst) in enumerate(((vol_in, vol), (img_in, pics), (tab_in, tab)))
    ]
    for copy in loads:
        copy.start()

    barrier = pltpu.get_barrier_semaphore()
    sheet = z * 8 + yc

    def greet(k, carry):
        to = (sheet + k) % 64
        pl.semaphore_signal(
            barrier,
            inc=1,
            device_id={"img": (to // 8) % 4 * 8 + to % 8, "slab": 2 * x + to // 32},
            device_id_type=pl.DeviceIdType.MESH,
        )
        return carry

    lax.fori_loop(1, 64, greet, 0)
    for k in range(1, 4):
        pl.semaphore_signal(
            barrier,
            inc=1,
            device_id={"img": img, "slab": 2 * ((x + k) % 4) + zh},
            device_id_type=pl.DeviceIdType.MESH,
        )

    loads[0].wait()
    for c in range(2):

        def cast(j, carry, c=c):
            volb[c, j] = vol[c, j].astype(BF16)
            return carry

        lax.fori_loop(0, 12, cast, 0)
    loads[1].wait()

    def sort_images(n, carry):
        for c in range(2):
            for t in range(3):
                strip[c, t] = pics[n, c, :, 128 * t : 128 * t + 128].astype(F32)
            for j in range(3):
                for t in range(3):
                    strips[j, c, t, pl.ds(n, 32, stride=8), :] = strip[
                        c, t, pl.ds(3 * x + j, 32, stride=12), :
                    ]
        return carry

    lax.fori_loop(0, 8, sort_images, 0)
    for c in range(2):

        def pack_images(j, carry, c=c):
            rows = jnp.concatenate([strips[j, c, t] for t in range(3)], axis=1)
            a[:, j, c] = rows.reshape(32, 8, L).astype(BF16)
            return carry

        lax.fori_loop(0, 3, pack_images, 0)

    pl.semaphore_wait(barrier, 66)
    for n in range(1, 4):
        to = (x + n) % 4
        remote(
            volb.at[:, pl.ds(3 * to, 3)], vbd.at[x],
            spread_send.at[1], spread_recv.at[1], img, 2 * to + zh,
        ).start()
    for turn in (2, 6, 1, 7, 0):
        to_z = (z + turn) % 8

        def spread(k, carry, turn=turn, to_z=to_z):
            to = (to_z % 4) * 8 + (yc + k) % 8
            to_slab = 2 * x + to_z // 4
            if turn in (2, 6):
                c = 0 if turn == 2 else 1
                remote(
                    a.at[to, :, c], xd.at[img, :, c],
                    spread_send.at[0], spread_recv.at[0], to, to_slab,
                ).start()
            else:
                remote(
                    a.at[to], xd.at[img], spread_send.at[0], spread_recv.at[0], to, to_slab
                ).start()
            if turn != 6:
                remote(
                    meta, md.at[img], spread_send.at[2], spread_recv.at[2], to, to_slab
                ).start()
            return carry

        lax.fori_loop(1 if turn == 0 else 0, 8, spread, 0)
    for n in range(1, 4):
        to = (x + n) % 4
        remote(
            vol.at[:, pl.ds(3 * to, 3)], vd.at[x],
            spread_send.at[3], spread_recv.at[3], img, 2 * to + zh,
        ).start()
    mine = [
        pltpu.make_async_copy(src, dst, own.at[n])
        for n, (src, dst) in enumerate(
            (
                (a.at[img], xd.at[img]),
                (volb.at[:, pl.ds(3 * x, 3)], vbd.at[x]),
                (meta, md.at[img]),
                (vol.at[:, pl.ds(3 * x, 3)], vd.at[x]),
            )
        )
    ]
    for copy in mine:
        copy.start()

    loads[2].wait()
    ct, st = whole(tab, 0), whole(tab, 1)
    cell = iota((256, GRID), 0)
    step = iota((256, GRID), 1)
    in_b = jnp.where((cell & 15) == step, 1.0, 0.0).astype(F32)
    in_a = jnp.where((cell >> 4) == step, 1.0, 0.0).astype(F32)
    col_c, col_s = dot_full(in_b, ct[:GRID]), dot_full(in_b, st[:GRID])
    row_ids = iota((L, 128), 0)
    at_rows = jnp.where(row_ids == 12 * img + 3 * x + iota((L, 128), 1), 1.0, 0.0).astype(F32)
    row_c = dot_full(in_a, dot_full(ct[:GRID], at_rows))
    row_s = dot_full(in_a, dot_full(st[:GRID], at_rows))
    for j in range(3):
        rc, rs = row_c[:, j : j + 1], row_s[:, j : j + 1]
        wt[j, :, :L] = col_c * rc - col_s * rs
        wt[j, :, L:] = col_s * rc + col_c * rs

    drain(md.at[pl.ds(0, 31)], spread_recv.at[2])
    mine[2].wait()
    values = md[...].reshape(256, 128)
    orient = values[:, 0:1].astype(I32)
    prior = values[:, 1:2].astype(I32)
    values_t = values.T
    orient_row = values_t[0:1, :].astype(I32)
    ids = iota((256, PRIOR), 1)
    in_cols = jnp.where((prior & 7) == ids, 1.0, 0.0).astype(F32)
    in_rows = jnp.where((prior >> 3) == ids, 1.0, 0.0).astype(F32)
    turn_c, turn_s = dot_full(in_cols, pr[:, :L]), dot_full(in_cols, pr[:, L:])
    row_turn_c = dot_full(in_rows, dot_full(pr[:, :L], at_rows))
    row_turn_s = dot_full(in_rows, dot_full(pr[:, L:], at_rows))
    for j in range(3):
        rc, rs = row_turn_c[:, j : j + 1], row_turn_s[:, j : j + 1]
        tt[j, 0] = turn_c * rc - turn_s * rs
        tt[j, 1] = turn_c * rs + turn_s * rc

    drain(vbd.at[pl.ds(0, 3)], spread_recv.at[1])
    mine[1].wait()
    drain(xd.at[pl.ds(0, 31)], spread_recv.at[0])
    mine[0].wait()
    first = 12 * img + 3 * x
    zid_row = plane_ids(iota((1, 192), 1), zh)
    zid_col = plane_ids(iota((192, 1), 0), zh)

    def picture(j, c):
        return xd[:, j, c].astype(F32).reshape(256, L)

    sc[...] = jnp.zeros_like(sc)

    def score(j, carry):
        pick = jnp.where(planes_of(orient, first + j) == zid_row, 1.0, 0.0).astype(BF16)
        sr, si = (
            dot(pick, jnp.concatenate([vbd[b, c, j] for b in range(4)], axis=0))
            for c in range(2)
        )
        xr, xi = picture(j, 0), picture(j, 1)
        pr_, pi_ = sr * xr + si * xi, sr * xi - si * xr
        tr, ti = tt[j, 0], tt[j, 1]
        lhs = jnp.concatenate([pr_ * tr - pi_ * ti, -(pr_ * ti + pi_ * tr)], axis=1)
        sc[...] += dot_full(lhs, wt[j], NT).reshape(32, 8, 256)
        return carry

    lax.fori_loop(0, 3, score, 0)

    def send_parts(k, carry):
        to = (img + k) % 32
        remote(sc.at[to], parts.at[img], post_send.at[0], post_recv.at[0], to, slab).start()
        return carry

    lax.fori_loop(1, 32, send_parts, 0)
    parts[img] = sc[img]

    lane = iota((L, 2 * L), 1)
    spot = lane % L
    is_re = jnp.logical_or(spot < 128, jnp.logical_and(spot >= 128, spot < 192))
    local = jnp.where(spot < 192, spot, jnp.where(spot < 256, spot - 64, spot - 256))
    kz = local + 48 * count(local, 48, 192) + 48 * (lane >= L).astype(I32)
    pick_z = jnp.where(iota((L, 2 * L), 0) == kz, 1.0, 0.0).astype(BF16)
    cth, ctl = halves(ct)
    sth, stl = halves(st)
    re_z = is_re[:1]
    for dst, c_part, s_part in ((ezh, cth, sth), (ezl, ctl, stl)):
        cz, sz = dot(c_part, pick_z), dot(s_part, pick_z)
        dst[:L] = jnp.where(re_z, cz, -sz).astype(BF16)
        dst[L:] = jnp.where(re_z, sz, cz).astype(BF16)
    lane = iota((L, L), 1)
    local = jnp.where(lane < 192, lane, lane - 192)
    ky = local + 12 * count(local, 12, 192) + 12 * core
    pick_y = jnp.where(iota((L, L), 0) == ky, 1.0, 0.0).astype(BF16)
    re_y = (lane < 192)[:1]
    for dst, c_part, s_part in ((eyh, cth, sth), (eyl, ctl, stl)):
        dst[...] = jnp.where(re_y, dot(c_part, pick_y), -dot(s_part, pick_y)).astype(BF16)
    for k in range(3):
        cx, sx = (
            jnp.concatenate([tab[p, t, pl.ds(k, 128, stride=3), :] for t in range(3)], axis=1)
            for p in range(2)
        )
        for n, (left, right) in enumerate(((cx, -sx), (sx, cx))):
            for side, value in enumerate((left, right)):
                high, low = halves(value)
                exh[k, 128 * n : 128 * n + 128, L * side : L * side + L] = high
                exl[k, 128 * n : 128 * n + 128, L * side : L * side + L] = low

    drain(parts.at[pl.ds(0, 31)], post_recv.at[0])
    sums[slab] = jnp.sum(parts[...], axis=0)

    def send_sums(k, carry):
        to = (slab + k) % 8
        remote(sums.at[slab], sums.at[slab], post_send.at[1], post_recv.at[1], img, to).start()
        return carry

    lax.fori_loop(1, 8, send_sums, 0)
    drain(sums.at[pl.ds(0, 7)], post_recv.at[1])
    logits = jnp.sum(sums[...], axis=0) / (2.0 * meta[:, 2:3])
    expo = jnp.exp(logits - jnp.max(logits, axis=1, keepdims=True))
    w[img] = expo / jnp.sum(expo, axis=1, keepdims=True)

    def send_weights(k, carry):
        to = (img + k) % 32
        remote(w.at[img], w.at[img], post_send.at[2], post_recv.at[2], to, slab).start()
        return carry

    lax.fori_loop(1, 32, send_weights, 0)
    drain(vd.at[pl.ds(0, 3)], spread_recv.at[3])
    mine[3].wait()
    drain(w.at[pl.ds(0, 31)], post_recv.at[2])

    def merge(j, carry):
        f = dot_full(w[...].reshape(256, 256), wt[j])
        fr, fi = f[:, :L], f[:, L:]
        tr, ti = tt[j, 0], tt[j, 1]
        gr, gi = tr * fr - ti * fi, tr * fi + ti * fr
        xr, xi = picture(j, 0), picture(j, 1)
        hit = jnp.where(planes_of(orient_row, first + j) == zid_col, 1.0, 0.0).astype(F32)
        share = 1.0 / (jnp.sum(hit, axis=1, keepdims=True) + 1.0)
        put = hit.astype(BF16)
        for c, part in enumerate((xr * gr + xi * gi, xi * gr - xr * gi)):
            back = dot(put, part.astype(BF16))
            rows = jnp.concatenate([vd[b, c, j] for b in range(4)], axis=0)
            high, low = halves((back + rows) * share)
            mh[j, :, L * c : L * c + L] = high
            ml[j, :, L * c : L * c + L] = low
        return carry

    lax.fori_loop(0, 3, merge, 0)

    for k in range(3):

        def x_lines(j, carry, k=k):
            gx = dot_split(exh[k], exl[k], mh[j], ml[j], NT)
            re, im = gx[:128], gx[128:]
            tiles = (
                re[:, :128],
                jnp.concatenate([re[:, 128:], im[:, 128:]], axis=1),
                im[:, :128],
            )
            for t in range(3):
                g[k, t, pl.ds(j, 128, stride=3), :] = tiles[t]
            return carry

        lax.fori_loop(0, 3, x_lines, 0)
        land = r.at[k, pl.ds(3 * zh, 3), pl.ds(3 * (4 * q + x), 3)]

        def send_lines(n, carry, k=k, land=land):
            to = (me + n) % 128
            remote(
                g.at[k, :, pl.ds(3 * to, 3)], land,
                plane_send.at[k], plane_recv.at[k], 2 * (to // 8) + core, to % 8,
            ).start()
            return carry

        lax.fori_loop(1, 128, send_lines, 0)
        pltpu.make_async_copy(g.at[k, :, pl.ds(3 * me, 3)], land, own.at[4 + k]).start()

    to = 2 * q + slab // 4
    for k in range(3):
        lines = g.at[k, :, pl.ds(0, 381)]
        pltpu.make_async_copy(
            g.at[k, :, pl.ds(0, 3)], g.at[k, :, pl.ds(0, 3)], own.at[4 + k]
        ).wait()
        drain(lines, plane_recv.at[k])
        th, tl = halves(jnp.concatenate([r[k, n] for n in range(6)], axis=1))
        u = dot_split(th, tl, ezh[...], ezl[...], NT)
        uh, ul = halves(jnp.concatenate([u[:, :L], u[:, L:]], axis=0))
        d[k] = dot_split(eyh[...], eyl[...], uh, ul, NN).reshape(8, 48, L)
        swap = remote(
            d.at[k, pl.ds(4 * (1 - core), 4)], other.at[k],
            swap_send.at[k], swap_recv.at[k], 2 * q + 1 - core, slab,
        )
        swap.start()
        swap.wait()
        total[k] = (d[k, pl.ds(4 * core, 4)] + other[k]) * SCALE
        place = out.at[3 * (slab % 4) + k]
        for n in range(4):
            here = jnp.logical_and(to == img, 4 * core + n == slab)

            @pl.when(here)
            def _(n=n, k=k, place=place):
                pltpu.make_async_copy(total.at[k, n], place, out_recv).start()

            @pl.when(jnp.logical_not(here))
            def _(n=n, k=k, place=place):
                remote(
                    total.at[k, n], place, out_send.at[n], out_recv, to, 4 * core + n
                ).start()

    drain(a.at[pl.ds(0, 31)], spread_send.at[0])
    drain(vbd.at[pl.ds(0, 3)], spread_send.at[1])
    drain(md.at[pl.ds(0, 31)], spread_send.at[2])
    drain(vd.at[pl.ds(0, 3)], spread_send.at[3])
    drain(parts.at[pl.ds(0, 31)], post_send.at[0])
    drain(sums.at[pl.ds(0, 7)], post_send.at[1])
    drain(w.at[pl.ds(0, 31)], post_send.at[2])
    for k in range(3):
        drain(g.at[k, :, pl.ds(0, 381)], plane_send.at[k])
    for n in range(4):
        here = jnp.logical_and(to == img, 4 * core + n == slab)

        @pl.when(jnp.logical_not(here))
        def _(n=n):
            drain(total.at[:, n], out_send.at[n])

    drain(out, out_recv)


ANY = pl.BlockSpec(memory_space=pl.ANY)
VMEM = pl.BlockSpec(memory_space=pltpu.VMEM)
DMA = pltpu.SemaphoreType.DMA


def per_device(images, volume, orient, prior_shift, noise_var):
    tab, pr = make_tables()
    vol = jnp.transpose(volume, (0, 2, 1, 3))
    meta = jnp.stack([orient.astype(F32), prior_shift.astype(F32), noise_var], axis=1)
    meta = jnp.pad(meta, ((0, 0), (0, 125)))
    buf = pltpu.VMEM
    scratch = [
        buf((8, 2, L, L), BF16),
        buf((2, 12, 48, L), F32),
        buf((2, 3, L, 128), F32),
        buf((2, 3, L, 128), F32),
        buf((3, 2, 3, 256, 128), F32),
        buf((32, 3, 2, 8, L), BF16),
        buf((2, 12, 48, L), BF16),
        buf((32, 3, 2, 8, L), BF16),
        buf((4, 2, 3, 48, L), BF16),
        buf((4, 2, 3, 48, L), F32),
        buf((32, 8, 128), F32),
        buf((3, 2, 256, L), F32),
        buf((3, 256, 2 * L), F32),
        buf((3, 256, 2 * L), BF16),
        buf((3, 256, 2 * L), BF16),
        buf((2 * L, 2 * L), BF16),
        buf((2 * L, 2 * L), BF16),
        buf((L, L), BF16),
        buf((L, L), BF16),
        buf((32, 8, 256), F32),
        buf((32, 8, 256), F32),
        buf((8, 8, 256), F32),
        buf((32, 8, 256), F32),
        buf((3, 192, 2 * L), BF16),
        buf((3, 192, 2 * L), BF16),
        buf((3, 3, L, 128), F32),
        buf((3, 6, 192, 128), F32),
        buf((3, 8, 48, L), F32),
        buf((3, 4, 48, L), F32),
        buf((3, 4, 48, L), F32),
        DMA((3,)),
        DMA((4,)),
        DMA((4,)),
        DMA((7,)),
        DMA((3,)),
        DMA((3,)),
        DMA((3,)),
        DMA((3,)),
        DMA((3,)),
        DMA((3,)),
        DMA((4,)),
        DMA(()),
    ]
    return pl.pallas_call(
        kernel,
        out_shape=jax.ShapeDtypeStruct((12, 48, L), F32),
        in_specs=[ANY, ANY, VMEM, ANY, VMEM],
        out_specs=VMEM,
        scratch_shapes=scratch,
        compiler_params=pltpu.CompilerParams(
            vmem_limit_bytes=VLIM, has_side_effects=True, collective_id=0
        ),
        name="step",
    )(images, vol, meta, tab, pr)


def solution(mesh):
    return jax.shard_map(
        per_device,
        mesh=mesh,
        in_specs=(
            P("img", None, None, None),
            P(None, "slab", "img", None),
            P("img"),
            P("img"),
            P("img"),
        ),
        out_specs=P("img", "slab", None),
        check_vma=False,
    )
```

```python
import math

import jax
import jax.numpy as jnp
import numpy as np
from jax import lax
from jax.experimental import pallas as pl
from jax.experimental.pallas import tpu as pltpu
from jax.sharding import PartitionSpec as P

GRID = 16
PRIOR = 8
NORIENT = 4096
L = 384
HALF = L // 2
SCALE = L ** (-1.5)
PRECISE = lax.Precision.HIGHEST
F32 = jnp.float32
BF16 = jnp.bfloat16
I32 = jnp.int32
VLIM = 62 * 1024 * 1024

NT = (((1,), (1,)), ((), ()))
NN = (((1,), (0,)), ((), ()))


def wave(product):
    angle = 2.0 * math.pi * np.mod(product, L) / L
    return np.cos(angle).astype(np.float32), np.sin(angle).astype(np.float32)


def make_tables():
    ids = np.arange(L)
    ct, st = wave(ids[:, None] * (ids[None, :] - HALF))
    shift = np.arange(PRIOR) - PRIOR // 2 - GRID // 2
    pr = np.concatenate(wave(shift[:, None] * (ids[None, :] - HALF)), axis=1)
    tiles = lambda a: np.ascontiguousarray(a.reshape(L, 3, 128).transpose(1, 0, 2))
    return np.stack([tiles(ct), tiles(st)]), pr


def remote(src, dst, send, recv, img, slab):
    return pltpu.make_async_remote_copy(
        src_ref=src,
        dst_ref=dst,
        send_sem=send,
        recv_sem=recv,
        device_id={"img": img, "slab": slab},
        device_id_type=pl.DeviceIdType.MESH,
    )


def drain(ref, sem):
    pltpu.make_async_copy(ref, ref, sem).wait()


def dot(a, b, dims=NN):
    return lax.dot_general(a, b, dims, preferred_element_type=F32)


def dot_full(a, b, dims=NN):
    return lax.dot_general(a, b, dims, precision=PRECISE, preferred_element_type=F32)


def halves(a):
    high = a.astype(BF16)
    return high, (a - high.astype(F32)).astype(BF16)


def dot_split(ah, al, bh, bl, dims):
    return dot(ah, bh, dims) + (dot(ah, bl, dims) + dot(al, bh, dims))


def iota(shape, axis):
    return lax.broadcasted_iota(I32, shape, axis)


def count(index, step, top):
    total = jnp.zeros_like(index)
    for edge in range(step, top, step):
        total += (index >= edge).astype(I32)
    return total


def plane_ids(index, zh):
    return index + 48 * count(index, 48, 192) + 48 * zh


def planes_of(orient, row):
    return (((row - HALF) * (orient - NORIENT // 2)) >> 11) + HALF


def power(n):
    total = jnp.ones(n.shape, F32)
    for bit in range(7):
        total *= jnp.where((n >> bit) & 1 == 1, 2.0 ** (2**bit), 1.0)
    return total


def pack(tiles):
    peak = jnp.maximum(jnp.maximum(jnp.abs(tiles[0]), jnp.abs(tiles[1])), jnp.abs(tiles[2]))
    peak = jnp.maximum(jnp.max(peak, axis=1, keepdims=True), 1e-30)
    level = jnp.ceil(jnp.log(peak) * (1.0 / math.log(2.0)) + 0.01)
    level = jnp.clip(level, -100.0, 20.0).astype(I32) + 101
    gain = power(121 - level)
    q0, q1, q2 = (jnp.floor(tile * gain + 0.5).astype(I32) for tile in tiles)
    flag = (level >> (iota(tiles[0].shape, 1) & 31)) & 1
    return (q0 << 11) | ((q2 >> 10) & 2047), (q1 << 11) | ((q2 & 1023) << 1) | flag


def unpack(one, two):
    lane = iota(one.shape, 1)
    flag = jnp.where(lane < 8, (two & 1) << (lane & 7), 0).astype(F32)
    level = jnp.sum(flag, axis=1, keepdims=True).astype(I32)
    gain = power(level) * 2.0**-121
    third = ((one & 2047) << 10) | ((two >> 1) & 1023)
    return [v.astype(F32) * gain for v in (one >> 11, two >> 11, (third << 11) >> 11)]


def whole(tab, part):
    return jnp.concatenate([tab[part, n] for n in range(3)], axis=1)


def kernel(
    img_in, vol_in, orient_in, prior_in, noise_in, tab_in, pr,
    out,
    meta, pics, vol, tab, strip, strips, a, volb, xd, vbd, vd, md, tt, wt,
    exh, exl, ezh, ezl, eyh, eyl, sc, parts, sums, w, mh, ml, lines, g, r, d, other, total,
    load, spread_send, spread_recv, own, post_send, post_recv,
    plane_send, plane_recv, swap_send, swap_recv, out_send, out_recv,
):
    img = lax.axis_index("img")
    slab = lax.axis_index("slab")
    zl, x, zh = img // 8, slab // 2, slab % 2
    q, core, yc = img // 2, img % 2, img % 8
    z = zh * 4 + zl
    me = q * 8 + slab

    loads = [
        pltpu.make_async_copy(src, dst, load.at[n])
        for n, (src, dst) in enumerate(((vol_in, vol), (img_in, pics), (tab_in, tab)))
    ]
    for copy in loads:
        copy.start()

    barrier = pltpu.get_barrier_semaphore()
    sheet = z * 8 + yc

    def greet(k, carry):
        to = (sheet + k) % 64
        pl.semaphore_signal(
            barrier,
            inc=1,
            device_id={"img": (to // 8) % 4 * 8 + to % 8, "slab": 2 * x + to // 32},
            device_id_type=pl.DeviceIdType.MESH,
        )
        return carry

    lax.fori_loop(1, 64, greet, 0)
    for k in range(1, 4):
        pl.semaphore_signal(
            barrier,
            inc=1,
            device_id={"img": img, "slab": 2 * ((x + k) % 4) + zh},
            device_id_type=pl.DeviceIdType.MESH,
        )

    entry, item = iota((8, 128), 0), iota((8, 128), 1)
    facts = jnp.zeros((8, 128), F32)
    for n in range(8):
        for m, ref in enumerate((orient_in, prior_in, noise_in)):
            here = jnp.logical_and(entry == n, item == m)
            facts = jnp.where(here, ref[n].astype(F32), facts)
    meta[...] = facts

    loads[0].wait()
    for c in range(2):

        def cast(j, carry, c=c):
            volb[c, j] = vol[c, j].astype(BF16)
            return carry

        lax.fori_loop(0, 12, cast, 0)
    loads[1].wait()

    def sort_images(n, carry):
        for c in range(2):
            for t in range(3):
                strip[c, t] = pics[n, c, :, 128 * t : 128 * t + 128].astype(F32)
            for j in range(3):
                for t in range(3):
                    strips[j, c, t, pl.ds(n, 32, stride=8), :] = strip[
                        c, t, pl.ds(3 * x + j, 32, stride=12), :
                    ]
        return carry

    lax.fori_loop(0, 8, sort_images, 0)
    for c in range(2):

        def pack_images(j, carry, c=c):
            rows = jnp.concatenate([strips[j, c, t] for t in range(3)], axis=1)
            a[:, j, c] = rows.reshape(32, 8, L).astype(BF16)
            return carry

        lax.fori_loop(0, 3, pack_images, 0)

    pl.semaphore_wait(barrier, 66)
    for n in range(1, 4):
        to = (x + n) % 4
        remote(
            volb.at[:, pl.ds(3 * to, 3)], vbd.at[x],
            spread_send.at[1], spread_recv.at[1], img, 2 * to + zh,
        ).start()
    for turn in (2, 6, 1, 7, 0):
        to_z = (z + turn) % 8

        def spread(k, carry, turn=turn, to_z=to_z):
            to = (to_z % 4) * 8 + (yc + k) % 8
            to_slab = 2 * x + to_z // 4
            if turn in (2, 6):
                c = 0 if turn == 2 else 1
                remote(
                    a.at[to, :, c], xd.at[img, :, c],
                    spread_send.at[0], spread_recv.at[0], to, to_slab,
                ).start()
            else:
                remote(
                    a.at[to], xd.at[img], spread_send.at[0], spread_recv.at[0], to, to_slab
                ).start()
            if turn != 6:
                remote(
                    meta, md.at[img], spread_send.at[2], spread_recv.at[2], to, to_slab
                ).start()
            return carry

        lax.fori_loop(1 if turn == 0 else 0, 8, spread, 0)
    mine = [
        pltpu.make_async_copy(src, dst, own.at[n])
        for n, (src, dst) in enumerate(
            (
                (a.at[img], xd.at[img]),
                (volb.at[:, pl.ds(3 * x, 3)], vbd.at[x]),
                (meta, md.at[img]),
                (vol.at[:, pl.ds(3 * x, 3)], vd.at[x]),
            )
        )
    ]
    for copy in mine:
        copy.start()

    loads[2].wait()
    ct, st = whole(tab, 0), whole(tab, 1)
    cell = iota((256, GRID), 0)
    step = iota((256, GRID), 1)
    in_b = jnp.where((cell & 15) == step, 1.0, 0.0).astype(F32)
    in_a = jnp.where((cell >> 4) == step, 1.0, 0.0).astype(F32)
    col_c, col_s = dot_full(in_b, ct[:GRID]), dot_full(in_b, st[:GRID])
    row_ids = iota((L, 128), 0)
    at_rows = jnp.where(row_ids == 12 * img + 3 * x + iota((L, 128), 1), 1.0, 0.0).astype(F32)
    row_c = dot_full(in_a, dot_full(ct[:GRID], at_rows))
    row_s = dot_full(in_a, dot_full(st[:GRID], at_rows))
    for j in range(3):
        rc, rs = row_c[:, j : j + 1], row_s[:, j : j + 1]
        wt[j, :, :L] = col_c * rc - col_s * rs
        wt[j, :, L:] = col_s * rc + col_c * rs

    drain(md.at[pl.ds(0, 31)], spread_recv.at[2])
    mine[2].wait()
    values = md[...].reshape(256, 128)
    orient = values[:, 0:1].astype(I32)
    prior = values[:, 1:2].astype(I32)
    values_t = values.T
    orient_row = values_t[0:1, :].astype(I32)
    ids = iota((256, PRIOR), 1)
    in_cols = jnp.where((prior & 7) == ids, 1.0, 0.0).astype(F32)
    in_rows = jnp.where((prior >> 3) == ids, 1.0, 0.0).astype(F32)
    turn_c, turn_s = dot_full(in_cols, pr[:, :L]), dot_full(in_cols, pr[:, L:])
    row_turn_c = dot_full(in_rows, dot_full(pr[:, :L], at_rows))
    row_turn_s = dot_full(in_rows, dot_full(pr[:, L:], at_rows))
    for j in range(3):
        rc, rs = row_turn_c[:, j : j + 1], row_turn_s[:, j : j + 1]
        tt[j, 0] = turn_c * rc - turn_s * rs
        tt[j, 1] = turn_c * rs + turn_s * rc

    drain(vbd.at[pl.ds(0, 3)], spread_recv.at[1])
    mine[1].wait()
    for n in range(1, 4):
        to = (x + n) % 4
        remote(
            vol.at[:, pl.ds(3 * to, 3)], vd.at[x],
            spread_send.at[3], spread_recv.at[3], img, 2 * to + zh,
        ).start()
    drain(xd.at[pl.ds(0, 31)], spread_recv.at[0])
    mine[0].wait()
    first = 12 * img + 3 * x
    zid_row = plane_ids(iota((1, 192), 1), zh)
    zid_col = plane_ids(iota((192, 1), 0), zh)

    def picture(j, c):
        return xd[:, j, c].astype(F32).reshape(256, L)

    sc[...] = jnp.zeros_like(sc)

    def score(j, carry):
        pick = jnp.where(planes_of(orient, first + j) == zid_row, 1.0, 0.0).astype(BF16)
        sr, si = (
            dot(pick, jnp.concatenate([vbd[b, c, j] for b in range(4)], axis=0))
            for c in range(2)
        )
        xr, xi = picture(j, 0), picture(j, 1)
        pr_, pi_ = sr * xr + si * xi, sr * xi - si * xr
        tr, ti = tt[j, 0], tt[j, 1]
        lhs = jnp.concatenate([pr_ * tr - pi_ * ti, -(pr_ * ti + pi_ * tr)], axis=1)
        sc[...] += dot_full(lhs, wt[j], NT).reshape(32, 8, 256)
        return carry

    lax.fori_loop(0, 3, score, 0)

    def send_parts(k, carry):
        to = (img + k) % 32
        remote(sc.at[to], parts.at[img], post_send.at[0], post_recv.at[0], to, slab).start()
        return carry

    lax.fori_loop(1, 32, send_parts, 0)
    parts[img] = sc[img]

    lane = iota((L, 2 * L), 1)
    spot = lane % L
    is_re = jnp.logical_or(spot < 128, jnp.logical_and(spot >= 128, spot < 192))
    local = jnp.where(spot < 192, spot, jnp.where(spot < 256, spot - 64, spot - 256))
    kz = local + 48 * count(local, 48, 192) + 48 * (lane >= L).astype(I32)
    pick_z = jnp.where(iota((L, 2 * L), 0) == kz, 1.0, 0.0).astype(BF16)
    cth, ctl = halves(ct)
    sth, stl = halves(st)
    re_z = is_re[:1]
    for dst, c_part, s_part in ((ezh, cth, sth), (ezl, ctl, stl)):
        cz, sz = dot(c_part, pick_z), dot(s_part, pick_z)
        dst[:L] = jnp.where(re_z, cz, -sz).astype(BF16)
        dst[L:] = jnp.where(re_z, sz, cz).astype(BF16)
    lane = iota((L, L), 1)
    local = jnp.where(lane < 192, lane, lane - 192)
    ky = local + 12 * count(local, 12, 192) + 12 * core
    pick_y = jnp.where(iota((L, L), 0) == ky, 1.0, 0.0).astype(BF16)
    re_y = (lane < 192)[:1]
    for dst, c_part, s_part in ((eyh, cth, sth), (eyl, ctl, stl)):
        dst[...] = jnp.where(re_y, dot(c_part, pick_y), -dot(s_part, pick_y)).astype(BF16)
    for k in range(3):
        cx, sx = (
            jnp.concatenate([tab[p, t, pl.ds(k, 128, stride=3), :] for t in range(3)], axis=1)
            for p in range(2)
        )
        for n, (left, right) in enumerate(((cx, -sx), (sx, cx))):
            for side, value in enumerate((left, right)):
                high, low = halves(value)
                exh[k, 128 * n : 128 * n + 128, L * side : L * side + L] = high
                exl[k, 128 * n : 128 * n + 128, L * side : L * side + L] = low

    drain(parts.at[pl.ds(0, 31)], post_recv.at[0])
    sums[slab] = jnp.sum(parts[...], axis=0)

    def send_sums(k, carry):
        to = (slab + k) % 8
        remote(sums.at[slab], sums.at[slab], post_send.at[1], post_recv.at[1], img, to).start()
        return carry

    lax.fori_loop(1, 8, send_sums, 0)
    drain(sums.at[pl.ds(0, 7)], post_recv.at[1])
    logits = jnp.sum(sums[...], axis=0) / (2.0 * meta[:, 2:3])
    expo = jnp.exp(logits - jnp.max(logits, axis=1, keepdims=True))
    w[img] = expo / jnp.sum(expo, axis=1, keepdims=True)

    def send_weights(k, carry):
        to = (img + k) % 32
        remote(w.at[img], w.at[img], post_send.at[2], post_recv.at[2], to, slab).start()
        return carry

    lax.fori_loop(1, 32, send_weights, 0)
    drain(vd.at[pl.ds(0, 3)], spread_recv.at[3])
    mine[3].wait()
    drain(w.at[pl.ds(0, 31)], post_recv.at[2])

    def merge(j, carry):
        f = dot_full(w[...].reshape(256, 256), wt[j])
        fr, fi = f[:, :L], f[:, L:]
        tr, ti = tt[j, 0], tt[j, 1]
        gr, gi = tr * fr - ti * fi, tr * fi + ti * fr
        xr, xi = picture(j, 0), picture(j, 1)
        hit = jnp.where(planes_of(orient_row, first + j) == zid_col, 1.0, 0.0).astype(F32)
        share = 1.0 / (jnp.sum(hit, axis=1, keepdims=True) + 1.0)
        put = hit.astype(BF16)
        for c, part in enumerate((xr * gr + xi * gi, xi * gr - xr * gi)):
            back = dot(put, part.astype(BF16))
            rows = jnp.concatenate([vd[b, c, j] for b in range(4)], axis=0)
            high, low = halves((back + rows) * share)
            mh[j, :, L * c : L * c + L] = high
            ml[j, :, L * c : L * c + L] = low
        return carry

    lax.fori_loop(0, 3, merge, 0)

    for k in range(3):

        def x_lines(j, carry, k=k):
            gx = dot_split(exh[k], exl[k], mh[j], ml[j], NT)
            re, im = gx[:128], gx[128:]
            tiles = (
                re[:, :128],
                jnp.concatenate([re[:, 128:], im[:, 128:]], axis=1),
                im[:, :128],
            )
            for t in range(3):
                lines[t, pl.ds(j, 128, stride=3), :] = tiles[t]
            return carry

        lax.fori_loop(0, 3, x_lines, 0)
        g[k, 0], g[k, 1] = pack([lines[t] for t in range(3)])
        land = r.at[k, pl.ds(2 * zh, 2), pl.ds(3 * (4 * q + x), 3)]

        def send_lines(n, carry, k=k, land=land):
            to = (me + n) % 128
            remote(
                g.at[k, :, pl.ds(3 * to, 3)], land,
                plane_send.at[k], plane_recv.at[k], 2 * (to // 8) + core, to % 8,
            ).start()
            return carry

        lax.fori_loop(1, 128, send_lines, 0)
        pltpu.make_async_copy(g.at[k, :, pl.ds(3 * me, 3)], land, own.at[4 + k]).start()

    to = 2 * q + slab // 4
    for k in range(3):
        pltpu.make_async_copy(
            g.at[k, :, pl.ds(0, 3)], g.at[k, :, pl.ds(0, 3)], own.at[4 + k]
        ).wait()
        drain(g.at[k, :, pl.ds(0, 381)], plane_recv.at[k])
        columns = unpack(r[k, 0], r[k, 1]) + unpack(r[k, 2], r[k, 3])
        th, tl = halves(jnp.concatenate(columns, axis=1))
        u = dot_split(th, tl, ezh[...], ezl[...], NT)
        uh, ul = halves(jnp.concatenate([u[:, :L], u[:, L:]], axis=0))
        d[k] = dot_split(eyh[...], eyl[...], uh, ul, NN).reshape(8, 48, L)
        swap = remote(
            d.at[k, pl.ds(4 * (1 - core), 4)], other.at[k],
            swap_send.at[k], swap_recv.at[k], 2 * q + 1 - core, slab,
        )
        swap.start()
        swap.wait()
        done = ((d[k, pl.ds(4 * core, 4)] + other[k]) * SCALE).reshape(192, L)
        words = pack([done[:, :128], done[:, 128:256], done[:, 256:]])
        for n in range(2):
            total[k, :, n] = words[n].reshape(4, 48, 128)
        place = out.at[3 * (slab % 4) + k]
        for n in range(4):
            here = jnp.logical_and(to == img, 4 * core + n == slab)

            @pl.when(here)
            def _(n=n, k=k, place=place):
                pltpu.make_async_copy(total.at[k, n], place, out_recv).start()

            @pl.when(jnp.logical_not(here))
            def _(n=n, k=k, place=place):
                remote(
                    total.at[k, n], place, out_send.at[n], out_recv, to, 4 * core + n
                ).start()

    drain(a.at[pl.ds(0, 31)], spread_send.at[0])
    drain(vbd.at[pl.ds(0, 3)], spread_send.at[1])
    drain(md.at[pl.ds(0, 31)], spread_send.at[2])
    drain(vd.at[pl.ds(0, 3)], spread_send.at[3])
    drain(parts.at[pl.ds(0, 31)], post_send.at[0])
    drain(sums.at[pl.ds(0, 7)], post_send.at[1])
    drain(w.at[pl.ds(0, 31)], post_send.at[2])
    for k in range(3):
        drain(g.at[k, :, pl.ds(0, 381)], plane_send.at[k])
    for n in range(4):
        here = jnp.logical_and(to == img, 4 * core + n == slab)

        @pl.when(jnp.logical_not(here))
        def _(n=n):
            drain(total.at[:, n], out_send.at[n])

    drain(out, out_recv)


def open_kernel(words, out):
    for n in range(4):
        one, two = (words[3 * n : 3 * n + 3, m].reshape(144, 128) for m in range(2))
        value = jnp.concatenate(unpack(one, two), axis=1)
        out[3 * n : 3 * n + 3] = value.reshape(3, 48, L)


ANY = pl.BlockSpec(memory_space=pl.ANY)
VMEM = pl.BlockSpec(memory_space=pltpu.VMEM)
DMA = pltpu.SemaphoreType.DMA


def per_device(images, volume, orient, prior_shift, noise_var):
    tab, pr = make_tables()
    vol = jnp.transpose(volume, (0, 2, 1, 3))
    buf = pltpu.VMEM
    scratch = [
        buf((8, 128), F32),
        buf((8, 2, L, L), BF16),
        buf((2, 12, 48, L), F32),
        buf((2, 3, L, 128), F32),
        buf((2, 3, L, 128), F32),
        buf((3, 2, 3, 256, 128), F32),
        buf((32, 3, 2, 8, L), BF16),
        buf((2, 12, 48, L), BF16),
        buf((32, 3, 2, 8, L), BF16),
        buf((4, 2, 3, 48, L), BF16),
        buf((4, 2, 3, 48, L), F32),
        buf((32, 8, 128), F32),
        buf((3, 2, 256, L), F32),
        buf((3, 256, 2 * L), F32),
        buf((3, 256, 2 * L), BF16),
        buf((3, 256, 2 * L), BF16),
        buf((2 * L, 2 * L), BF16),
        buf((2 * L, 2 * L), BF16),
        buf((L, L), BF16),
        buf((L, L), BF16),
        buf((32, 8, 256), F32),
        buf((32, 8, 256), F32),
        buf((8, 8, 256), F32),
        buf((32, 8, 256), F32),
        buf((3, 192, 2 * L), BF16),
        buf((3, 192, 2 * L), BF16),
        buf((3, L, 128), F32),
        buf((3, 2, L, 128), I32),
        buf((3, 4, 192, 128), I32),
        buf((3, 8, 48, L), F32),
        buf((3, 4, 48, L), F32),
        buf((3, 4, 2, 48, 128), I32),
        DMA((3,)),
        DMA((4,)),
        DMA((4,)),
        DMA((7,)),
        DMA((3,)),
        DMA((3,)),
        DMA((3,)),
        DMA((3,)),
        DMA((3,)),
        DMA((3,)),
        DMA((4,)),
        DMA(()),
    ]
    smem = pl.BlockSpec(memory_space=pltpu.SMEM)
    words = pl.pallas_call(
        kernel,
        out_shape=jax.ShapeDtypeStruct((12, 2, 48, 128), I32),
        in_specs=[ANY, ANY, smem, smem, smem, ANY, VMEM],
        out_specs=VMEM,
        scratch_shapes=scratch,
        compiler_params=pltpu.CompilerParams(
            vmem_limit_bytes=VLIM, has_side_effects=True, collective_id=0
        ),
        name="step",
    )(images, vol, orient, prior_shift, noise_var, tab, pr)
    return pl.pallas_call(
        open_kernel,
        out_shape=jax.ShapeDtypeStruct((12, 48, L), F32),
        in_specs=[VMEM],
        out_specs=VMEM,
        name="open",
    )(words)


def solution(mesh):
    return jax.shard_map(
        per_device,
        mesh=mesh,
        in_specs=(
            P("img", None, None, None),
            P(None, "slab", "img", None),
            P("img"),
            P("img"),
            P("img"),
        ),
        out_specs=P("img", "slab", None),
        check_vma=False,
    )
```

```python
import math

import jax
import jax.numpy as jnp
import numpy as np
from jax import lax
from jax.experimental import pallas as pl
from jax.experimental.pallas import tpu as pltpu
from jax.sharding import PartitionSpec as P

GRID = 16
PRIOR = 8
NORIENT = 4096
L = 384
HALF = L // 2
SCALE = L ** (-1.5)
PRECISE = lax.Precision.HIGHEST
F32 = jnp.float32
BF16 = jnp.bfloat16
I32 = jnp.int32
VLIM = 62 * 1024 * 1024

NT = (((1,), (1,)), ((), ()))
NN = (((1,), (0,)), ((), ()))


def wave(product):
    angle = 2.0 * math.pi * np.mod(product, L) / L
    return np.cos(angle).astype(np.float32), np.sin(angle).astype(np.float32)


def make_tables():
    ids = np.arange(L)
    ct, st = wave(ids[:, None] * (ids[None, :] - HALF))
    shift = np.arange(PRIOR) - PRIOR // 2 - GRID // 2
    pr = np.concatenate(wave(shift[:, None] * (ids[None, :] - HALF)), axis=1)
    tiles = lambda a: np.ascontiguousarray(a.reshape(L, 3, 128).transpose(1, 0, 2))
    return np.stack([tiles(ct), tiles(st)]), pr


def remote(src, dst, send, recv, img, slab):
    return pltpu.make_async_remote_copy(
        src_ref=src,
        dst_ref=dst,
        send_sem=send,
        recv_sem=recv,
        device_id={"img": img, "slab": slab},
        device_id_type=pl.DeviceIdType.MESH,
    )


def drain(ref, sem):
    pltpu.make_async_copy(ref, ref, sem).wait()


def dot(a, b, dims=NN):
    return lax.dot_general(a, b, dims, preferred_element_type=F32)


def dot_full(a, b, dims=NN):
    return lax.dot_general(a, b, dims, precision=PRECISE, preferred_element_type=F32)


def halves(a):
    high = a.astype(BF16)
    return high, (a - high.astype(F32)).astype(BF16)


def dot_split(ah, al, bh, bl, dims):
    return dot(ah, bh, dims) + (dot(ah, bl, dims) + dot(al, bh, dims))


def iota(shape, axis):
    return lax.broadcasted_iota(I32, shape, axis)


def count(index, step, top):
    total = jnp.zeros_like(index)
    for edge in range(step, top, step):
        total += (index >= edge).astype(I32)
    return total


def plane_ids(index, zh):
    return index + 48 * count(index, 48, 192) + 48 * zh


def planes_of(orient, row):
    return (((row - HALF) * (orient - NORIENT // 2)) >> 11) + HALF


def power(n):
    total = jnp.ones(n.shape, F32)
    for bit in range(7):
        total *= jnp.where((n >> bit) & 1 == 1, 2.0 ** (2**bit), 1.0)
    return total


def pack(tiles):
    peak = jnp.maximum(jnp.maximum(jnp.abs(tiles[0]), jnp.abs(tiles[1])), jnp.abs(tiles[2]))
    peak = jnp.maximum(jnp.max(peak, axis=1, keepdims=True), 1e-30)
    level = jnp.ceil(jnp.log(peak) * (1.0 / math.log(2.0)) + 0.01)
    level = jnp.clip(level, -100.0, 20.0).astype(I32) + 101
    gain = power(121 - level)
    q0, q1, q2 = (jnp.floor(tile * gain + 0.5).astype(I32) for tile in tiles)
    flag = (level >> (iota(tiles[0].shape, 1) & 31)) & 1
    return (q0 << 11) | ((q2 >> 10) & 2047), (q1 << 11) | ((q2 & 1023) << 1) | flag


def unpack(one, two):
    lane = iota(one.shape, 1)
    flag = jnp.where(lane < 8, (two & 1) << (lane & 7), 0).astype(F32)
    level = jnp.sum(flag, axis=1, keepdims=True).astype(I32)
    gain = power(level) * 2.0**-121
    third = ((one & 2047) << 10) | ((two >> 1) & 1023)
    return [v.astype(F32) * gain for v in (one >> 11, two >> 11, (third << 11) >> 11)]


def whole(tab, part):
    return jnp.concatenate([tab[part, n] for n in range(3)], axis=1)


def kernel(
    img_in, vol_in, orient_in, prior_in, noise_in, tab_in, pr,
    out,
    meta, pics, vol, tab, strip, strips, a, volb, voll, xd, vbd, vld, md, tt, wt,
    exh, exl, ezh, ezl, eyh, eyl, puts, shares, sc, parts, sums, w, mh, ml, lines, g, r, d, other, total,
    load, spread_send, spread_recv, own, post_send, post_recv,
    plane_send, plane_recv, swap_send, swap_recv, out_send, out_recv,
):
    img = lax.axis_index("img")
    slab = lax.axis_index("slab")
    zl, x, zh = img // 8, slab // 2, slab % 2
    q, core, yc = img // 2, img % 2, img % 8
    z = zh * 4 + zl
    me = q * 8 + slab

    loads = [
        pltpu.make_async_copy(src, dst, load.at[n])
        for n, (src, dst) in enumerate(((vol_in, vol), (img_in, pics), (tab_in, tab)))
    ]
    for copy in loads:
        copy.start()

    barrier = pltpu.get_barrier_semaphore()
    sheet = z * 8 + yc

    def greet(k, carry):
        to = (sheet + k) % 64
        pl.semaphore_signal(
            barrier,
            inc=1,
            device_id={"img": (to // 8) % 4 * 8 + to % 8, "slab": 2 * x + to // 32},
            device_id_type=pl.DeviceIdType.MESH,
        )
        return carry

    lax.fori_loop(1, 64, greet, 0)
    for k in range(1, 4):
        pl.semaphore_signal(
            barrier,
            inc=1,
            device_id={"img": img, "slab": 2 * ((x + k) % 4) + zh},
            device_id_type=pl.DeviceIdType.MESH,
        )

    entry, item = iota((8, 128), 0), iota((8, 128), 1)
    facts = jnp.zeros((8, 128), F32)
    for n in range(8):
        for m, ref in enumerate((orient_in, prior_in, noise_in)):
            here = jnp.logical_and(entry == n, item == m)
            facts = jnp.where(here, ref[n].astype(F32), facts)
    meta[...] = facts

    loads[0].wait()
    for c in range(2):

        def cast(j, carry, c=c):
            volb[c, j], voll[c, j] = halves(vol[c, j])
            return carry

        lax.fori_loop(0, 12, cast, 0)
    loads[1].wait()

    def widen(n, carry):
        for c in range(2):
            for t in range(3):
                strip[n, c, t] = pics[n, c, :, 128 * t : 128 * t + 128].astype(F32)
        return carry

    lax.fori_loop(0, 8, widen, 0)

    def sort_images(j, carry):
        def gather(n, inner):
            for c in range(2):
                for t in range(3):
                    strips[c, t, pl.ds(n, 32, stride=8), :] = strip[
                        n, c, t, pl.ds(3 * x + j, 32, stride=12), :
                    ]
            return inner

        lax.fori_loop(0, 8, gather, 0)
        for c in range(2):
            rows = jnp.concatenate([strips[c, t] for t in range(3)], axis=1)
            a[j, :, c] = rows.reshape(32, 8, L).astype(BF16)
        return carry

    sort_images(0, 0)
    pl.semaphore_wait(barrier, 66)

    def send_map(src, dst, n):
        for k in range(1, 4):
            to = (x + k) % 4
            remote(
                src.at[:, pl.ds(3 * to, 3)], dst.at[x],
                spread_send.at[n], spread_recv.at[n], img, 2 * to + zh,
            ).start()

    def send_images(j, carry):
        for turn in (2, 6, 1, 7, 0):
            to_z = (z + turn) % 8

            def spread(k, inner, turn=turn, to_z=to_z):
                to = (to_z % 4) * 8 + (yc + k) % 8
                to_slab = 2 * x + to_z // 4
                if turn in (2, 6):
                    c = 0 if turn == 2 else 1
                    src, dst = a.at[j, to, c], xd.at[j, img, c]
                else:
                    src, dst = a.at[j, to], xd.at[j, img]
                remote(src, dst, spread_send.at[j], spread_recv.at[j], to, to_slab).start()
                return inner

            lax.fori_loop(1 if turn == 0 else 0, 8, spread, 0)
        pltpu.make_async_copy(a.at[j, img], xd.at[j, img], own.at[j]).start()
        return carry

    send_map(volb, vbd, 3)
    for turn in (2, 1, 7, 0):
        to_z = (z + turn) % 8

        def send_meta(k, carry, to_z=to_z):
            to = (to_z % 4) * 8 + (yc + k) % 8
            remote(
                meta, md.at[img], spread_send.at[5], spread_recv.at[5], to, 2 * x + to_z // 4
            ).start()
            return carry

        lax.fori_loop(1 if turn == 0 else 0, 8, send_meta, 0)
    send_images(0, 0)

    def next_images(j, carry):
        return send_images(j, sort_images(j, carry))

    lax.fori_loop(1, 3, next_images, 0)
    mine = [
        pltpu.make_async_copy(src, dst, own.at[3 + n])
        for n, (src, dst) in enumerate(
            (
                (volb.at[:, pl.ds(3 * x, 3)], vbd.at[x]),
                (voll.at[:, pl.ds(3 * x, 3)], vld.at[x]),
                (meta, md.at[img]),
            )
        )
    ]
    for copy in mine:
        copy.start()

    loads[2].wait()
    ct, st = whole(tab, 0), whole(tab, 1)
    cell = iota((256, GRID), 0)
    step = iota((256, GRID), 1)
    in_b = jnp.where((cell & 15) == step, 1.0, 0.0).astype(F32)
    in_a = jnp.where((cell >> 4) == step, 1.0, 0.0).astype(F32)
    col_c, col_s = dot_full(in_b, ct[:GRID]), dot_full(in_b, st[:GRID])
    row_ids = iota((L, 128), 0)
    at_rows = jnp.where(row_ids == 12 * img + 3 * x + iota((L, 128), 1), 1.0, 0.0).astype(F32)
    row_c = dot_full(in_a, dot_full(ct[:GRID], at_rows))
    row_s = dot_full(in_a, dot_full(st[:GRID], at_rows))
    for j in range(3):
        rc, rs = row_c[:, j : j + 1], row_s[:, j : j + 1]
        wt[j, :, :L] = col_c * rc - col_s * rs
        wt[j, :, L:] = col_s * rc + col_c * rs

    drain(md.at[pl.ds(0, 31)], spread_recv.at[5])
    mine[2].wait()
    values = md[...].reshape(256, 128)
    orient = values[:, 0:1].astype(I32)
    prior = values[:, 1:2].astype(I32)
    values_t = values.T
    orient_row = values_t[0:1, :].astype(I32)
    ids = iota((256, PRIOR), 1)
    in_cols = jnp.where((prior & 7) == ids, 1.0, 0.0).astype(F32)
    in_rows = jnp.where((prior >> 3) == ids, 1.0, 0.0).astype(F32)
    turn_c, turn_s = dot_full(in_cols, pr[:, :L]), dot_full(in_cols, pr[:, L:])
    row_turn_c = dot_full(in_rows, dot_full(pr[:, :L], at_rows))
    row_turn_s = dot_full(in_rows, dot_full(pr[:, L:], at_rows))
    for j in range(3):
        rc, rs = row_turn_c[:, j : j + 1], row_turn_s[:, j : j + 1]
        tt[j, 0] = turn_c * rc - turn_s * rs
        tt[j, 1] = turn_c * rs + turn_s * rc

    drain(vbd.at[pl.ds(0, 3)], spread_recv.at[3])
    mine[0].wait()
    send_map(voll, vld, 4)
    first = 12 * img + 3 * x
    zid_row = plane_ids(iota((1, 192), 1), zh)
    zid_col = plane_ids(iota((192, 1), 0), zh)

    def picture(j, c):
        return xd[j, :, c].astype(F32).reshape(256, L)

    sc[...] = jnp.zeros_like(sc)

    def score(j, carry):
        drain(xd.at[j, pl.ds(0, 31)], spread_recv.at[j])
        pltpu.make_async_copy(xd.at[j, 0], xd.at[j, 0], own.at[j]).wait()
        pick = jnp.where(planes_of(orient, first + j) == zid_row, 1.0, 0.0).astype(BF16)
        sr, si = (
            dot(pick, jnp.concatenate([vbd[b, c, j] for b in range(4)], axis=0))
            for c in range(2)
        )
        xr, xi = picture(j, 0), picture(j, 1)
        tr, ti = tt[j, 0], tt[j, 1]
        rr, ii, ri, ir = xr * tr, xi * ti, xr * ti, xi * tr
        tr, ti = rr - ii, ri + ir
        tt[j, 0] = rr + ii
        tt[j, 1] = ir - ri
        lhs = jnp.concatenate([sr * tr + si * ti, si * tr - sr * ti], axis=1)
        sc[...] += dot_full(lhs, wt[j], NT).reshape(32, 8, 256)
        return carry

    lax.fori_loop(0, 3, score, 0)

    def send_parts(k, carry):
        to = (img + k) % 32
        remote(sc.at[to], parts.at[img], post_send.at[0], post_recv.at[0], to, slab).start()
        return carry

    lax.fori_loop(1, 32, send_parts, 0)
    parts[img] = sc[img]

    lane = iota((L, 2 * L), 1)
    spot = lane % L
    is_re = jnp.logical_or(spot < 128, jnp.logical_and(spot >= 128, spot < 192))
    local = jnp.where(spot < 192, spot, jnp.where(spot < 256, spot - 64, spot - 256))
    kz = local + 48 * count(local, 48, 192) + 48 * (lane >= L).astype(I32)
    pick_z = jnp.where(iota((L, 2 * L), 0) == kz, 1.0, 0.0).astype(BF16)
    cth, ctl = halves(ct)
    sth, stl = halves(st)
    re_z = is_re[:1]
    for dst, c_part, s_part in ((ezh, cth, sth), (ezl, ctl, stl)):
        cz, sz = dot(c_part, pick_z), dot(s_part, pick_z)
        dst[:L] = jnp.where(re_z, cz, -sz).astype(BF16)
        dst[L:] = jnp.where(re_z, sz, cz).astype(BF16)
    lane = iota((L, L), 1)
    local = jnp.where(lane < 192, lane, lane - 192)
    ky = local + 12 * count(local, 12, 192) + 12 * core
    pick_y = jnp.where(iota((L, L), 0) == ky, 1.0, 0.0).astype(BF16)
    re_y = (lane < 192)[:1]
    for dst, c_part, s_part in ((eyh, cth, sth), (eyl, ctl, stl)):
        dst[...] = jnp.where(re_y, dot(c_part, pick_y), -dot(s_part, pick_y)).astype(BF16)
    for k in range(3):
        cx, sx = (
            jnp.concatenate([tab[p, t, pl.ds(k, 128, stride=3), :] for t in range(3)], axis=1)
            for p in range(2)
        )
        for n, (left, right) in enumerate(((cx, -sx), (sx, cx))):
            for side, value in enumerate((left, right)):
                high, low = halves(value)
                exh[k, 128 * n : 128 * n + 128, L * side : L * side + L] = high
                exl[k, 128 * n : 128 * n + 128, L * side : L * side + L] = low

    for j in range(3):
        hit = jnp.where(planes_of(orient_row, first + j) == zid_col, 1.0, 0.0).astype(F32)
        puts[j] = hit.astype(BF16)
        share = 1.0 / (jnp.sum(hit, axis=1, keepdims=True) + 1.0)
        shares[j] = jnp.broadcast_to(share, (192, L))

    drain(parts.at[pl.ds(0, 31)], post_recv.at[0])
    sums[slab] = jnp.sum(parts[...], axis=0)

    def send_sums(k, carry):
        to = (slab + k) % 8
        remote(sums.at[slab], sums.at[slab], post_send.at[1], post_recv.at[1], img, to).start()
        return carry

    lax.fori_loop(1, 8, send_sums, 0)
    drain(sums.at[pl.ds(0, 7)], post_recv.at[1])
    logits = jnp.sum(sums[...], axis=0) / (2.0 * meta[:, 2:3])
    expo = jnp.exp(logits - jnp.max(logits, axis=1, keepdims=True))
    w[img] = expo / jnp.sum(expo, axis=1, keepdims=True)

    def send_weights(k, carry):
        to = (img + k) % 32
        remote(w.at[img], w.at[img], post_send.at[2], post_recv.at[2], to, slab).start()
        return carry

    lax.fori_loop(1, 32, send_weights, 0)
    drain(vld.at[pl.ds(0, 3)], spread_recv.at[4])
    mine[1].wait()
    drain(w.at[pl.ds(0, 31)], post_recv.at[2])

    def merge(j, carry):
        f = dot_full(w[...].reshape(256, 256), wt[j])
        fr, fi = f[:, :L], f[:, L:]
        xr, xi = tt[j, 0], tt[j, 1]
        for c, part in enumerate((xr * fr + xi * fi, xi * fr - xr * fi)):
            back = dot(puts[j], part.astype(BF16))
            rows = jnp.concatenate(
                [vbd[b, c, j].astype(F32) + vld[b, c, j].astype(F32) for b in range(4)], axis=0
            )
            high, low = halves((back + rows) * shares[j])
            mh[j, :, L * c : L * c + L] = high
            ml[j, :, L * c : L * c + L] = low
        return carry

    lax.fori_loop(0, 3, merge, 0)

    for k in range(3):

        def x_lines(j, carry, k=k):
            gx = dot_split(exh[k], exl[k], mh[j], ml[j], NT)
            re, im = gx[:128], gx[128:]
            tiles = (
                re[:, :128],
                jnp.concatenate([re[:, 128:], im[:, 128:]], axis=1),
                im[:, :128],
            )
            for t in range(3):
                lines[t, pl.ds(j, 128, stride=3), :] = tiles[t]
            return carry

        lax.fori_loop(0, 3, x_lines, 0)
        g[k, 0], g[k, 1] = pack([lines[t] for t in range(3)])
        land = r.at[k, pl.ds(2 * zh, 2), pl.ds(3 * (4 * q + x), 3)]

        def send_lines(n, carry, k=k, land=land):
            to = (me + n) % 128
            remote(
                g.at[k, :, pl.ds(3 * to, 3)], land,
                plane_send.at[k], plane_recv.at[k], 2 * (to // 8) + core, to % 8,
            ).start()
            return carry

        lax.fori_loop(1, 128, send_lines, 0)
        pltpu.make_async_copy(g.at[k, :, pl.ds(3 * me, 3)], land, own.at[6 + k]).start()

    to = 2 * q + slab // 4

    def deliver(k):
        place = out.at[3 * (slab % 4) + k]
        for n in range(4):
            here = jnp.logical_and(to == img, 4 * core + n == slab)

            @pl.when(here)
            def _(n=n):
                pltpu.make_async_copy(total.at[k, n], place, out_recv).start()

            @pl.when(jnp.logical_not(here))
            def _(n=n):
                remote(
                    total.at[k, n], place, out_send.at[n], out_recv, to, 4 * core + n
                ).start()

    for k in range(3):
        pltpu.make_async_copy(
            g.at[k, :, pl.ds(0, 3)], g.at[k, :, pl.ds(0, 3)], own.at[6 + k]
        ).wait()
        drain(g.at[k, :, pl.ds(0, 381)], plane_recv.at[k])
        if k == 2:
            deliver(0)
            deliver(1)
        columns = unpack(r[k, 0], r[k, 1]) + unpack(r[k, 2], r[k, 3])
        th, tl = halves(jnp.concatenate(columns, axis=1))
        u = dot_split(th, tl, ezh[...], ezl[...], NT)
        uh, ul = halves(jnp.concatenate([u[:, :L], u[:, L:]], axis=0))
        theirs, ours = pl.ds(192 * (1 - core), 192), pl.ds(192 * core, 192)
        d[k] = dot_split(eyh[theirs], eyl[theirs], uh, ul, NN).reshape(4, 48, L)
        swap = remote(
            d.at[k], other.at[k], swap_send.at[k], swap_recv.at[k], 2 * q + 1 - core, slab
        )
        swap.start()
        done = dot_split(eyh[ours], eyl[ours], uh, ul, NN)
        swap.wait()
        done = (done + other[k].reshape(192, L)) * SCALE
        words = pack([done[:, :128], done[:, 128:256], done[:, 256:]])
        for n in range(2):
            total[k, :, n] = words[n].reshape(4, 48, 128)
        if k == 2:
            deliver(2)

    for j in range(3):
        drain(a.at[j, pl.ds(0, 31)], spread_send.at[j])
    drain(vbd.at[pl.ds(0, 3)], spread_send.at[3])
    drain(vld.at[pl.ds(0, 3)], spread_send.at[4])
    drain(md.at[pl.ds(0, 31)], spread_send.at[5])
    drain(parts.at[pl.ds(0, 31)], post_send.at[0])
    drain(sums.at[pl.ds(0, 7)], post_send.at[1])
    drain(w.at[pl.ds(0, 31)], post_send.at[2])
    for k in range(3):
        drain(g.at[k, :, pl.ds(0, 381)], plane_send.at[k])
    for n in range(4):
        here = jnp.logical_and(to == img, 4 * core + n == slab)

        @pl.when(jnp.logical_not(here))
        def _(n=n):
            drain(total.at[:, n], out_send.at[n])

    drain(out, out_recv)


def open_kernel(words, out):
    one, two = (words[:, m].reshape(144, 128) for m in range(2))
    out[...] = jnp.concatenate(unpack(one, two), axis=1).reshape(3, 48, L)


ANY = pl.BlockSpec(memory_space=pl.ANY)
VMEM = pl.BlockSpec(memory_space=pltpu.VMEM)
DMA = pltpu.SemaphoreType.DMA


def per_device(images, volume, orient, prior_shift, noise_var):
    tab, pr = make_tables()
    vol = jnp.transpose(volume, (0, 2, 1, 3))
    buf = pltpu.VMEM
    scratch = [
        buf((8, 128), F32),
        buf((8, 2, L, L), BF16),
        buf((2, 12, 48, L), F32),
        buf((2, 3, L, 128), F32),
        buf((8, 2, 3, L, 128), F32),
        buf((2, 3, 256, 128), F32),
        buf((3, 32, 2, 8, L), BF16),
        buf((2, 12, 48, L), BF16),
        buf((2, 12, 48, L), BF16),
        buf((3, 32, 2, 8, L), BF16),
        buf((4, 2, 3, 48, L), BF16),
        buf((4, 2, 3, 48, L), BF16),
        buf((32, 8, 128), F32),
        buf((3, 2, 256, L), F32),
        buf((3, 256, 2 * L), F32),
        buf((3, 256, 2 * L), BF16),
        buf((3, 256, 2 * L), BF16),
        buf((2 * L, 2 * L), BF16),
        buf((2 * L, 2 * L), BF16),
        buf((L, L), BF16),
        buf((L, L), BF16),
        buf((3, 192, 256), BF16),
        buf((3, 192, L), F32),
        buf((32, 8, 256), F32),
        buf((32, 8, 256), F32),
        buf((8, 8, 256), F32),
        buf((32, 8, 256), F32),
        buf((3, 192, 2 * L), BF16),
        buf((3, 192, 2 * L), BF16),
        buf((3, L, 128), F32),
        buf((3, 2, L, 128), I32),
        buf((3, 4, 192, 128), I32),
        buf((3, 4, 48, L), F32),
        buf((3, 4, 48, L), F32),
        buf((3, 4, 2, 48, 128), I32),
        DMA((3,)),
        DMA((6,)),
        DMA((6,)),
        DMA((9,)),
        DMA((3,)),
        DMA((3,)),
        DMA((3,)),
        DMA((3,)),
        DMA((3,)),
        DMA((3,)),
        DMA((4,)),
        DMA(()),
    ]
    smem = pl.BlockSpec(memory_space=pltpu.SMEM)
    words = pl.pallas_call(
        kernel,
        out_shape=jax.ShapeDtypeStruct((12, 2, 48, 128), I32),
        in_specs=[ANY, ANY, smem, smem, smem, ANY, VMEM],
        out_specs=VMEM,
        scratch_shapes=scratch,
        compiler_params=pltpu.CompilerParams(
            vmem_limit_bytes=VLIM, has_side_effects=True, collective_id=0
        ),
        name="step",
    )(images, vol, orient, prior_shift, noise_var, tab, pr)
    return pl.pallas_call(
        open_kernel,
        out_shape=jax.ShapeDtypeStruct((12, 48, L), F32),
        grid=(4,),
        in_specs=[pl.BlockSpec((3, 2, 48, 128), lambda n: (n, 0, 0, 0))],
        out_specs=pl.BlockSpec((3, 48, L), lambda n: (n, 0, 0)),
        name="open",
    )(words)


def solution(mesh):
    return jax.shard_map(
        per_device,
        mesh=mesh,
        in_specs=(
            P("img", None, None, None),
            P(None, "slab", "img", None),
            P("img"),
            P("img"),
            P("img"),
        ),
        out_specs=P("img", "slab", None),
        check_vma=False,
    )
```

```python
import math

import jax
import jax.numpy as jnp
import numpy as np
from jax import lax
from jax.experimental import pallas as pl
from jax.experimental.pallas import tpu as pltpu
from jax.sharding import PartitionSpec as P

GRID = 16
PRIOR = 8
NORIENT = 4096
L = 384
HALF = L // 2
SCALE = L ** (-1.5)
PRECISE = lax.Precision.HIGHEST
F32 = jnp.float32
BF16 = jnp.bfloat16
I32 = jnp.int32
VLIM = 62 * 1024 * 1024

NT = (((1,), (1,)), ((), ()))
NN = (((1,), (0,)), ((), ()))


def wave(product):
    angle = 2.0 * math.pi * np.mod(product, L) / L
    return np.cos(angle).astype(np.float32), np.sin(angle).astype(np.float32)


def thirds(a):
    high = a.astype(BF16)
    rest = a - high.astype(np.float32)
    middle = rest.astype(BF16)
    return high, middle, (rest - middle.astype(np.float32)).astype(BF16)


def make_tables():
    ids = np.arange(L)
    ct, st = wave(ids[:, None] * (ids[None, :] - HALF))
    shift = np.arange(PRIOR) - PRIOR // 2 - GRID // 2
    turns = wave(shift[:, None] * (ids[None, :] - HALF))
    small = thirds(np.concatenate([ct[:GRID], st[:GRID], turns[0], turns[1]], axis=0))
    cols = np.concatenate(
        [
            np.concatenate([ct[:GRID], st[:GRID]], axis=1),
            np.concatenate([-st[:GRID], ct[:GRID]], axis=1),
        ],
        axis=0,
    )
    high, middle, low = thirds(cols)
    cols = np.concatenate([high, middle, high, middle, low, high], axis=0)
    tiles = lambda a: np.ascontiguousarray(a.reshape(L, 3, 128).transpose(1, 0, 2))
    return np.stack([tiles(ct), tiles(st)]), np.stack(small), cols


def remote(src, dst, send, recv, img, slab):
    return pltpu.make_async_remote_copy(
        src_ref=src,
        dst_ref=dst,
        send_sem=send,
        recv_sem=recv,
        device_id={"img": img, "slab": slab},
        device_id_type=pl.DeviceIdType.MESH,
    )


def drain(ref, sem):
    pltpu.make_async_copy(ref, ref, sem).wait()


def dot(a, b, dims=NN):
    return lax.dot_general(a, b, dims, preferred_element_type=F32)


def dot_full(a, b, dims=NN):
    return lax.dot_general(a, b, dims, precision=PRECISE, preferred_element_type=F32)


def halves(a):
    high = a.astype(BF16)
    return high, (a - high.astype(F32)).astype(BF16)


def dot_split(ah, al, bh, bl, dims):
    return dot(ah, bh, dims) + (dot(ah, bl, dims) + dot(al, bh, dims))


def iota(shape, axis):
    return lax.broadcasted_iota(I32, shape, axis)


def count(index, step, top):
    total = jnp.zeros_like(index)
    for edge in range(step, top, step):
        total += (index >= edge).astype(I32)
    return total


def plane_ids(index, zh):
    return index + 48 * count(index, 48, 192) + 48 * zh


def planes_of(orient, row):
    return (((row - HALF) * (orient - NORIENT // 2)) >> 11) + HALF


def power(n):
    total = jnp.ones(n.shape, F32)
    for bit in range(7):
        total *= jnp.where((n >> bit) & 1 == 1, 2.0 ** (2**bit), 1.0)
    return total


def pack(tiles):
    peak = jnp.maximum(jnp.maximum(jnp.abs(tiles[0]), jnp.abs(tiles[1])), jnp.abs(tiles[2]))
    peak = jnp.maximum(jnp.max(peak, axis=1, keepdims=True), 1e-30)
    level = jnp.ceil(jnp.log(peak) * (1.0 / math.log(2.0)) + 0.01)
    level = jnp.clip(level, -100.0, 20.0).astype(I32) + 101
    gain = power(121 - level)
    q0, q1, q2 = (jnp.floor(tile * gain + 0.5).astype(I32) for tile in tiles)
    flag = (level >> (iota(tiles[0].shape, 1) & 31)) & 1
    return (q0 << 11) | ((q2 >> 10) & 2047), (q1 << 11) | ((q2 & 1023) << 1) | flag


def unpack(one, two):
    lane = iota(one.shape, 1)
    flag = jnp.where(lane < 8, (two & 1) << (lane & 7), 0).astype(F32)
    level = jnp.sum(flag, axis=1, keepdims=True).astype(I32)
    gain = power(level) * 2.0**-121
    third = ((one & 2047) << 10) | ((two >> 1) & 1023)
    return [v.astype(F32) * gain for v in (one >> 11, two >> 11, (third << 11) >> 11)]


def whole(tab, part):
    return jnp.concatenate([tab[part, n] for n in range(3)], axis=1)


def kernel(
    img_in, vol_in, orient_in, prior_in, noise_in, tab_in, small, cols,
    out,
    meta, pics, vol, tab, strip, strips, a, volb, voll, xd, vbd, vld, md, tt, wt,
    exh, exl, ezh, ezl, eyh, eyl, rt, puts, shares, sc, parts, sums, w, mh, ml, lines, g, r, d, other, total,
    load, spread_send, spread_recv, own, post_send, post_recv,
    plane_send, plane_recv, swap_send, swap_recv, out_send, out_recv,
):
    img = lax.axis_index("img")
    slab = lax.axis_index("slab")
    zl, x, zh = img // 8, slab // 2, slab % 2
    q, core, yc = img // 2, img % 2, img % 8
    z = zh * 4 + zl
    me = q * 8 + slab

    loads = [
        pltpu.make_async_copy(src, dst, load.at[n])
        for n, (src, dst) in enumerate(((vol_in, vol), (img_in, pics), (tab_in, tab)))
    ]
    for copy in loads:
        copy.start()

    barrier = pltpu.get_barrier_semaphore()
    for turn in (2, 6, 1, 7, 0):
        to_z = (z + turn) % 8

        def greet(k, carry, to_z=to_z):
            pl.semaphore_signal(
                barrier,
                inc=1,
                device_id={"img": to_z % 4 * 8 + (yc + k) % 8, "slab": 2 * x + to_z // 4},
                device_id_type=pl.DeviceIdType.MESH,
            )
            return carry

        lax.fori_loop(1 if turn == 0 else 0, 8, greet, 0)
    for k in range(1, 4):
        pl.semaphore_signal(
            barrier,
            inc=1,
            device_id={"img": img, "slab": 2 * ((x + k) % 4) + zh},
            device_id_type=pl.DeviceIdType.MESH,
        )

    entry, item = iota((8, 128), 0), iota((8, 128), 1)
    facts = jnp.zeros((8, 128), F32)
    for n in range(8):
        for m, ref in enumerate((orient_in, prior_in, noise_in)):
            here = jnp.logical_and(entry == n, item == m)
            facts = jnp.where(here, ref[n].astype(F32), facts)
    meta[...] = facts

    loads[0].wait()
    for c in range(2):

        def cast(j, carry, c=c):
            volb[c, j], voll[c, j] = halves(vol[c, j])
            return carry

        lax.fori_loop(0, 12, cast, 0)
    loads[1].wait()

    def widen(n, carry):
        for c in range(2):
            for t in range(3):
                strip[n, c, t] = pics[n, c, :, 128 * t : 128 * t + 128].astype(F32)
        return carry

    lax.fori_loop(0, 8, widen, 0)

    def sort_images(j, carry):
        def gather(n, inner):
            for c in range(2):
                for t in range(3):
                    strips[c, t, pl.ds(n, 32, stride=8), :] = strip[
                        n, c, t, pl.ds(3 * x + j, 32, stride=12), :
                    ]
            return inner

        lax.fori_loop(0, 8, gather, 0)
        for c in range(2):
            rows = jnp.concatenate([strips[c, t] for t in range(3)], axis=1)
            a[j, :, c] = rows.reshape(32, 8, L).astype(BF16)
        return carry

    sort_images(0, 0)
    pl.semaphore_wait(barrier, 42)

    def send_map(src, dst, n):
        for k in range(1, 4):
            to = (x + k) % 4
            remote(
                src.at[:, pl.ds(3 * to, 3)], dst.at[x],
                spread_send.at[n], spread_recv.at[n], img, 2 * to + zh,
            ).start()

    def send_images(j, carry):
        for turn in (2, 6, 1, 7, 0):
            to_z = (z + turn) % 8

            def spread(k, inner, turn=turn, to_z=to_z):
                to = (to_z % 4) * 8 + (yc + k) % 8
                to_slab = 2 * x + to_z // 4
                if turn in (2, 6):
                    c = 0 if turn == 2 else 1
                    src, dst = a.at[j, to, c], xd.at[j, img, c]
                else:
                    src, dst = a.at[j, to], xd.at[j, img]
                remote(src, dst, spread_send.at[j], spread_recv.at[j], to, to_slab).start()
                return inner

            lax.fori_loop(1 if turn == 0 else 0, 8, spread, 0)
        pltpu.make_async_copy(a.at[j, img], xd.at[j, img], own.at[j]).start()
        return carry

    send_map(volb, vbd, 3)
    for turn in (2, 1, 7, 0):
        to_z = (z + turn) % 8

        def send_meta(k, carry, to_z=to_z):
            to = (to_z % 4) * 8 + (yc + k) % 8
            remote(
                meta, md.at[img], spread_send.at[5], spread_recv.at[5], to, 2 * x + to_z // 4
            ).start()
            return carry

        lax.fori_loop(1 if turn == 0 else 0, 8, send_meta, 0)
    send_images(0, 0)

    def next_images(j, carry):
        return send_images(j, sort_images(j, carry))

    lax.fori_loop(1, 3, next_images, 0)
    mine = [
        pltpu.make_async_copy(src, dst, own.at[3 + n])
        for n, (src, dst) in enumerate(
            (
                (volb.at[:, pl.ds(3 * x, 3)], vbd.at[x]),
                (voll.at[:, pl.ds(3 * x, 3)], vld.at[x]),
                (meta, md.at[img]),
            )
        )
    ]
    for copy in mine:
        copy.start()

    loads[2].wait()
    cell = iota((256, 3 * GRID), 0)
    step = iota((256, 3 * GRID), 1) & 15
    in_b = jnp.where((cell & 15) == step, 1.0, 0.0).astype(BF16)
    in_a = jnp.where((cell >> 4) == step, 1.0, 0.0).astype(BF16)

    def parts_of(first, size):
        return jnp.concatenate([small[n, first : first + size] for n in range(3)], axis=0)

    def stacked(a):
        high, middle = halves(a)
        low = (a - high.astype(F32) - middle.astype(F32)).astype(BF16)
        return jnp.concatenate([high, middle, low], axis=0)

    col_c, col_s = dot(in_b, parts_of(0, GRID)), dot(in_b, parts_of(GRID, GRID))
    row_ids = iota((L, 128), 0)
    at_rows = jnp.where(row_ids == 12 * img + 3 * x + iota((L, 128), 1), 1.0, 0.0).astype(BF16)
    here = dot(small[0], at_rows) + dot(small[1], at_rows) + dot(small[2], at_rows)
    row_c = dot(in_a, stacked(here[:GRID]))
    row_s = dot(in_a, stacked(here[GRID : 2 * GRID]))
    for j in range(3):
        rc, rs = row_c[:, j : j + 1], row_s[:, j : j + 1]
        wt[j, :, :L] = col_c * rc - col_s * rs
        wt[j, :, L:] = col_s * rc + col_c * rs

    drain(md.at[pl.ds(0, 31)], spread_recv.at[5])
    mine[2].wait()
    values = md[...].reshape(256, 128)
    orient = values[:, 0:1].astype(I32)
    prior = values[:, 1:2].astype(I32)
    values_t = values.T
    orient_row = values_t[0:1, :].astype(I32)
    ids = iota((256, 3 * PRIOR), 1) & 7
    in_cols = jnp.where((prior & 7) == ids, 1.0, 0.0).astype(BF16)
    in_rows = jnp.where((prior >> 3) == ids, 1.0, 0.0).astype(BF16)
    turn_c, turn_s = (dot(in_cols, parts_of(2 * GRID + PRIOR * n, PRIOR)) for n in range(2))
    row_turn_c, row_turn_s = (
        dot(in_rows, stacked(here[2 * GRID + PRIOR * n : 2 * GRID + PRIOR * n + PRIOR]))
        for n in range(2)
    )
    for j in range(3):
        rc, rs = row_turn_c[:, j : j + 1], row_turn_s[:, j : j + 1]
        tt[j, 0] = turn_c * rc - turn_s * rs
        tt[j, 1] = turn_c * rs + turn_s * rc

    drain(vbd.at[pl.ds(0, 3)], spread_recv.at[3])
    mine[0].wait()
    send_map(voll, vld, 4)
    first = 12 * img + 3 * x
    zid_row = plane_ids(iota((1, 192), 1), zh)
    zid_col = plane_ids(iota((192, 1), 0), zh)

    def picture(j, c):
        return xd[j, :, c].astype(F32).reshape(256, L)

    sc[...] = jnp.zeros_like(sc)

    def score(j, carry):
        drain(xd.at[j, pl.ds(0, 31)], spread_recv.at[j])
        pltpu.make_async_copy(xd.at[j, 0], xd.at[j, 0], own.at[j]).wait()
        pick = jnp.where(planes_of(orient, first + j) == zid_row, 1.0, 0.0).astype(BF16)
        sr, si = (
            dot(pick, jnp.concatenate([vbd[b, c, j] for b in range(4)], axis=0))
            for c in range(2)
        )
        xr, xi = picture(j, 0), picture(j, 1)
        tr, ti = tt[j, 0], tt[j, 1]
        rr, ii, ri, ir = xr * tr, xi * ti, xr * ti, xi * tr
        tr, ti = rr - ii, ri + ir
        tt[j, 0] = rr + ii
        tt[j, 1] = ir - ri
        lhs = jnp.concatenate([sr * tr + si * ti, si * tr - sr * ti], axis=1)
        sc[...] += dot_full(lhs, wt[j], NT).reshape(32, 8, 256)
        return carry

    lax.fori_loop(0, 3, score, 0)

    def send_parts(k, carry):
        to = (img + k) % 32
        remote(sc.at[to], parts.at[img], post_send.at[0], post_recv.at[0], to, slab).start()
        return carry

    lax.fori_loop(1, 32, send_parts, 0)
    parts[img] = sc[img]

    ct, st = whole(tab, 0), whole(tab, 1)
    lane = iota((256, 192), 1)
    same = ((iota((256, 192), 0) ^ lane) & 15) == 0
    for j in range(3):
        wave_of = jnp.where((lane & 16) == 0, row_c[:, j : j + 1], row_s[:, j : j + 1])
        rt[j] = jnp.where(same, wave_of, 0.0)
    lane = iota((L, 2 * L), 1)
    spot = lane % L
    is_re = jnp.logical_or(spot < 128, jnp.logical_and(spot >= 128, spot < 192))
    local = jnp.where(spot < 192, spot, jnp.where(spot < 256, spot - 64, spot - 256))
    kz = local + 48 * count(local, 48, 192) + 48 * (lane >= L).astype(I32)
    pick_z = jnp.where(iota((L, 2 * L), 0) == kz, 1.0, 0.0).astype(BF16)
    cth, ctl = halves(ct)
    sth, stl = halves(st)
    re_z = is_re[:1]
    for dst, c_part, s_part in ((ezh, cth, sth), (ezl, ctl, stl)):
        cz, sz = dot(c_part, pick_z), dot(s_part, pick_z)
        dst[:L] = jnp.where(re_z, cz, -sz).astype(BF16)
        dst[L:] = jnp.where(re_z, sz, cz).astype(BF16)
    lane = iota((L, L), 1)
    local = jnp.where(lane < 192, lane, lane - 192)
    ky = local + 12 * count(local, 12, 192) + 12 * core
    pick_y = jnp.where(iota((L, L), 0) == ky, 1.0, 0.0).astype(BF16)
    re_y = (lane < 192)[:1]
    for dst, c_part, s_part in ((eyh, cth, sth), (eyl, ctl, stl)):
        dst[...] = jnp.where(re_y, dot(c_part, pick_y), -dot(s_part, pick_y)).astype(BF16)
    for k in range(3):
        cx, sx = (
            jnp.concatenate([tab[p, t, pl.ds(k, 128, stride=3), :] for t in range(3)], axis=1)
            for p in range(2)
        )
        for n, (left, right) in enumerate(((cx, -sx), (sx, cx))):
            for side, value in enumerate((left, right)):
                high, low = halves(value)
                exh[k, 128 * n : 128 * n + 128, L * side : L * side + L] = high
                exl[k, 128 * n : 128 * n + 128, L * side : L * side + L] = low

    for j in range(3):
        hit = jnp.where(planes_of(orient_row, first + j) == zid_col, 1.0, 0.0).astype(F32)
        puts[j] = hit.astype(BF16)
        share = 1.0 / (jnp.sum(hit, axis=1, keepdims=True) + 1.0)
        shares[j] = jnp.broadcast_to(share, (192, L))

    drain(parts.at[pl.ds(0, 31)], post_recv.at[0])
    sums[slab] = jnp.sum(parts[...], axis=0)

    def send_sums(k, carry):
        to = (slab + k) % 8
        remote(sums.at[slab], sums.at[slab], post_send.at[1], post_recv.at[1], img, to).start()
        return carry

    lax.fori_loop(1, 8, send_sums, 0)
    drain(sums.at[pl.ds(0, 7)], post_recv.at[1])
    logits = jnp.sum(sums[...], axis=0) / (2.0 * meta[:, 2:3])
    expo = jnp.exp(logits - jnp.max(logits, axis=1, keepdims=True))
    w[img] = expo / jnp.sum(expo, axis=1, keepdims=True)

    def send_weights(k, carry):
        to = (img + k) % 32
        remote(w.at[img], w.at[img], post_send.at[2], post_recv.at[2], to, slab).start()
        return carry

    lax.fori_loop(1, 32, send_weights, 0)
    drain(vld.at[pl.ds(0, 3)], spread_recv.at[4])
    mine[1].wait()
    drain(w.at[pl.ds(0, 31)], post_recv.at[2])

    def merge(j, carry):
        rows = dot_full(w[...].reshape(256, 256), rt[j])
        high, middle = halves(rows)
        low = (rows - high.astype(F32) - middle.astype(F32)).astype(BF16)
        group = iota((256, 192), 1) >> 5
        use_middle = jnp.logical_or(group == 2, group == 3)
        rows = jnp.where(use_middle, middle.astype(F32), high.astype(F32))
        rows = jnp.where(group == 5, low.astype(F32), rows).astype(BF16)
        f = dot(rows, cols[...])
        fr, fi = f[:, :L], f[:, L:]
        xr, xi = tt[j, 0], tt[j, 1]
        for c, part in enumerate((xr * fr + xi * fi, xi * fr - xr * fi)):
            back = dot(puts[j], part.astype(BF16))
            rows = jnp.concatenate(
                [vbd[b, c, j].astype(F32) + vld[b, c, j].astype(F32) for b in range(4)], axis=0
            )
            high, low = halves((back + rows) * shares[j])
            mh[j, :, L * c : L * c + L] = high
            ml[j, :, L * c : L * c + L] = low
        return carry

    lax.fori_loop(0, 3, merge, 0)

    for k in range(3):

        def x_lines(j, carry, k=k):
            gx = dot_split(exh[k], exl[k], mh[j], ml[j], NT)
            re, im = gx[:128], gx[128:]
            tiles = (
                re[:, :128],
                jnp.concatenate([re[:, 128:], im[:, 128:]], axis=1),
                im[:, :128],
            )
            for t in range(3):
                lines[t, pl.ds(j, 128, stride=3), :] = tiles[t]
            return carry

        lax.fori_loop(0, 3, x_lines, 0)
        g[k, 0], g[k, 1] = pack([lines[t] for t in range(3)])
        land = r.at[k, pl.ds(2 * zh, 2), pl.ds(3 * (4 * q + x), 3)]

        def send_lines(n, carry, k=k, land=land):
            to = (me + n) % 128
            remote(
                g.at[k, :, pl.ds(3 * to, 3)], land,
                plane_send.at[k], plane_recv.at[k], 2 * (to // 8) + core, to % 8,
            ).start()
            return carry

        lax.fori_loop(1, 128, send_lines, 0)
        pltpu.make_async_copy(g.at[k, :, pl.ds(3 * me, 3)], land, own.at[6 + k]).start()

    to = 2 * q + slab // 4

    def deliver(k):
        place = out.at[3 * (slab % 4) + k]
        for n in range(4):
            here = jnp.logical_and(to == img, 4 * core + n == slab)

            @pl.when(here)
            def _(n=n):
                pltpu.make_async_copy(total.at[k, n], place, out_recv).start()

            @pl.when(jnp.logical_not(here))
            def _(n=n):
                remote(
                    total.at[k, n], place, out_send.at[n], out_recv, to, 4 * core + n
                ).start()

    for k in range(3):
        pltpu.make_async_copy(
            g.at[k, :, pl.ds(0, 3)], g.at[k, :, pl.ds(0, 3)], own.at[6 + k]
        ).wait()
        drain(g.at[k, :, pl.ds(0, 381)], plane_recv.at[k])
        if k == 2:
            deliver(0)
            deliver(1)
        columns = unpack(r[k, 0], r[k, 1]) + unpack(r[k, 2], r[k, 3])
        th, tl = halves(jnp.concatenate(columns, axis=1))
        u = dot_split(th, tl, ezh[...], ezl[...], NT)
        uh, ul = halves(jnp.concatenate([u[:, :L], u[:, L:]], axis=0))
        theirs, ours = pl.ds(192 * (1 - core), 192), pl.ds(192 * core, 192)
        d[k] = dot_split(eyh[theirs], eyl[theirs], uh, ul, NN).reshape(4, 48, L)
        swap = remote(
            d.at[k], other.at[k], swap_send.at[k], swap_recv.at[k], 2 * q + 1 - core, slab
        )
        swap.start()
        done = dot_split(eyh[ours], eyl[ours], uh, ul, NN)
        swap.wait()
        done = (done + other[k].reshape(192, L)) * SCALE
        words = pack([done[:, :128], done[:, 128:256], done[:, 256:]])
        for n in range(2):
            total[k, :, n] = words[n].reshape(4, 48, 128)
        if k == 2:
            deliver(2)

    for j in range(3):
        drain(a.at[j, pl.ds(0, 31)], spread_send.at[j])
    drain(vbd.at[pl.ds(0, 3)], spread_send.at[3])
    drain(vld.at[pl.ds(0, 3)], spread_send.at[4])
    drain(md.at[pl.ds(0, 31)], spread_send.at[5])
    drain(parts.at[pl.ds(0, 31)], post_send.at[0])
    drain(sums.at[pl.ds(0, 7)], post_send.at[1])
    drain(w.at[pl.ds(0, 31)], post_send.at[2])
    for k in range(3):
        drain(g.at[k, :, pl.ds(0, 381)], plane_send.at[k])
    for n in range(4):
        here = jnp.logical_and(to == img, 4 * core + n == slab)

        @pl.when(jnp.logical_not(here))
        def _(n=n):
            drain(total.at[:, n], out_send.at[n])

    drain(out, out_recv)


def open_kernel(words, out):
    for n in range(4):
        one, two = (words[3 * n : 3 * n + 3, m].reshape(144, 128) for m in range(2))
        value = jnp.concatenate(unpack(one, two), axis=1)
        out[3 * n : 3 * n + 3] = value.reshape(3, 48, L)


ANY = pl.BlockSpec(memory_space=pl.ANY)
VMEM = pl.BlockSpec(memory_space=pltpu.VMEM)
DMA = pltpu.SemaphoreType.DMA


def per_device(images, volume, orient, prior_shift, noise_var):
    tab, small, cols = make_tables()
    vol = jnp.transpose(volume, (0, 2, 1, 3))
    buf = pltpu.VMEM
    scratch = [
        buf((8, 128), F32),
        buf((8, 2, L, L), BF16),
        buf((2, 12, 48, L), F32),
        buf((2, 3, L, 128), F32),
        buf((8, 2, 3, L, 128), F32),
        buf((2, 3, 256, 128), F32),
        buf((3, 32, 2, 8, L), BF16),
        buf((2, 12, 48, L), BF16),
        buf((2, 12, 48, L), BF16),
        buf((3, 32, 2, 8, L), BF16),
        buf((4, 2, 3, 48, L), BF16),
        buf((4, 2, 3, 48, L), BF16),
        buf((32, 8, 128), F32),
        buf((3, 2, 256, L), F32),
        buf((3, 256, 2 * L), F32),
        buf((3, 256, 2 * L), BF16),
        buf((3, 256, 2 * L), BF16),
        buf((2 * L, 2 * L), BF16),
        buf((2 * L, 2 * L), BF16),
        buf((L, L), BF16),
        buf((L, L), BF16),
        buf((3, 256, 192), F32),
        buf((3, 192, 256), BF16),
        buf((3, 192, L), F32),
        buf((32, 8, 256), F32),
        buf((32, 8, 256), F32),
        buf((8, 8, 256), F32),
        buf((32, 8, 256), F32),
        buf((3, 192, 2 * L), BF16),
        buf((3, 192, 2 * L), BF16),
        buf((3, L, 128), F32),
        buf((3, 2, L, 128), I32),
        buf((3, 4, 192, 128), I32),
        buf((3, 4, 48, L), F32),
        buf((3, 4, 48, L), F32),
        buf((3, 4, 2, 48, 128), I32),
        DMA((3,)),
        DMA((6,)),
        DMA((6,)),
        DMA((9,)),
        DMA((3,)),
        DMA((3,)),
        DMA((3,)),
        DMA((3,)),
        DMA((3,)),
        DMA((3,)),
        DMA((4,)),
        DMA(()),
    ]
    smem = pl.BlockSpec(memory_space=pltpu.SMEM)
    words = pl.pallas_call(
        kernel,
        out_shape=jax.ShapeDtypeStruct((12, 2, 48, 128), I32),
        in_specs=[ANY, ANY, smem, smem, smem, ANY, VMEM, VMEM],
        out_specs=VMEM,
        scratch_shapes=scratch,
        compiler_params=pltpu.CompilerParams(
            vmem_limit_bytes=VLIM, has_side_effects=True, collective_id=0
        ),
        name="step",
    )(images, vol, orient, prior_shift, noise_var, tab, small, cols)
    return pl.pallas_call(
        open_kernel,
        out_shape=jax.ShapeDtypeStruct((12, 48, L), F32),
        in_specs=[VMEM],
        out_specs=VMEM,
        name="open",
    )(words)


def solution(mesh):
    return jax.shard_map(
        per_device,
        mesh=mesh,
        in_specs=(
            P("img", None, None, None),
            P(None, "slab", "img", None),
            P("img"),
            P("img"),
            P("img"),
        ),
        out_specs=P("img", "slab", None),
        check_vma=False,
    )
```

```python
import math

import jax
import jax.numpy as jnp
import numpy as np
from jax import lax
from jax.experimental import pallas as pl
from jax.experimental.pallas import tpu as pltpu
from jax.sharding import PartitionSpec as P

GRID = 16
PRIOR = 8
NORIENT = 4096
L = 384
HALF = L // 2
SCALE = L ** (-1.5)
PRECISE = lax.Precision.HIGHEST
F32 = jnp.float32
BF16 = jnp.bfloat16
I32 = jnp.int32
VLIM = 62 * 1024 * 1024

NT = (((1,), (1,)), ((), ()))
NN = (((1,), (0,)), ((), ()))


def wave(product):
    angle = 2.0 * math.pi * np.mod(product, L) / L
    return np.cos(angle).astype(np.float32), np.sin(angle).astype(np.float32)


def thirds(a):
    high = a.astype(BF16)
    rest = a - high.astype(np.float32)
    middle = rest.astype(BF16)
    return high, middle, (rest - middle.astype(np.float32)).astype(BF16)


def make_tables():
    ids = np.arange(L)
    ct, st = wave(ids[:, None] * (ids[None, :] - HALF))
    shift = np.arange(PRIOR) - PRIOR // 2 - GRID // 2
    turns = wave(shift[:, None] * (ids[None, :] - HALF))
    small = thirds(np.concatenate([ct[:GRID], st[:GRID], turns[0], turns[1]], axis=0))
    cols = np.concatenate(
        [
            np.concatenate([ct[:GRID], st[:GRID]], axis=1),
            np.concatenate([-st[:GRID], ct[:GRID]], axis=1),
        ],
        axis=0,
    )
    high, middle, low = thirds(cols)
    cols = np.concatenate([high, middle, high, middle, low, high], axis=0)
    tiles = lambda a: np.ascontiguousarray(a.reshape(L, 3, 128).transpose(1, 0, 2))
    return np.stack([tiles(ct), tiles(st)]), np.stack(small), cols


def remote(src, dst, send, recv, img, slab):
    return pltpu.make_async_remote_copy(
        src_ref=src,
        dst_ref=dst,
        send_sem=send,
        recv_sem=recv,
        device_id={"img": img, "slab": slab},
        device_id_type=pl.DeviceIdType.MESH,
    )


def drain(ref, sem):
    pltpu.make_async_copy(ref, ref, sem).wait()


def dot(a, b, dims=NN):
    return lax.dot_general(a, b, dims, preferred_element_type=F32)


def dot_full(a, b, dims=NN):
    return lax.dot_general(a, b, dims, precision=PRECISE, preferred_element_type=F32)


def halves(a):
    high = a.astype(BF16)
    return high, (a - high.astype(F32)).astype(BF16)


def dot_split(ah, al, bh, bl, dims):
    return dot(ah, bh, dims) + (dot(ah, bl, dims) + dot(al, bh, dims))


def iota(shape, axis):
    return lax.broadcasted_iota(I32, shape, axis)


def count(index, step, top):
    total = jnp.zeros_like(index)
    for edge in range(step, top, step):
        total += (index >= edge).astype(I32)
    return total


def plane_ids(index, zh):
    return index + 48 * count(index, 48, 192) + 48 * zh


def planes_of(orient, row):
    return (((row - HALF) * (orient - NORIENT // 2)) >> 11) + HALF


def power(n):
    total = jnp.ones(n.shape, F32)
    for bit in range(7):
        total *= jnp.where((n >> bit) & 1 == 1, 2.0 ** (2**bit), 1.0)
    return total


def pack(tiles):
    peak = jnp.maximum(jnp.maximum(jnp.abs(tiles[0]), jnp.abs(tiles[1])), jnp.abs(tiles[2]))
    peak = jnp.maximum(jnp.max(peak, axis=1, keepdims=True), 1e-30)
    level = jnp.ceil(jnp.log(peak) * (1.0 / math.log(2.0)) + 0.01)
    level = jnp.clip(level, -100.0, 20.0).astype(I32) + 101
    gain = power(121 - level)
    q0, q1, q2 = (jnp.floor(tile * gain + 0.5).astype(I32) for tile in tiles)
    flag = (level >> (iota(tiles[0].shape, 1) & 31)) & 1
    return (q0 << 11) | ((q2 >> 10) & 2047), (q1 << 11) | ((q2 & 1023) << 1) | flag


def unpack(one, two):
    lane = iota(one.shape, 1)
    flag = jnp.where(lane < 8, (two & 1) << (lane & 7), 0).astype(F32)
    level = jnp.sum(flag, axis=1, keepdims=True).astype(I32)
    gain = power(level) * 2.0**-121
    third = ((one & 2047) << 10) | ((two >> 1) & 1023)
    return [v.astype(F32) * gain for v in (one >> 11, two >> 11, (third << 11) >> 11)]


def whole(tab, part):
    return jnp.concatenate([tab[part, n] for n in range(3)], axis=1)


def kernel(
    img_in, vol_in, orient_in, prior_in, noise_in, tab_in, small, cols,
    out,
    meta, pics, vol, tab, strip, strips, a, volb, voll, xd, vbd, vld, md, tt, wt,
    exh, exl, ezh, ezl, eyh, eyl, rt, puts, shares, sc, parts, sums, w, mh, ml, lines, g, r, d, other, total,
    load, spread_send, spread_recv, own, post_send, post_recv,
    plane_send, plane_recv, swap_send, swap_recv, out_send, out_recv,
):
    img = lax.axis_index("img")
    slab = lax.axis_index("slab")
    zl, x, zh = img // 8, slab // 2, slab % 2
    q, core, yc = img // 2, img % 2, img % 8
    z = zh * 4 + zl
    me = q * 8 + slab

    loads = [
        pltpu.make_async_copy(src, dst, load.at[n])
        for n, (src, dst) in enumerate(((vol_in, vol), (img_in, pics), (tab_in, tab)))
    ]
    for copy in loads:
        copy.start()

    barrier = pltpu.get_barrier_semaphore()
    for turn in (2, 6, 1, 7, 0):
        to_z = (z + turn) % 8

        def greet(k, carry, to_z=to_z):
            pl.semaphore_signal(
                barrier,
                inc=1,
                device_id={"img": to_z % 4 * 8 + (yc + k) % 8, "slab": 2 * x + to_z // 4},
                device_id_type=pl.DeviceIdType.MESH,
            )
            return carry

        lax.fori_loop(1 if turn == 0 else 0, 8, greet, 0)
    for k in range(1, 4):
        pl.semaphore_signal(
            barrier,
            inc=1,
            device_id={"img": img, "slab": 2 * ((x + k) % 4) + zh},
            device_id_type=pl.DeviceIdType.MESH,
        )

    entry, item = iota((8, 128), 0), iota((8, 128), 1)
    facts = jnp.zeros((8, 128), F32)
    for n in range(8):
        for m, ref in enumerate((orient_in, prior_in, noise_in)):
            here = jnp.logical_and(entry == n, item == m)
            facts = jnp.where(here, ref[n].astype(F32), facts)
    meta[...] = facts

    loads[0].wait()
    for c in range(2):

        def cast(j, carry, c=c):
            volb[c, j], voll[c, j] = halves(vol[c, j])
            return carry

        lax.fori_loop(0, 12, cast, 0)
    loads[1].wait()

    def widen(n, carry):
        for c in range(2):
            for t in range(3):
                strip[n, c, t] = pics[n, c, :, 128 * t : 128 * t + 128].astype(F32)
        return carry

    lax.fori_loop(0, 8, widen, 0)

    def sort_images(j, carry):
        def gather(n, inner):
            for c in range(2):
                for t in range(3):
                    strips[c, t, pl.ds(n, 32, stride=8), :] = strip[
                        n, c, t, pl.ds(3 * x + j, 32, stride=12), :
                    ]
            return inner

        lax.fori_loop(0, 8, gather, 0)
        for c in range(2):
            rows = jnp.concatenate([strips[c, t] for t in range(3)], axis=1)
            a[j, :, c] = rows.reshape(32, 8, L).astype(BF16)
        return carry

    sort_images(0, 0)
    pl.semaphore_wait(barrier, 42)

    def send_map(src, dst, n):
        for k in range(1, 4):
            to = (x + k) % 4
            remote(
                src.at[:, pl.ds(3 * to, 3)], dst.at[x],
                spread_send.at[n], spread_recv.at[n], img, 2 * to + zh,
            ).start()

    def send_images(j, carry):
        for turn in (2, 6, 1, 7, 0):
            to_z = (z + turn) % 8

            def spread(k, inner, turn=turn, to_z=to_z):
                to = (to_z % 4) * 8 + (yc + k) % 8
                to_slab = 2 * x + to_z // 4
                if turn in (2, 6):
                    c = 0 if turn == 2 else 1
                    src, dst = a.at[j, to, c], xd.at[j, img, c]
                else:
                    src, dst = a.at[j, to], xd.at[j, img]
                remote(src, dst, spread_send.at[j], spread_recv.at[j], to, to_slab).start()
                return inner

            lax.fori_loop(1 if turn == 0 else 0, 8, spread, 0)
        pltpu.make_async_copy(a.at[j, img], xd.at[j, img], own.at[j]).start()
        return carry

    send_map(volb, vbd, 3)
    for turn in (2, 1, 7, 0):
        to_z = (z + turn) % 8

        def send_meta(k, carry, to_z=to_z):
            to = (to_z % 4) * 8 + (yc + k) % 8
            remote(
                meta, md.at[img], spread_send.at[5], spread_recv.at[5], to, 2 * x + to_z // 4
            ).start()
            return carry

        lax.fori_loop(1 if turn == 0 else 0, 8, send_meta, 0)
    send_images(0, 0)

    def next_images(j, carry):
        return send_images(j, sort_images(j, carry))

    lax.fori_loop(1, 3, next_images, 0)
    mine = [
        pltpu.make_async_copy(src, dst, own.at[3 + n])
        for n, (src, dst) in enumerate(
            (
                (volb.at[:, pl.ds(3 * x, 3)], vbd.at[x]),
                (voll.at[:, pl.ds(3 * x, 3)], vld.at[x]),
                (meta, md.at[img]),
            )
        )
    ]
    for copy in mine:
        copy.start()

    loads[2].wait()
    cell = iota((256, 3 * GRID), 0)
    step = iota((256, 3 * GRID), 1) & 15
    in_b = jnp.where((cell & 15) == step, 1.0, 0.0).astype(BF16)
    in_a = jnp.where((cell >> 4) == step, 1.0, 0.0).astype(BF16)

    def parts_of(first, size):
        return jnp.concatenate([small[n, first : first + size] for n in range(3)], axis=0)

    def stacked(a):
        high, middle = halves(a)
        low = (a - high.astype(F32) - middle.astype(F32)).astype(BF16)
        return jnp.concatenate([high, middle, low], axis=0)

    col_c, col_s = dot(in_b, parts_of(0, GRID)), dot(in_b, parts_of(GRID, GRID))
    row_ids = iota((L, 128), 0)
    at_rows = jnp.where(row_ids == 12 * img + 3 * x + iota((L, 128), 1), 1.0, 0.0).astype(BF16)
    here = dot(small[0], at_rows) + dot(small[1], at_rows) + dot(small[2], at_rows)
    row_c = dot(in_a, stacked(here[:GRID]))
    row_s = dot(in_a, stacked(here[GRID : 2 * GRID]))
    for j in range(3):
        rc, rs = row_c[:, j : j + 1], row_s[:, j : j + 1]
        wt[j, :, :L] = col_c * rc - col_s * rs
        wt[j, :, L:] = col_s * rc + col_c * rs

    drain(md.at[pl.ds(0, 31)], spread_recv.at[5])
    mine[2].wait()
    values = md[...].reshape(256, 128)
    orient = values[:, 0:1].astype(I32)
    prior = values[:, 1:2].astype(I32)
    values_t = values.T
    orient_row = values_t[0:1, :].astype(I32)
    ids = iota((256, 3 * PRIOR), 1) & 7
    in_cols = jnp.where((prior & 7) == ids, 1.0, 0.0).astype(BF16)
    in_rows = jnp.where((prior >> 3) == ids, 1.0, 0.0).astype(BF16)
    turn_c, turn_s = (dot(in_cols, parts_of(2 * GRID + PRIOR * n, PRIOR)) for n in range(2))
    row_turn_c, row_turn_s = (
        dot(in_rows, stacked(here[2 * GRID + PRIOR * n : 2 * GRID + PRIOR * n + PRIOR]))
        for n in range(2)
    )
    for j in range(3):
        rc, rs = row_turn_c[:, j : j + 1], row_turn_s[:, j : j + 1]
        tt[j, 0] = turn_c * rc - turn_s * rs
        tt[j, 1] = turn_c * rs + turn_s * rc

    drain(vbd.at[pl.ds(0, 3)], spread_recv.at[3])
    mine[0].wait()
    send_map(voll, vld, 4)
    first = 12 * img + 3 * x
    zid_row = plane_ids(iota((1, 192), 1), zh)
    zid_col = plane_ids(iota((192, 1), 0), zh)

    def picture(j, c):
        return xd[j, :, c].astype(F32).reshape(256, L)

    sc[...] = jnp.zeros_like(sc)

    def score(j, carry):
        drain(xd.at[j, pl.ds(0, 31)], spread_recv.at[j])
        pltpu.make_async_copy(xd.at[j, 0], xd.at[j, 0], own.at[j]).wait()
        pick = jnp.where(planes_of(orient, first + j) == zid_row, 1.0, 0.0).astype(BF16)
        sr, si = (
            dot(pick, jnp.concatenate([vbd[b, c, j] for b in range(4)], axis=0))
            for c in range(2)
        )
        xr, xi = picture(j, 0), picture(j, 1)
        tr, ti = tt[j, 0], tt[j, 1]
        rr, ii, ri, ir = xr * tr, xi * ti, xr * ti, xi * tr
        tr, ti = rr - ii, ri + ir
        tt[j, 0] = rr + ii
        tt[j, 1] = ir - ri
        lhs = jnp.concatenate([sr * tr + si * ti, si * tr - sr * ti], axis=1)
        sc[...] += dot_full(lhs, wt[j], NT).reshape(32, 8, 256)
        return carry

    lax.fori_loop(0, 3, score, 0)

    layer = yc * 4 + x

    def send_parts(k, carry):
        to = (layer + k) % 32
        remote(
            sc.at[to], parts.at[layer], post_send.at[0], post_recv.at[0],
            zl * 8 + to // 4, 2 * (to % 4) + zh,
        ).start()
        return carry

    lax.fori_loop(1, 32, send_parts, 0)
    parts[layer] = sc[layer]

    lane = iota((256, 192), 1)
    same = ((iota((256, 192), 0) ^ lane) & 15) == 0
    for j in range(3):
        wave_of = jnp.where((lane & 16) == 0, row_c[:, j : j + 1], row_s[:, j : j + 1])
        rt[j] = jnp.where(same, wave_of, 0.0)
    for k in range(3):
        cx, sx = (
            jnp.concatenate([tab[p, t, pl.ds(k, 128, stride=3), :] for t in range(3)], axis=1)
            for p in range(2)
        )
        for n, (left, right) in enumerate(((cx, -sx), (sx, cx))):
            for side, value in enumerate((left, right)):
                high, low = halves(value)
                exh[k, 128 * n : 128 * n + 128, L * side : L * side + L] = high
                exl[k, 128 * n : 128 * n + 128, L * side : L * side + L] = low

    for j in range(3):
        hit = jnp.where(planes_of(orient_row, first + j) == zid_col, 1.0, 0.0).astype(F32)
        puts[j] = hit.astype(BF16)
        share = 1.0 / (jnp.sum(hit, axis=1, keepdims=True) + 1.0)
        shares[j] = jnp.broadcast_to(share, (192, L))

    drain(parts.at[pl.ds(0, 31)], post_recv.at[0])
    sums[z] = jnp.sum(parts[...], axis=0)

    def send_sums(k, carry):
        to = (z + k) % 8
        remote(
            sums.at[z], sums.at[z], post_send.at[1], post_recv.at[1],
            to % 4 * 8 + yc, 2 * x + to // 4,
        ).start()
        return carry

    lax.fori_loop(1, 8, send_sums, 0)
    ct, st = whole(tab, 0), whole(tab, 1)
    lane = iota((L, 2 * L), 1)
    spot = lane % L
    is_re = jnp.logical_or(spot < 128, jnp.logical_and(spot >= 128, spot < 192))
    local = jnp.where(spot < 192, spot, jnp.where(spot < 256, spot - 64, spot - 256))
    kz = local + 48 * count(local, 48, 192) + 48 * (lane >= L).astype(I32)
    pick_z = jnp.where(iota((L, 2 * L), 0) == kz, 1.0, 0.0).astype(BF16)
    cth, ctl = halves(ct)
    sth, stl = halves(st)
    re_z = is_re[:1]
    for dst, c_part, s_part in ((ezh, cth, sth), (ezl, ctl, stl)):
        cz, sz = dot(c_part, pick_z), dot(s_part, pick_z)
        dst[:L] = jnp.where(re_z, cz, -sz).astype(BF16)
        dst[L:] = jnp.where(re_z, sz, cz).astype(BF16)
    drain(sums.at[pl.ds(0, 7)], post_recv.at[1])
    logits = jnp.sum(sums[...], axis=0) / (2.0 * md[layer][:, 2:3])
    expo = jnp.exp(logits - jnp.max(logits, axis=1, keepdims=True))
    w[layer] = expo / jnp.sum(expo, axis=1, keepdims=True)

    def send_weights(k, carry):
        to = (layer + k) % 32
        remote(
            w.at[layer], w.at[layer], post_send.at[2], post_recv.at[2],
            zl * 8 + to // 4, 2 * (to % 4) + zh,
        ).start()
        return carry

    lax.fori_loop(1, 32, send_weights, 0)
    lane = iota((L, L), 1)
    local = jnp.where(lane < 192, lane, lane - 192)
    ky = local + 12 * count(local, 12, 192) + 12 * core
    pick_y = jnp.where(iota((L, L), 0) == ky, 1.0, 0.0).astype(BF16)
    re_y = (lane < 192)[:1]
    for dst, c_part, s_part in ((eyh, cth, sth), (eyl, ctl, stl)):
        dst[...] = jnp.where(re_y, dot(c_part, pick_y), -dot(s_part, pick_y)).astype(BF16)
    drain(vld.at[pl.ds(0, 3)], spread_recv.at[4])
    mine[1].wait()
    drain(w.at[pl.ds(0, 31)], post_recv.at[2])

    def merge(j, carry):
        rows = dot_full(w[...].reshape(256, 256), rt[j])
        high, middle = halves(rows)
        low = (rows - high.astype(F32) - middle.astype(F32)).astype(BF16)
        group = iota((256, 192), 1) >> 5
        use_middle = jnp.logical_or(group == 2, group == 3)
        rows = jnp.where(use_middle, middle.astype(F32), high.astype(F32))
        rows = jnp.where(group == 5, low.astype(F32), rows).astype(BF16)
        f = dot(rows, cols[...])
        fr, fi = f[:, :L], f[:, L:]
        xr, xi = tt[j, 0], tt[j, 1]
        for c, part in enumerate((xr * fr + xi * fi, xi * fr - xr * fi)):
            back = dot(puts[j], part.astype(BF16))
            rows = jnp.concatenate(
                [vbd[b, c, j].astype(F32) + vld[b, c, j].astype(F32) for b in range(4)], axis=0
            )
            high, low = halves((back + rows) * shares[j])
            mh[j, :, L * c : L * c + L] = high
            ml[j, :, L * c : L * c + L] = low
        return carry

    lax.fori_loop(0, 3, merge, 0)

    for k in range(3):

        def x_lines(j, carry, k=k):
            gx = dot_split(exh[k], exl[k], mh[j], ml[j], NT)
            re, im = gx[:128], gx[128:]
            tiles = (
                re[:, :128],
                jnp.concatenate([re[:, 128:], im[:, 128:]], axis=1),
                im[:, :128],
            )
            for t in range(3):
                lines[t, pl.ds(j, 128, stride=3), :] = tiles[t]
            return carry

        lax.fori_loop(0, 3, x_lines, 0)
        g[k, 0], g[k, 1] = pack([lines[t] for t in range(3)])
        land = r.at[k, pl.ds(2 * zh, 2), pl.ds(3 * (4 * q + x), 3)]

        def send_lines(n, carry, k=k, land=land):
            to = (me + n) % 128
            remote(
                g.at[k, :, pl.ds(3 * to, 3)], land,
                plane_send.at[k], plane_recv.at[k], 2 * (to // 8) + core, to % 8,
            ).start()
            return carry

        lax.fori_loop(1, 128, send_lines, 0)
        pltpu.make_async_copy(g.at[k, :, pl.ds(3 * me, 3)], land, own.at[6 + k]).start()

    to = 2 * q + slab // 4

    def deliver(k):
        place = out.at[3 * (slab % 4) + k]
        for n in range(4):
            here = jnp.logical_and(to == img, 4 * core + n == slab)

            @pl.when(here)
            def _(n=n):
                pltpu.make_async_copy(total.at[k, n], place, out_recv).start()

            @pl.when(jnp.logical_not(here))
            def _(n=n):
                remote(
                    total.at[k, n], place, out_send.at[n], out_recv, to, 4 * core + n
                ).start()

    for k in range(3):
        pltpu.make_async_copy(
            g.at[k, :, pl.ds(0, 3)], g.at[k, :, pl.ds(0, 3)], own.at[6 + k]
        ).wait()
        drain(g.at[k, :, pl.ds(0, 381)], plane_recv.at[k])
        if k == 2:
            deliver(0)
            deliver(1)
        columns = unpack(r[k, 0], r[k, 1]) + unpack(r[k, 2], r[k, 3])
        th, tl = halves(jnp.concatenate(columns, axis=1))
        u = dot_split(th, tl, ezh[...], ezl[...], NT)
        uh, ul = halves(jnp.concatenate([u[:, :L], u[:, L:]], axis=0))
        theirs, ours = pl.ds(192 * (1 - core), 192), pl.ds(192 * core, 192)
        d[k] = dot_split(eyh[theirs], eyl[theirs], uh, ul, NN).reshape(4, 48, L)
        swap = remote(
            d.at[k], other.at[k], swap_send.at[k], swap_recv.at[k], 2 * q + 1 - core, slab
        )
        swap.start()
        done = dot_split(eyh[ours], eyl[ours], uh, ul, NN)
        swap.wait()
        done = (done + other[k].reshape(192, L)) * SCALE
        words = pack([done[:, :128], done[:, 128:256], done[:, 256:]])
        for n in range(2):
            total[k, :, n] = words[n].reshape(4, 48, 128)
        if k == 2:
            deliver(2)

    for j in range(3):
        drain(a.at[j, pl.ds(0, 31)], spread_send.at[j])
    drain(vbd.at[pl.ds(0, 3)], spread_send.at[3])
    drain(vld.at[pl.ds(0, 3)], spread_send.at[4])
    drain(md.at[pl.ds(0, 31)], spread_send.at[5])
    drain(parts.at[pl.ds(0, 31)], post_send.at[0])
    drain(sums.at[pl.ds(0, 7)], post_send.at[1])
    drain(w.at[pl.ds(0, 31)], post_send.at[2])
    for k in range(3):
        drain(g.at[k, :, pl.ds(0, 381)], plane_send.at[k])
    for n in range(4):
        here = jnp.logical_and(to == img, 4 * core + n == slab)

        @pl.when(jnp.logical_not(here))
        def _(n=n):
            drain(total.at[:, n], out_send.at[n])

    drain(out, out_recv)


def open_kernel(words, out):
    for n in range(4):
        one, two = (words[3 * n : 3 * n + 3, m].reshape(144, 128) for m in range(2))
        value = jnp.concatenate(unpack(one, two), axis=1)
        out[3 * n : 3 * n + 3] = value.reshape(3, 48, L)


ANY = pl.BlockSpec(memory_space=pl.ANY)
VMEM = pl.BlockSpec(memory_space=pltpu.VMEM)
DMA = pltpu.SemaphoreType.DMA


def per_device(images, volume, orient, prior_shift, noise_var):
    tab, small, cols = make_tables()
    vol = jnp.transpose(volume, (0, 2, 1, 3))
    buf = pltpu.VMEM
    scratch = [
        buf((8, 128), F32),
        buf((8, 2, L, L), BF16),
        buf((2, 12, 48, L), F32),
        buf((2, 3, L, 128), F32),
        buf((8, 2, 3, L, 128), F32),
        buf((2, 3, 256, 128), F32),
        buf((3, 32, 2, 8, L), BF16),
        buf((2, 12, 48, L), BF16),
        buf((2, 12, 48, L), BF16),
        buf((3, 32, 2, 8, L), BF16),
        buf((4, 2, 3, 48, L), BF16),
        buf((4, 2, 3, 48, L), BF16),
        buf((32, 8, 128), F32),
        buf((3, 2, 256, L), F32),
        buf((3, 256, 2 * L), F32),
        buf((3, 256, 2 * L), BF16),
        buf((3, 256, 2 * L), BF16),
        buf((2 * L, 2 * L), BF16),
        buf((2 * L, 2 * L), BF16),
        buf((L, L), BF16),
        buf((L, L), BF16),
        buf((3, 256, 192), F32),
        buf((3, 192, 256), BF16),
        buf((3, 192, L), F32),
        buf((32, 8, 256), F32),
        buf((32, 8, 256), F32),
        buf((8, 8, 256), F32),
        buf((32, 8, 256), F32),
        buf((3, 192, 2 * L), BF16),
        buf((3, 192, 2 * L), BF16),
        buf((3, L, 128), F32),
        buf((3, 2, L, 128), I32),
        buf((3, 4, 192, 128), I32),
        buf((3, 4, 48, L), F32),
        buf((3, 4, 48, L), F32),
        buf((3, 4, 2, 48, 128), I32),
        DMA((3,)),
        DMA((6,)),
        DMA((6,)),
        DMA((9,)),
        DMA((3,)),
        DMA((3,)),
        DMA((3,)),
        DMA((3,)),
        DMA((3,)),
        DMA((3,)),
        DMA((4,)),
        DMA(()),
    ]
    smem = pl.BlockSpec(memory_space=pltpu.SMEM)
    words = pl.pallas_call(
        kernel,
        out_shape=jax.ShapeDtypeStruct((12, 2, 48, 128), I32),
        in_specs=[ANY, ANY, smem, smem, smem, ANY, VMEM, VMEM],
        out_specs=VMEM,
        scratch_shapes=scratch,
        compiler_params=pltpu.CompilerParams(
            vmem_limit_bytes=VLIM, has_side_effects=True, collective_id=0
        ),
        name="step",
    )(images, vol, orient, prior_shift, noise_var, tab, small, cols)
    return pl.pallas_call(
        open_kernel,
        out_shape=jax.ShapeDtypeStruct((12, 48, L), F32),
        in_specs=[VMEM],
        out_specs=VMEM,
        name="open",
    )(words)


def solution(mesh):
    return jax.shard_map(
        per_device,
        mesh=mesh,
        in_specs=(
            P("img", None, None, None),
            P(None, "slab", "img", None),
            P("img"),
            P("img"),
            P("img"),
        ),
        out_specs=P("img", "slab", None),
        check_vma=False,
    )
```

```python
import math

import jax
import jax.numpy as jnp
import numpy as np
from jax import lax
from jax.experimental import pallas as pl
from jax.experimental.pallas import tpu as pltpu
from jax.sharding import PartitionSpec as P

GRID = 16
PRIOR = 8
NORIENT = 4096
L = 384
HALF = L // 2
SCALE = L ** (-1.5)
PRECISE = lax.Precision.HIGHEST
F32 = jnp.float32
BF16 = jnp.bfloat16
I32 = jnp.int32
VLIM = 62 * 1024 * 1024

NT = (((1,), (1,)), ((), ()))
NN = (((1,), (0,)), ((), ()))


def wave(product):
    angle = 2.0 * math.pi * np.mod(product, L) / L
    return np.cos(angle).astype(np.float32), np.sin(angle).astype(np.float32)


def thirds(a):
    high = a.astype(BF16)
    rest = a - high.astype(np.float32)
    middle = rest.astype(BF16)
    return high, middle, (rest - middle.astype(np.float32)).astype(BF16)


def make_tables():
    ids = np.arange(L)
    ct, st = wave(ids[:, None] * (ids[None, :] - HALF))
    shift = np.arange(PRIOR) - PRIOR // 2 - GRID // 2
    turns = wave(shift[:, None] * (ids[None, :] - HALF))
    small = thirds(np.concatenate([ct[:GRID], st[:GRID], turns[0], turns[1]], axis=0))
    cols = np.concatenate(
        [
            np.concatenate([ct[:GRID], st[:GRID]], axis=1),
            np.concatenate([-st[:GRID], ct[:GRID]], axis=1),
        ],
        axis=0,
    )
    high, middle, low = thirds(cols)
    cols = np.concatenate([high, middle, high, middle, low, high], axis=0)
    tiles = lambda a: np.ascontiguousarray(a.reshape(L, 3, 128).transpose(1, 0, 2))
    return np.stack([tiles(ct), tiles(st)]), np.stack(small), cols


def remote(src, dst, send, recv, img, slab):
    return pltpu.make_async_remote_copy(
        src_ref=src,
        dst_ref=dst,
        send_sem=send,
        recv_sem=recv,
        device_id={"img": img, "slab": slab},
        device_id_type=pl.DeviceIdType.MESH,
    )


def drain(ref, sem):
    pltpu.make_async_copy(ref, ref, sem).wait()


def dot(a, b, dims=NN):
    return lax.dot_general(a, b, dims, preferred_element_type=F32)


def dot_full(a, b, dims=NN):
    return lax.dot_general(a, b, dims, precision=PRECISE, preferred_element_type=F32)


def halves(a):
    high = a.astype(BF16)
    return high, (a - high.astype(F32)).astype(BF16)


def dot_split(ah, al, bh, bl, dims):
    return dot(ah, bh, dims) + (dot(ah, bl, dims) + dot(al, bh, dims))


def iota(shape, axis):
    return lax.broadcasted_iota(I32, shape, axis)


def count(index, step, top):
    total = jnp.zeros_like(index)
    for edge in range(step, top, step):
        total += (index >= edge).astype(I32)
    return total


def plane_ids(index, zh):
    return index + 48 * count(index, 48, 192) + 48 * zh


def planes_of(orient, row):
    return (((row - HALF) * (orient - NORIENT // 2)) >> 11) + HALF


def power(n):
    total = jnp.ones(n.shape, F32)
    for bit in range(7):
        total *= jnp.where((n >> bit) & 1 == 1, 2.0 ** (2**bit), 1.0)
    return total


def pack(tiles):
    peak = jnp.maximum(jnp.maximum(jnp.abs(tiles[0]), jnp.abs(tiles[1])), jnp.abs(tiles[2]))
    peak = jnp.maximum(jnp.max(peak, axis=1, keepdims=True), 1e-30)
    level = jnp.ceil(jnp.log(peak) * (1.0 / math.log(2.0)) + 0.01)
    level = jnp.clip(level, -100.0, 20.0).astype(I32) + 101
    gain = power(121 - level)
    q0, q1, q2 = (jnp.floor(tile * gain + 0.5).astype(I32) for tile in tiles)
    flag = (level >> (iota(tiles[0].shape, 1) & 31)) & 1
    return (q0 << 11) | ((q2 >> 10) & 2047), (q1 << 11) | ((q2 & 1023) << 1) | flag


def unpack(one, two):
    lane = iota(one.shape, 1)
    flag = jnp.where(lane < 8, (two & 1) << (lane & 7), 0).astype(F32)
    level = jnp.sum(flag, axis=1, keepdims=True).astype(I32)
    gain = power(level) * 2.0**-121
    third = ((one & 2047) << 10) | ((two >> 1) & 1023)
    return [v.astype(F32) * gain for v in (one >> 11, two >> 11, (third << 11) >> 11)]


def whole(tab, part):
    return jnp.concatenate([tab[part, n] for n in range(3)], axis=1)


def kernel(
    img_in, vol_in, orient_in, prior_in, noise_in, tab_in, small, cols,
    out,
    meta, pics, vol, tab, strip, strips, a, volb, voll, xd, vbd, vld, md, tt, wt,
    exh, exl, ezh, ezl, eyh, eyl, rt, puts, shares, sc, parts, sums, w, mh, ml, lines, g, r, d, other, total,
    load, spread_send, spread_recv, own, post_send, post_recv,
    plane_send, plane_recv, swap_send, swap_recv, out_send, out_recv,
):
    img = lax.axis_index("img")
    slab = lax.axis_index("slab")
    zl, x, zh = img // 8, slab // 2, slab % 2
    q, core, yc = img // 2, img % 2, img % 8
    z = zh * 4 + zl
    me = q * 8 + slab

    loads = [
        pltpu.make_async_copy(src, dst, load.at[n])
        for n, (src, dst) in enumerate(((vol_in, vol), (img_in, pics), (tab_in, tab)))
    ]
    for copy in loads:
        copy.start()

    barrier = pltpu.get_barrier_semaphore()
    for turn in (2, 6, 1, 7, 0):
        to_z = (z + turn) % 8

        def greet(k, carry, to_z=to_z):
            pl.semaphore_signal(
                barrier,
                inc=1,
                device_id={"img": to_z % 4 * 8 + (yc + k) % 8, "slab": 2 * x + to_z // 4},
                device_id_type=pl.DeviceIdType.MESH,
            )
            return carry

        lax.fori_loop(1 if turn == 0 else 0, 8, greet, 0)
    for k in range(1, 4):
        pl.semaphore_signal(
            barrier,
            inc=1,
            device_id={"img": img, "slab": 2 * ((x + k) % 4) + zh},
            device_id_type=pl.DeviceIdType.MESH,
        )

    entry, item = iota((8, 128), 0), iota((8, 128), 1)
    facts = jnp.zeros((8, 128), F32)
    for n in range(8):
        for m, ref in enumerate((orient_in, prior_in, noise_in)):
            here = jnp.logical_and(entry == n, item == m)
            facts = jnp.where(here, ref[n].astype(F32), facts)
    meta[...] = facts

    loads[0].wait()
    for c in range(2):

        def cast(j, carry, c=c):
            volb[c, j], voll[c, j] = halves(vol[c, j])
            return carry

        lax.fori_loop(0, 12, cast, 0)
    loads[1].wait()

    def widen(n, carry):
        for c in range(2):
            for t in range(3):
                strip[n, c, t] = pics[n, c, :, 128 * t : 128 * t + 128].astype(F32)
        return carry

    lax.fori_loop(0, 8, widen, 0)

    def sort_images(j, carry):
        def gather(n, inner):
            for c in range(2):
                for t in range(3):
                    strips[c, t, pl.ds(n, 32, stride=8), :] = strip[
                        n, c, t, pl.ds(3 * x + j, 32, stride=12), :
                    ]
            return inner

        lax.fori_loop(0, 8, gather, 0)
        for c in range(2):
            rows = jnp.concatenate([strips[c, t] for t in range(3)], axis=1)
            a[j, :, c] = rows.reshape(32, 8, L).astype(BF16)
        return carry

    sort_images(0, 0)
    pl.semaphore_wait(barrier, 42)

    def send_map(src, dst, n):
        for k in range(1, 4):
            to = (x + k) % 4
            remote(
                src.at[:, pl.ds(3 * to, 3)], dst.at[x],
                spread_send.at[n], spread_recv.at[n], img, 2 * to + zh,
            ).start()

    def send_images(j, carry):
        for turn in (2, 6, 1, 7, 0):
            to_z = (z + turn) % 8

            def spread(k, inner, turn=turn, to_z=to_z):
                to = (to_z % 4) * 8 + (yc + k) % 8
                to_slab = 2 * x + to_z // 4
                if turn in (2, 6):
                    c = 0 if turn == 2 else 1
                    src, dst = a.at[j, to, c], xd.at[j, img, c]
                else:
                    src, dst = a.at[j, to], xd.at[j, img]
                remote(src, dst, spread_send.at[j], spread_recv.at[j], to, to_slab).start()
                return inner

            lax.fori_loop(1 if turn == 0 else 0, 8, spread, 0)
        pltpu.make_async_copy(a.at[j, img], xd.at[j, img], own.at[j]).start()
        return carry

    send_map(volb, vbd, 3)
    for turn in (2, 1, 7, 0):
        to_z = (z + turn) % 8

        def send_meta(k, carry, to_z=to_z):
            to = (to_z % 4) * 8 + (yc + k) % 8
            remote(
                meta, md.at[img], spread_send.at[5], spread_recv.at[5], to, 2 * x + to_z // 4
            ).start()
            return carry

        lax.fori_loop(1 if turn == 0 else 0, 8, send_meta, 0)
    send_images(0, 0)

    def next_images(j, carry):
        return send_images(j, sort_images(j, carry))

    lax.fori_loop(1, 3, next_images, 0)
    mine = [
        pltpu.make_async_copy(src, dst, own.at[3 + n])
        for n, (src, dst) in enumerate(
            (
                (volb.at[:, pl.ds(3 * x, 3)], vbd.at[x]),
                (voll.at[:, pl.ds(3 * x, 3)], vld.at[x]),
                (meta, md.at[img]),
            )
        )
    ]
    for copy in mine:
        copy.start()

    loads[2].wait()
    cell = iota((256, 3 * GRID), 0)
    step = iota((256, 3 * GRID), 1) & 15
    in_b = jnp.where((cell & 15) == step, 1.0, 0.0).astype(BF16)
    in_a = jnp.where((cell >> 4) == step, 1.0, 0.0).astype(BF16)

    def parts_of(first, size):
        return jnp.concatenate([small[n, first : first + size] for n in range(3)], axis=0)

    def stacked(a):
        high, middle = halves(a)
        low = (a - high.astype(F32) - middle.astype(F32)).astype(BF16)
        return jnp.concatenate([high, middle, low], axis=0)

    col_c, col_s = dot(in_b, parts_of(0, GRID)), dot(in_b, parts_of(GRID, GRID))
    row_ids = iota((L, 128), 0)
    at_rows = jnp.where(row_ids == 12 * img + 3 * x + iota((L, 128), 1), 1.0, 0.0).astype(BF16)
    here = dot(small[0], at_rows) + dot(small[1], at_rows) + dot(small[2], at_rows)
    row_c = dot(in_a, stacked(here[:GRID]))
    row_s = dot(in_a, stacked(here[GRID : 2 * GRID]))
    for j in range(3):
        rc, rs = row_c[:, j : j + 1], row_s[:, j : j + 1]
        wt[j, :, :L] = col_c * rc - col_s * rs
        wt[j, :, L:] = col_s * rc + col_c * rs

    drain(md.at[pl.ds(0, 31)], spread_recv.at[5])
    mine[2].wait()
    values = md[...].reshape(256, 128)
    orient = values[:, 0:1].astype(I32)
    prior = values[:, 1:2].astype(I32)
    values_t = values.T
    orient_row = values_t[0:1, :].astype(I32)
    ids = iota((256, 3 * PRIOR), 1) & 7
    in_cols = jnp.where((prior & 7) == ids, 1.0, 0.0).astype(BF16)
    in_rows = jnp.where((prior >> 3) == ids, 1.0, 0.0).astype(BF16)
    turn_c, turn_s = (dot(in_cols, parts_of(2 * GRID + PRIOR * n, PRIOR)) for n in range(2))
    row_turn_c, row_turn_s = (
        dot(in_rows, stacked(here[2 * GRID + PRIOR * n : 2 * GRID + PRIOR * n + PRIOR]))
        for n in range(2)
    )
    for j in range(3):
        rc, rs = row_turn_c[:, j : j + 1], row_turn_s[:, j : j + 1]
        tt[j, 0] = turn_c * rc - turn_s * rs
        tt[j, 1] = turn_c * rs + turn_s * rc

    drain(vbd.at[pl.ds(0, 3)], spread_recv.at[3])
    mine[0].wait()
    send_map(voll, vld, 4)
    first = 12 * img + 3 * x
    zid_row = plane_ids(iota((1, 192), 1), zh)
    zid_col = plane_ids(iota((192, 1), 0), zh)

    def picture(j, c):
        return xd[j, :, c].astype(F32).reshape(256, L)

    sc[...] = jnp.zeros_like(sc)

    def score(j, carry):
        drain(xd.at[j, pl.ds(0, 31)], spread_recv.at[j])
        pltpu.make_async_copy(xd.at[j, 0], xd.at[j, 0], own.at[j]).wait()
        pick = jnp.where(planes_of(orient, first + j) == zid_row, 1.0, 0.0).astype(BF16)
        sr, si = (
            dot(pick, jnp.concatenate([vbd[b, c, j] for b in range(4)], axis=0))
            for c in range(2)
        )
        xr, xi = picture(j, 0), picture(j, 1)
        tr, ti = tt[j, 0], tt[j, 1]
        rr, ii, ri, ir = xr * tr, xi * ti, xr * ti, xi * tr
        tr, ti = rr - ii, ri + ir
        tt[j, 0] = rr + ii
        tt[j, 1] = ir - ri
        lhs = jnp.concatenate([sr * tr + si * ti, si * tr - sr * ti], axis=1)
        sc[...] += dot_full(lhs, wt[j], NT).reshape(32, 8, 256)
        return carry

    lax.fori_loop(0, 3, score, 0)

    layer = yc * 4 + x

    def send_parts(k, carry):
        to = (layer + k) % 32
        remote(
            sc.at[to], parts.at[layer], post_send.at[0], post_recv.at[0],
            zl * 8 + to // 4, 2 * (to % 4) + zh,
        ).start()
        return carry

    lax.fori_loop(1, 32, send_parts, 0)
    parts[layer] = sc[layer]

    lane = iota((256, 192), 1)
    same = ((iota((256, 192), 0) ^ lane) & 15) == 0
    for j in range(3):
        wave_of = jnp.where((lane & 16) == 0, row_c[:, j : j + 1], row_s[:, j : j + 1])
        rt[j] = jnp.where(same, wave_of, 0.0)
    for k in range(3):
        cx, sx = (
            jnp.concatenate([tab[p, t, pl.ds(k, 128, stride=3), :] for t in range(3)], axis=1)
            for p in range(2)
        )
        for n, (left, right) in enumerate(((cx, -sx), (sx, cx))):
            for side, value in enumerate((left, right)):
                high, low = halves(value)
                exh[k, 128 * n : 128 * n + 128, L * side : L * side + L] = high
                exl[k, 128 * n : 128 * n + 128, L * side : L * side + L] = low

    for j in range(3):
        hit = jnp.where(planes_of(orient_row, first + j) == zid_col, 1.0, 0.0).astype(F32)
        puts[j] = hit.astype(BF16)
        share = 1.0 / (jnp.sum(hit, axis=1, keepdims=True) + 1.0)
        shares[j] = jnp.broadcast_to(share, (192, L))

    drain(parts.at[pl.ds(0, 31)], post_recv.at[0])
    sums[z] = jnp.sum(parts[...], axis=0)

    def send_sums(k, carry):
        to = (z + k) % 8
        remote(
            sums.at[z], sums.at[z], post_send.at[1], post_recv.at[1],
            to % 4 * 8 + yc, 2 * x + to // 4,
        ).start()
        return carry

    lax.fori_loop(1, 8, send_sums, 0)
    ct, st = whole(tab, 0), whole(tab, 1)
    lane = iota((L, 2 * L), 1)
    spot = lane % L
    is_re = jnp.logical_or(spot < 128, jnp.logical_and(spot >= 128, spot < 192))
    local = jnp.where(spot < 192, spot, jnp.where(spot < 256, spot - 64, spot - 256))
    kz = local + 48 * count(local, 48, 192) + 48 * (lane >= L).astype(I32)
    pick_z = jnp.where(iota((L, 2 * L), 0) == kz, 1.0, 0.0).astype(BF16)
    cth, ctl = halves(ct)
    sth, stl = halves(st)
    re_z = is_re[:1]
    for dst, c_part, s_part in ((ezh, cth, sth), (ezl, ctl, stl)):
        cz, sz = dot(c_part, pick_z), dot(s_part, pick_z)
        dst[:L] = jnp.where(re_z, cz, -sz).astype(BF16)
        dst[L:] = jnp.where(re_z, sz, cz).astype(BF16)
    drain(sums.at[pl.ds(0, 7)], post_recv.at[1])
    logits = jnp.sum(sums[...], axis=0) / (2.0 * md[layer][:, 2:3])
    expo = jnp.exp(logits - jnp.max(logits, axis=1, keepdims=True))
    w[layer] = expo / jnp.sum(expo, axis=1, keepdims=True)

    def send_weights(k, carry):
        to = (layer + k) % 32
        remote(
            w.at[layer], w.at[layer], post_send.at[2], post_recv.at[2],
            zl * 8 + to // 4, 2 * (to % 4) + zh,
        ).start()
        return carry

    lax.fori_loop(1, 32, send_weights, 0)
    lane = iota((L, L), 1)
    local = jnp.where(lane < 192, lane, lane - 192)
    ky = local + 12 * count(local, 12, 192) + 12 * core
    pick_y = jnp.where(iota((L, L), 0) == ky, 1.0, 0.0).astype(BF16)
    re_y = (lane < 192)[:1]
    for dst, c_part, s_part in ((eyh, cth, sth), (eyl, ctl, stl)):
        dst[...] = jnp.where(re_y, dot(c_part, pick_y), -dot(s_part, pick_y)).astype(BF16)
    drain(vld.at[pl.ds(0, 3)], spread_recv.at[4])
    mine[1].wait()
    drain(w.at[pl.ds(0, 31)], post_recv.at[2])

    def merge(j, carry):
        rows = dot_full(w[...].reshape(256, 256), rt[j])
        high, middle = halves(rows)
        low = (rows - high.astype(F32) - middle.astype(F32)).astype(BF16)
        group = iota((256, 192), 1) >> 5
        use_middle = jnp.logical_or(group == 2, group == 3)
        rows = jnp.where(use_middle, middle.astype(F32), high.astype(F32))
        rows = jnp.where(group == 5, low.astype(F32), rows).astype(BF16)
        f = dot(rows, cols[...])
        fr, fi = f[:, :L], f[:, L:]
        xr, xi = tt[j, 0], tt[j, 1]
        for c, part in enumerate((xr * fr + xi * fi, xi * fr - xr * fi)):
            back = dot(puts[j], part.astype(BF16))
            rows = jnp.concatenate(
                [vbd[b, c, j].astype(F32) + vld[b, c, j].astype(F32) for b in range(4)], axis=0
            )
            high, low = halves((back + rows) * shares[j])
            mh[j, :, L * c : L * c + L] = high
            ml[j, :, L * c : L * c + L] = low
        return carry

    lax.fori_loop(0, 3, merge, 0)

    for k in range(3):

        def x_lines(j, carry, k=k):
            gx = dot_split(exh[k], exl[k], mh[j], ml[j], NT)
            re, im = gx[:128], gx[128:]
            tiles = (
                re[:, :128],
                jnp.concatenate([re[:, 128:], im[:, 128:]], axis=1),
                im[:, :128],
            )
            for t in range(3):
                lines[t, pl.ds(j, 128, stride=3), :] = tiles[t]
            return carry

        lax.fori_loop(0, 3, x_lines, 0)
        g[k, 0], g[k, 1] = pack([lines[t] for t in range(3)])
        land = r.at[k, pl.ds(2 * zh, 2), pl.ds(3 * (4 * q + x), 3)]

        def send_lines(n, carry, k=k, land=land):
            to = (me + n) % 128
            remote(
                g.at[k, :, pl.ds(3 * to, 3)], land,
                plane_send.at[k], plane_recv.at[k], 2 * (to // 8) + core, to % 8,
            ).start()
            return carry

        lax.fori_loop(1, 128, send_lines, 0)
        pltpu.make_async_copy(g.at[k, :, pl.ds(3 * me, 3)], land, own.at[6 + k]).start()

    to = 2 * q + slab // 4

    def deliver(k, across):
        place = out.at[3 * (slab % 4) + k]
        for half in range(2):
            n = 2 * half + (1 - zh if across else zh)
            here = jnp.logical_and(to == img, 4 * core + n == slab)

            @pl.when(here)
            def _(n=n):
                pltpu.make_async_copy(total.at[k, n], place, out_recv).start()

            @pl.when(jnp.logical_not(here))
            def _(n=n):
                remote(
                    total.at[k, n], place, out_send.at[n], out_recv, to, 4 * core + n
                ).start()

    for k in range(3):
        pltpu.make_async_copy(
            g.at[k, :, pl.ds(0, 3)], g.at[k, :, pl.ds(0, 3)], own.at[6 + k]
        ).wait()
        if k == 2:
            drain(g.at[k, :, pl.ds(0, 381)], plane_send.at[k])
            deliver(0, True)
            deliver(1, True)
            deliver(0, False)
            deliver(1, False)
        drain(g.at[k, :, pl.ds(0, 381)], plane_recv.at[k])
        columns = unpack(r[k, 0], r[k, 1]) + unpack(r[k, 2], r[k, 3])
        th, tl = halves(jnp.concatenate(columns, axis=1))
        u = dot_split(th, tl, ezh[...], ezl[...], NT)
        uh, ul = halves(jnp.concatenate([u[:, :L], u[:, L:]], axis=0))
        theirs, ours = pl.ds(192 * (1 - core), 192), pl.ds(192 * core, 192)
        d[k] = dot_split(eyh[theirs], eyl[theirs], uh, ul, NN).reshape(4, 48, L)
        swap = remote(
            d.at[k], other.at[k], swap_send.at[k], swap_recv.at[k], 2 * q + 1 - core, slab
        )
        swap.start()
        done = dot_split(eyh[ours], eyl[ours], uh, ul, NN)
        swap.wait()
        done = (done + other[k].reshape(192, L)) * SCALE
        words = pack([done[:, :128], done[:, 128:256], done[:, 256:]])
        for n in range(2):
            total[k, :, n] = words[n].reshape(4, 48, 128)
        if k == 2:
            deliver(2, True)
            deliver(2, False)

    for j in range(3):
        drain(a.at[j, pl.ds(0, 31)], spread_send.at[j])
    drain(vbd.at[pl.ds(0, 3)], spread_send.at[3])
    drain(vld.at[pl.ds(0, 3)], spread_send.at[4])
    drain(md.at[pl.ds(0, 31)], spread_send.at[5])
    drain(parts.at[pl.ds(0, 31)], post_send.at[0])
    drain(sums.at[pl.ds(0, 7)], post_send.at[1])
    drain(w.at[pl.ds(0, 31)], post_send.at[2])
    for k in range(2):
        drain(g.at[k, :, pl.ds(0, 381)], plane_send.at[k])
    for n in range(4):
        here = jnp.logical_and(to == img, 4 * core + n == slab)

        @pl.when(jnp.logical_not(here))
        def _(n=n):
            drain(total.at[:, n], out_send.at[n])

    drain(out, out_recv)


def open_kernel(words, out):
    for n in range(4):
        one, two = (words[3 * n : 3 * n + 3, m].reshape(144, 128) for m in range(2))
        value = jnp.concatenate(unpack(one, two), axis=1)
        out[3 * n : 3 * n + 3] = value.reshape(3, 48, L)


ANY = pl.BlockSpec(memory_space=pl.ANY)
VMEM = pl.BlockSpec(memory_space=pltpu.VMEM)
DMA = pltpu.SemaphoreType.DMA


def per_device(images, volume, orient, prior_shift, noise_var):
    tab, small, cols = make_tables()
    vol = jnp.transpose(volume, (0, 2, 1, 3))
    buf = pltpu.VMEM
    scratch = [
        buf((8, 128), F32),
        buf((8, 2, L, L), BF16),
        buf((2, 12, 48, L), F32),
        buf((2, 3, L, 128), F32),
        buf((8, 2, 3, L, 128), F32),
        buf((2, 3, 256, 128), F32),
        buf((3, 32, 2, 8, L), BF16),
        buf((2, 12, 48, L), BF16),
        buf((2, 12, 48, L), BF16),
        buf((3, 32, 2, 8, L), BF16),
        buf((4, 2, 3, 48, L), BF16),
        buf((4, 2, 3, 48, L), BF16),
        buf((32, 8, 128), F32),
        buf((3, 2, 256, L), F32),
        buf((3, 256, 2 * L), F32),
        buf((3, 256, 2 * L), BF16),
        buf((3, 256, 2 * L), BF16),
        buf((2 * L, 2 * L), BF16),
        buf((2 * L, 2 * L), BF16),
        buf((L, L), BF16),
        buf((L, L), BF16),
        buf((3, 256, 192), F32),
        buf((3, 192, 256), BF16),
        buf((3, 192, L), F32),
        buf((32, 8, 256), F32),
        buf((32, 8, 256), F32),
        buf((8, 8, 256), F32),
        buf((32, 8, 256), F32),
        buf((3, 192, 2 * L), BF16),
        buf((3, 192, 2 * L), BF16),
        buf((3, L, 128), F32),
        buf((3, 2, L, 128), I32),
        buf((3, 4, 192, 128), I32),
        buf((3, 4, 48, L), F32),
        buf((3, 4, 48, L), F32),
        buf((3, 4, 2, 48, 128), I32),
        DMA((3,)),
        DMA((6,)),
        DMA((6,)),
        DMA((9,)),
        DMA((3,)),
        DMA((3,)),
        DMA((3,)),
        DMA((3,)),
        DMA((3,)),
        DMA((3,)),
        DMA((4,)),
        DMA(()),
    ]
    smem = pl.BlockSpec(memory_space=pltpu.SMEM)
    words = pl.pallas_call(
        kernel,
        out_shape=jax.ShapeDtypeStruct((12, 2, 48, 128), I32),
        in_specs=[ANY, ANY, smem, smem, smem, ANY, VMEM, VMEM],
        out_specs=VMEM,
        scratch_shapes=scratch,
        compiler_params=pltpu.CompilerParams(
            vmem_limit_bytes=VLIM, has_side_effects=True, collective_id=0
        ),
        name="step",
    )(images, vol, orient, prior_shift, noise_var, tab, small, cols)
    return pl.pallas_call(
        open_kernel,
        out_shape=jax.ShapeDtypeStruct((12, 48, L), F32),
        in_specs=[VMEM],
        out_specs=VMEM,
        name="open",
    )(words)


def solution(mesh):
    return jax.shard_map(
        per_device,
        mesh=mesh,
        in_specs=(
            P("img", None, None, None),
            P(None, "slab", "img", None),
            P("img"),
            P("img"),
            P("img"),
        ),
        out_specs=P("img", "slab", None),
        check_vma=False,
    )
```

```python
import math

import jax
import jax.numpy as jnp
import numpy as np
from jax import lax
from jax.experimental import pallas as pl
from jax.experimental.pallas import tpu as pltpu
from jax.sharding import PartitionSpec as P

GRID = 16
PRIOR = 8
NORIENT = 4096
L = 384
HALF = L // 2
SCALE = L ** (-1.5)
PRECISE = lax.Precision.HIGHEST
F32 = jnp.float32
BF16 = jnp.bfloat16
I32 = jnp.int32
VLIM = 62 * 1024 * 1024

NT = (((1,), (1,)), ((), ()))
NN = (((1,), (0,)), ((), ()))


def wave(product):
    angle = 2.0 * math.pi * np.mod(product, L) / L
    return np.cos(angle).astype(np.float32), np.sin(angle).astype(np.float32)


def thirds(a):
    high = a.astype(BF16)
    rest = a - high.astype(np.float32)
    middle = rest.astype(BF16)
    return high, middle, (rest - middle.astype(np.float32)).astype(BF16)


def make_tables():
    ids = np.arange(L)
    ct, st = wave(ids[:, None] * (ids[None, :] - HALF))
    shift = np.arange(PRIOR) - PRIOR // 2 - GRID // 2
    turns = wave(shift[:, None] * (ids[None, :] - HALF))
    small = thirds(np.concatenate([ct[:GRID], st[:GRID], turns[0], turns[1]], axis=0))
    cols = np.concatenate(
        [
            np.concatenate([ct[:GRID], st[:GRID]], axis=1),
            np.concatenate([-st[:GRID], ct[:GRID]], axis=1),
        ],
        axis=0,
    )
    high, middle, low = thirds(cols)
    cols = np.concatenate([high, middle, high, middle, low, high], axis=0)
    tiles = lambda a: np.ascontiguousarray(a.reshape(L, 3, 128).transpose(1, 0, 2))
    return np.stack([tiles(ct), tiles(st)]), np.stack(small), cols


def remote(src, dst, send, recv, img, slab):
    return pltpu.make_async_remote_copy(
        src_ref=src,
        dst_ref=dst,
        send_sem=send,
        recv_sem=recv,
        device_id={"img": img, "slab": slab},
        device_id_type=pl.DeviceIdType.MESH,
    )


def drain(ref, sem):
    pltpu.make_async_copy(ref, ref, sem).wait()


def dot(a, b, dims=NN):
    return lax.dot_general(a, b, dims, preferred_element_type=F32)


def dot_full(a, b, dims=NN):
    return lax.dot_general(a, b, dims, precision=PRECISE, preferred_element_type=F32)


def halves(a):
    high = a.astype(BF16)
    return high, (a - high.astype(F32)).astype(BF16)


def dot_split(ah, al, bh, bl, dims):
    return dot(ah, bh, dims) + (dot(ah, bl, dims) + dot(al, bh, dims))


def iota(shape, axis):
    return lax.broadcasted_iota(I32, shape, axis)


def count(index, step, top):
    total = jnp.zeros_like(index)
    for edge in range(step, top, step):
        total += (index >= edge).astype(I32)
    return total


def plane_ids(index, zh):
    return index + 48 * count(index, 48, 192) + 48 * zh


def planes_of(orient, row):
    return (((row - HALF) * (orient - NORIENT // 2)) >> 11) + HALF


def power(n):
    total = jnp.ones(n.shape, F32)
    for bit in range(7):
        total *= jnp.where((n >> bit) & 1 == 1, 2.0 ** (2**bit), 1.0)
    return total


def pack(tiles):
    peak = jnp.maximum(jnp.maximum(jnp.abs(tiles[0]), jnp.abs(tiles[1])), jnp.abs(tiles[2]))
    peak = jnp.maximum(jnp.max(peak, axis=1, keepdims=True), 1e-30)
    level = jnp.ceil(jnp.log(peak) * (1.0 / math.log(2.0)) + 0.01)
    level = jnp.clip(level, -100.0, 20.0).astype(I32) + 101
    gain = power(121 - level)
    q0, q1, q2 = (jnp.floor(tile * gain + 0.5).astype(I32) for tile in tiles)
    flag = (level >> (iota(tiles[0].shape, 1) & 31)) & 1
    return (q0 << 11) | ((q2 >> 10) & 2047), (q1 << 11) | ((q2 & 1023) << 1) | flag


def unpack(one, two):
    lane = iota(one.shape, 1)
    flag = jnp.where(lane < 8, (two & 1) << (lane & 7), 0).astype(F32)
    level = jnp.sum(flag, axis=1, keepdims=True).astype(I32)
    gain = power(level) * 2.0**-121
    third = ((one & 2047) << 10) | ((two >> 1) & 1023)
    return [v.astype(F32) * gain for v in (one >> 11, two >> 11, (third << 11) >> 11)]


def whole(tab, part):
    return jnp.concatenate([tab[part, n] for n in range(3)], axis=1)


def kernel(
    img_in, vol_in, orient_in, prior_in, noise_in, tab_in, small, cols,
    out,
    meta, pics, vol, tab, strip, strips, a, volb, voll, xd, vbd, vld, md, tt, wt,
    exh, exl, ezh, ezl, eyh, eyl, rt, puts, shares, sc, parts, sums, w, mh, ml, lines, g, r, d, other, total,
    load, spread_send, spread_recv, own, post_send, post_recv,
    plane_send, plane_recv, swap_send, swap_recv, out_send, out_recv,
):
    img = lax.axis_index("img")
    slab = lax.axis_index("slab")
    zl, x, zh = img // 8, slab // 2, slab % 2
    q, core, yc = img // 2, img % 2, img % 8
    z = zh * 4 + zl
    me = q * 8 + slab

    loads = [
        pltpu.make_async_copy(src, dst, load.at[n])
        for n, (src, dst) in enumerate(((vol_in, vol), (img_in, pics), (tab_in, tab)))
    ]
    for copy in loads:
        copy.start()

    barrier = pltpu.get_barrier_semaphore()
    for turn in (2, 6, 1, 7, 0):
        to_z = (z + turn) % 8

        def greet(k, carry, to_z=to_z):
            pl.semaphore_signal(
                barrier,
                inc=1,
                device_id={"img": to_z % 4 * 8 + (yc + k) % 8, "slab": 2 * x + to_z // 4},
                device_id_type=pl.DeviceIdType.MESH,
            )
            return carry

        lax.fori_loop(1 if turn == 0 else 0, 8, greet, 0)
    for k in range(1, 4):
        pl.semaphore_signal(
            barrier,
            inc=1,
            device_id={"img": img, "slab": 2 * ((x + k) % 4) + zh},
            device_id_type=pl.DeviceIdType.MESH,
        )

    entry, item = iota((8, 128), 0), iota((8, 128), 1)
    facts = jnp.zeros((8, 128), F32)
    for n in range(8):
        for m, ref in enumerate((orient_in, prior_in, noise_in)):
            here = jnp.logical_and(entry == n, item == m)
            facts = jnp.where(here, ref[n].astype(F32), facts)
    meta[...] = facts

    loads[0].wait()
    for c in range(2):

        def cast(j, carry, c=c):
            volb[c, j], voll[c, j] = halves(vol[c, j])
            return carry

        lax.fori_loop(0, 12, cast, 0)
    loads[1].wait()

    def widen(n, carry):
        for c in range(2):
            for t in range(3):
                strip[n, c, t] = pics[n, c, :, 128 * t : 128 * t + 128].astype(F32)
        return carry

    lax.fori_loop(0, 8, widen, 0)

    def sort_images(j, carry):
        def gather(n, inner):
            for c in range(2):
                for t in range(3):
                    strips[c, t, pl.ds(n, 32, stride=8), :] = strip[
                        n, c, t, pl.ds(3 * x + j, 32, stride=12), :
                    ]
            return inner

        lax.fori_loop(0, 8, gather, 0)
        for c in range(2):
            rows = jnp.concatenate([strips[c, t] for t in range(3)], axis=1)
            a[j, :, c] = rows.reshape(32, 8, L).astype(BF16)
        return carry

    sort_images(0, 0)
    pl.semaphore_wait(barrier, 42)

    def send_map(src, dst, n):
        for k in range(1, 4):
            to = (x + k) % 4
            remote(
                src.at[:, pl.ds(3 * to, 3)], dst.at[x],
                spread_send.at[n], spread_recv.at[n], img, 2 * to + zh,
            ).start()

    def send_images(j, carry):
        for turn in (2, 6, 1, 7, 0):
            to_z = (z + turn) % 8

            def spread(k, inner, turn=turn, to_z=to_z):
                to = (to_z % 4) * 8 + (yc + k) % 8
                to_slab = 2 * x + to_z // 4
                if turn in (2, 6):
                    c = 0 if turn == 2 else 1
                    src, dst = a.at[j, to, c], xd.at[j, img, c]
                else:
                    src, dst = a.at[j, to], xd.at[j, img]
                remote(src, dst, spread_send.at[j], spread_recv.at[j], to, to_slab).start()
                return inner

            lax.fori_loop(1 if turn == 0 else 0, 8, spread, 0)
        pltpu.make_async_copy(a.at[j, img], xd.at[j, img], own.at[j]).start()
        return carry

    send_map(volb, vbd, 3)
    for turn in (2, 1, 7, 0):
        to_z = (z + turn) % 8

        def send_meta(k, carry, to_z=to_z):
            to = (to_z % 4) * 8 + (yc + k) % 8
            remote(
                meta, md.at[img], spread_send.at[5], spread_recv.at[5], to, 2 * x + to_z // 4
            ).start()
            return carry

        lax.fori_loop(1 if turn == 0 else 0, 8, send_meta, 0)
    send_images(0, 0)

    def next_images(j, carry):
        return send_images(j, sort_images(j, carry))

    lax.fori_loop(1, 3, next_images, 0)
    mine = [
        pltpu.make_async_copy(src, dst, own.at[3 + n])
        for n, (src, dst) in enumerate(
            (
                (volb.at[:, pl.ds(3 * x, 3)], vbd.at[x]),
                (voll.at[:, pl.ds(3 * x, 3)], vld.at[x]),
                (meta, md.at[img]),
            )
        )
    ]
    for copy in mine:
        copy.start()

    loads[2].wait()
    cell = iota((256, 3 * GRID), 0)
    step = iota((256, 3 * GRID), 1) & 15
    in_b = jnp.where((cell & 15) == step, 1.0, 0.0).astype(BF16)
    in_a = jnp.where((cell >> 4) == step, 1.0, 0.0).astype(BF16)

    def parts_of(first, size):
        return jnp.concatenate([small[n, first : first + size] for n in range(3)], axis=0)

    def stacked(a):
        high, middle = halves(a)
        low = (a - high.astype(F32) - middle.astype(F32)).astype(BF16)
        return jnp.concatenate([high, middle, low], axis=0)

    col_c, col_s = dot(in_b, parts_of(0, GRID)), dot(in_b, parts_of(GRID, GRID))
    row_ids = iota((L, 128), 0)
    at_rows = jnp.where(row_ids == 12 * img + 3 * x + iota((L, 128), 1), 1.0, 0.0).astype(BF16)
    here = dot(small[0], at_rows) + dot(small[1], at_rows) + dot(small[2], at_rows)
    row_c = dot(in_a, stacked(here[:GRID]))
    row_s = dot(in_a, stacked(here[GRID : 2 * GRID]))
    for j in range(3):
        rc, rs = row_c[:, j : j + 1], row_s[:, j : j + 1]
        wt[j, :, :L] = col_c * rc - col_s * rs
        wt[j, :, L:] = col_s * rc + col_c * rs

    drain(md.at[pl.ds(0, 31)], spread_recv.at[5])
    mine[2].wait()
    values = md[...].reshape(256, 128)
    orient = values[:, 0:1].astype(I32)
    prior = values[:, 1:2].astype(I32)
    values_t = values.T
    orient_row = values_t[0:1, :].astype(I32)
    ids = iota((256, 3 * PRIOR), 1) & 7
    in_cols = jnp.where((prior & 7) == ids, 1.0, 0.0).astype(BF16)
    in_rows = jnp.where((prior >> 3) == ids, 1.0, 0.0).astype(BF16)
    turn_c, turn_s = (dot(in_cols, parts_of(2 * GRID + PRIOR * n, PRIOR)) for n in range(2))
    row_turn_c, row_turn_s = (
        dot(in_rows, stacked(here[2 * GRID + PRIOR * n : 2 * GRID + PRIOR * n + PRIOR]))
        for n in range(2)
    )
    for j in range(3):
        rc, rs = row_turn_c[:, j : j + 1], row_turn_s[:, j : j + 1]
        tt[j, 0] = turn_c * rc - turn_s * rs
        tt[j, 1] = turn_c * rs + turn_s * rc

    drain(vbd.at[pl.ds(0, 3)], spread_recv.at[3])
    mine[0].wait()
    send_map(voll, vld, 4)
    first = 12 * img + 3 * x
    zid_row = plane_ids(iota((1, 192), 1), zh)
    zid_col = plane_ids(iota((192, 1), 0), zh)

    def picture(j, c):
        return xd[j, :, c].astype(F32).reshape(256, L)

    sc[...] = jnp.zeros_like(sc)

    def score(j, carry):
        drain(xd.at[j, pl.ds(0, 31)], spread_recv.at[j])
        pltpu.make_async_copy(xd.at[j, 0], xd.at[j, 0], own.at[j]).wait()
        pick = jnp.where(planes_of(orient, first + j) == zid_row, 1.0, 0.0).astype(BF16)
        sr, si = (
            dot(pick, jnp.concatenate([vbd[b, c, j] for b in range(4)], axis=0))
            for c in range(2)
        )
        xr, xi = picture(j, 0), picture(j, 1)
        tr, ti = tt[j, 0], tt[j, 1]
        rr, ii, ri, ir = xr * tr, xi * ti, xr * ti, xi * tr
        tr, ti = rr - ii, ri + ir
        tt[j, 0] = rr + ii
        tt[j, 1] = ir - ri
        lhs = jnp.concatenate([sr * tr + si * ti, si * tr - sr * ti], axis=1)
        sc[...] += dot_full(lhs, wt[j], NT).reshape(32, 8, 256)
        return carry

    lax.fori_loop(0, 3, score, 0)

    layer = yc * 4 + x

    def send_parts(k, carry):
        to = (layer + k) % 32
        remote(
            sc.at[to], parts.at[layer], post_send.at[0], post_recv.at[0],
            zl * 8 + to // 4, 2 * (to % 4) + zh,
        ).start()
        return carry

    lax.fori_loop(1, 32, send_parts, 0)
    parts[layer] = sc[layer]

    lane = iota((256, 192), 1)
    same = ((iota((256, 192), 0) ^ lane) & 15) == 0
    for j in range(3):
        wave_of = jnp.where((lane & 16) == 0, row_c[:, j : j + 1], row_s[:, j : j + 1])
        rt[j] = jnp.where(same, wave_of, 0.0)
    for k in range(3):
        cx, sx = (
            jnp.concatenate([tab[p, t, pl.ds(k, 128, stride=3), :] for t in range(3)], axis=1)
            for p in range(2)
        )
        for n, (left, right) in enumerate(((cx, -sx), (sx, cx))):
            for side, value in enumerate((left, right)):
                high, low = halves(value)
                exh[k, 128 * n : 128 * n + 128, L * side : L * side + L] = high
                exl[k, 128 * n : 128 * n + 128, L * side : L * side + L] = low

    for j in range(3):
        hit = jnp.where(planes_of(orient_row, first + j) == zid_col, 1.0, 0.0).astype(F32)
        puts[j] = hit.astype(BF16)
        share = 1.0 / (jnp.sum(hit, axis=1, keepdims=True) + 1.0)
        shares[j] = jnp.broadcast_to(share, (192, L))

    drain(parts.at[pl.ds(0, 31)], post_recv.at[0])
    sums[z] = jnp.sum(parts[...], axis=0)

    def send_sums(k, carry):
        to = (z + k) % 8
        remote(
            sums.at[z], sums.at[z], post_send.at[1], post_recv.at[1],
            to % 4 * 8 + yc, 2 * x + to // 4,
        ).start()
        return carry

    lax.fori_loop(1, 8, send_sums, 0)
    ct, st = whole(tab, 0), whole(tab, 1)
    lane = iota((L, 2 * L), 1)
    spot = lane % L
    is_re = jnp.logical_or(spot < 128, jnp.logical_and(spot >= 128, spot < 192))
    local = jnp.where(spot < 192, spot, jnp.where(spot < 256, spot - 64, spot - 256))
    kz = local + 48 * count(local, 48, 192) + 48 * (lane >= L).astype(I32)
    pick_z = jnp.where(iota((L, 2 * L), 0) == kz, 1.0, 0.0).astype(BF16)
    cth, ctl = halves(ct)
    sth, stl = halves(st)
    re_z = is_re[:1]
    for dst, c_part, s_part in ((ezh, cth, sth), (ezl, ctl, stl)):
        cz, sz = dot(c_part, pick_z), dot(s_part, pick_z)
        dst[:L] = jnp.where(re_z, cz, -sz).astype(BF16)
        dst[L:] = jnp.where(re_z, sz, cz).astype(BF16)
    drain(sums.at[pl.ds(0, 7)], post_recv.at[1])
    logits = jnp.sum(sums[...], axis=0) / (2.0 * md[layer][:, 2:3])
    expo = jnp.exp(logits - jnp.max(logits, axis=1, keepdims=True))
    w[layer] = expo / jnp.sum(expo, axis=1, keepdims=True)

    def send_weights(k, carry):
        to = (layer + k) % 32
        remote(
            w.at[layer], w.at[layer], post_send.at[2], post_recv.at[2],
            zl * 8 + to // 4, 2 * (to % 4) + zh,
        ).start()
        return carry

    lax.fori_loop(1, 32, send_weights, 0)
    lane = iota((L, L), 1)
    local = jnp.where(lane < 192, lane, lane - 192)
    ky = local + 12 * count(local, 12, 192) + 12 * core
    pick_y = jnp.where(iota((L, L), 0) == ky, 1.0, 0.0).astype(BF16)
    re_y = (lane < 192)[:1]
    for dst, c_part, s_part in ((eyh, cth, sth), (eyl, ctl, stl)):
        dst[...] = jnp.where(re_y, dot(c_part, pick_y), -dot(s_part, pick_y)).astype(BF16)
    drain(vld.at[pl.ds(0, 3)], spread_recv.at[4])
    mine[1].wait()
    drain(w.at[pl.ds(0, 31)], post_recv.at[2])

    def merge(j, carry):
        rows = dot_full(w[...].reshape(256, 256), rt[j])
        high, middle = halves(rows)
        low = (rows - high.astype(F32) - middle.astype(F32)).astype(BF16)
        group = iota((256, 192), 1) >> 5
        use_middle = jnp.logical_or(group == 2, group == 3)
        rows = jnp.where(use_middle, middle.astype(F32), high.astype(F32))
        rows = jnp.where(group == 5, low.astype(F32), rows).astype(BF16)
        f = dot(rows, cols[...])
        fr, fi = f[:, :L], f[:, L:]
        xr, xi = tt[j, 0], tt[j, 1]
        for c, part in enumerate((xr * fr + xi * fi, xi * fr - xr * fi)):
            back = dot(puts[j], part.astype(BF16))
            rows = jnp.concatenate(
                [vbd[b, c, j].astype(F32) + vld[b, c, j].astype(F32) for b in range(4)], axis=0
            )
            high, low = halves((back + rows) * shares[j])
            mh[j, :, L * c : L * c + L] = high
            ml[j, :, L * c : L * c + L] = low
        return carry

    lax.fori_loop(0, 3, merge, 0)

    def x_group(k, outer):
        def x_lines(j, carry):
            gx = dot_split(exh[k], exl[k], mh[j], ml[j], NT)
            re, im = gx[:128], gx[128:]
            tiles = (
                re[:, :128],
                jnp.concatenate([re[:, 128:], im[:, 128:]], axis=1),
                im[:, :128],
            )
            for t in range(3):
                lines[t, pl.ds(j, 128, stride=3), :] = tiles[t]
            return carry

        lax.fori_loop(0, 3, x_lines, 0)
        g[k, 0], g[k, 1] = pack([lines[t] for t in range(3)])
        land = r.at[k, pl.ds(2 * zh, 2), pl.ds(3 * (4 * q + x), 3)]

        def send_lines(n, carry):
            to = (me + n) % 128
            remote(
                g.at[k, :, pl.ds(3 * to, 3)], land,
                plane_send.at[k], plane_recv.at[k], 2 * (to // 8) + core, to % 8,
            ).start()
            return carry

        lax.fori_loop(1, 128, send_lines, 0)
        pltpu.make_async_copy(g.at[k, :, pl.ds(3 * me, 3)], land, own.at[6 + k]).start()
        return outer

    lax.fori_loop(0, 3, x_group, 0)

    to = 2 * q + slab // 4

    def deliver(k, across):
        place = out.at[3 * (slab % 4) + k]
        for half in range(2):
            n = 2 * half + (1 - zh if across else zh)
            here = jnp.logical_and(to == img, 4 * core + n == slab)

            @pl.when(here)
            def _(n=n):
                pltpu.make_async_copy(total.at[k, n], place, out_recv).start()

            @pl.when(jnp.logical_not(here))
            def _(n=n):
                remote(
                    total.at[k, n], place, out_send.at[n], out_recv, to, 4 * core + n
                ).start()

    def planes(k, outer):
        pltpu.make_async_copy(
            g.at[k, :, pl.ds(0, 3)], g.at[k, :, pl.ds(0, 3)], own.at[6 + k]
        ).wait()
        @pl.when(k == 2)
        def _():
            drain(g.at[2, :, pl.ds(0, 381)], plane_send.at[2])
            deliver(0, True)
            deliver(1, True)
            deliver(0, False)
            deliver(1, False)

        drain(g.at[k, :, pl.ds(0, 381)], plane_recv.at[k])
        columns = unpack(r[k, 0], r[k, 1]) + unpack(r[k, 2], r[k, 3])
        th, tl = halves(jnp.concatenate(columns, axis=1))
        u = dot_split(th, tl, ezh[...], ezl[...], NT)
        uh, ul = halves(jnp.concatenate([u[:, :L], u[:, L:]], axis=0))
        theirs, ours = pl.ds(192 * (1 - core), 192), pl.ds(192 * core, 192)
        d[k] = dot_split(eyh[theirs], eyl[theirs], uh, ul, NN).reshape(4, 48, L)
        swap = remote(
            d.at[k], other.at[k], swap_send.at[k], swap_recv.at[k], 2 * q + 1 - core, slab
        )
        swap.start()
        done = dot_split(eyh[ours], eyl[ours], uh, ul, NN)
        swap.wait()
        done = (done + other[k].reshape(192, L)) * SCALE
        words = pack([done[:, :128], done[:, 128:256], done[:, 256:]])
        for n in range(2):
            total[k, :, n] = words[n].reshape(4, 48, 128)

        @pl.when(k == 2)
        def _():
            deliver(2, True)
            deliver(2, False)

        return outer

    lax.fori_loop(0, 3, planes, 0)

    for j in range(3):
        drain(a.at[j, pl.ds(0, 31)], spread_send.at[j])
    drain(vbd.at[pl.ds(0, 3)], spread_send.at[3])
    drain(vld.at[pl.ds(0, 3)], spread_send.at[4])
    drain(md.at[pl.ds(0, 31)], spread_send.at[5])
    drain(parts.at[pl.ds(0, 31)], post_send.at[0])
    drain(sums.at[pl.ds(0, 7)], post_send.at[1])
    drain(w.at[pl.ds(0, 31)], post_send.at[2])
    for k in range(2):
        drain(g.at[k, :, pl.ds(0, 381)], plane_send.at[k])
    for n in range(4):
        here = jnp.logical_and(to == img, 4 * core + n == slab)

        @pl.when(jnp.logical_not(here))
        def _(n=n):
            drain(total.at[:, n], out_send.at[n])

    drain(out, out_recv)


def open_kernel(words, out):
    for n in range(4):
        one, two = (words[3 * n : 3 * n + 3, m].reshape(144, 128) for m in range(2))
        value = jnp.concatenate(unpack(one, two), axis=1)
        out[3 * n : 3 * n + 3] = value.reshape(3, 48, L)


ANY = pl.BlockSpec(memory_space=pl.ANY)
VMEM = pl.BlockSpec(memory_space=pltpu.VMEM)
DMA = pltpu.SemaphoreType.DMA


def per_device(images, volume, orient, prior_shift, noise_var):
    tab, small, cols = make_tables()
    vol = jnp.transpose(volume, (0, 2, 1, 3))
    buf = pltpu.VMEM
    scratch = [
        buf((8, 128), F32),
        buf((8, 2, L, L), BF16),
        buf((2, 12, 48, L), F32),
        buf((2, 3, L, 128), F32),
        buf((8, 2, 3, L, 128), F32),
        buf((2, 3, 256, 128), F32),
        buf((3, 32, 2, 8, L), BF16),
        buf((2, 12, 48, L), BF16),
        buf((2, 12, 48, L), BF16),
        buf((3, 32, 2, 8, L), BF16),
        buf((4, 2, 3, 48, L), BF16),
        buf((4, 2, 3, 48, L), BF16),
        buf((32, 8, 128), F32),
        buf((3, 2, 256, L), F32),
        buf((3, 256, 2 * L), F32),
        buf((3, 256, 2 * L), BF16),
        buf((3, 256, 2 * L), BF16),
        buf((2 * L, 2 * L), BF16),
        buf((2 * L, 2 * L), BF16),
        buf((L, L), BF16),
        buf((L, L), BF16),
        buf((3, 256, 192), F32),
        buf((3, 192, 256), BF16),
        buf((3, 192, L), F32),
        buf((32, 8, 256), F32),
        buf((32, 8, 256), F32),
        buf((8, 8, 256), F32),
        buf((32, 8, 256), F32),
        buf((3, 192, 2 * L), BF16),
        buf((3, 192, 2 * L), BF16),
        buf((3, L, 128), F32),
        buf((3, 2, L, 128), I32),
        buf((3, 4, 192, 128), I32),
        buf((3, 4, 48, L), F32),
        buf((3, 4, 48, L), F32),
        buf((3, 4, 2, 48, 128), I32),
        DMA((3,)),
        DMA((6,)),
        DMA((6,)),
        DMA((9,)),
        DMA((3,)),
        DMA((3,)),
        DMA((3,)),
        DMA((3,)),
        DMA((3,)),
        DMA((3,)),
        DMA((4,)),
        DMA(()),
    ]
    smem = pl.BlockSpec(memory_space=pltpu.SMEM)
    words = pl.pallas_call(
        kernel,
        out_shape=jax.ShapeDtypeStruct((12, 2, 48, 128), I32),
        in_specs=[ANY, ANY, smem, smem, smem, ANY, VMEM, VMEM],
        out_specs=VMEM,
        scratch_shapes=scratch,
        compiler_params=pltpu.CompilerParams(
            vmem_limit_bytes=VLIM, has_side_effects=True, collective_id=0
        ),
        name="step",
    )(images, vol, orient, prior_shift, noise_var, tab, small, cols)
    return pl.pallas_call(
        open_kernel,
        out_shape=jax.ShapeDtypeStruct((12, 48, L), F32),
        in_specs=[VMEM],
        out_specs=VMEM,
        name="open",
    )(words)


def solution(mesh):
    return jax.shard_map(
        per_device,
        mesh=mesh,
        in_specs=(
            P("img", None, None, None),
            P(None, "slab", "img", None),
            P("img"),
            P("img"),
            P("img"),
        ),
        out_specs=P("img", "slab", None),
        check_vma=False,
    )
```

```python
import math

import jax
import jax.numpy as jnp
import numpy as np
from jax import lax
from jax.experimental import pallas as pl
from jax.experimental.pallas import tpu as pltpu
from jax.sharding import PartitionSpec as P

GRID = 16
PRIOR = 8
NORIENT = 4096
L = 384
HALF = L // 2
SCALE = L ** (-1.5)
PRECISE = lax.Precision.HIGHEST
F32 = jnp.float32
BF16 = jnp.bfloat16
I32 = jnp.int32
VLIM = 62 * 1024 * 1024

NT = (((1,), (1,)), ((), ()))
NN = (((1,), (0,)), ((), ()))


def wave(product):
    angle = 2.0 * math.pi * np.mod(product, L) / L
    return np.cos(angle).astype(np.float32), np.sin(angle).astype(np.float32)


def thirds(a):
    high = a.astype(BF16)
    rest = a - high.astype(np.float32)
    middle = rest.astype(BF16)
    return high, middle, (rest - middle.astype(np.float32)).astype(BF16)


def make_tables():
    ids = np.arange(L)
    ct, st = wave(ids[:, None] * (ids[None, :] - HALF))
    shift = np.arange(PRIOR) - PRIOR // 2 - GRID // 2
    turns = wave(shift[:, None] * (ids[None, :] - HALF))
    small = thirds(np.concatenate([ct[:GRID], st[:GRID], turns[0], turns[1]], axis=0))
    cols = np.concatenate(
        [
            np.concatenate([ct[:GRID], st[:GRID]], axis=1),
            np.concatenate([-st[:GRID], ct[:GRID]], axis=1),
        ],
        axis=0,
    )
    high, middle, low = thirds(cols)
    cols = np.concatenate([high, middle, high, middle, low, high], axis=0)
    tiles = lambda a: np.ascontiguousarray(a.reshape(L, 3, 128).transpose(1, 0, 2))
    return np.stack([tiles(ct), tiles(st)]), np.stack(small), cols


def remote(src, dst, send, recv, img, slab):
    return pltpu.make_async_remote_copy(
        src_ref=src,
        dst_ref=dst,
        send_sem=send,
        recv_sem=recv,
        device_id={"img": img, "slab": slab},
        device_id_type=pl.DeviceIdType.MESH,
    )


def drain(ref, sem):
    pltpu.make_async_copy(ref, ref, sem).wait()


def dot(a, b, dims=NN):
    return lax.dot_general(a, b, dims, preferred_element_type=F32)


def dot_full(a, b, dims=NN):
    return lax.dot_general(a, b, dims, precision=PRECISE, preferred_element_type=F32)


def halves(a):
    high = a.astype(BF16)
    return high, (a - high.astype(F32)).astype(BF16)


def dot_split(ah, al, bh, bl, dims):
    return dot(ah, bh, dims) + (dot(ah, bl, dims) + dot(al, bh, dims))


def iota(shape, axis):
    return lax.broadcasted_iota(I32, shape, axis)


def count(index, step, top):
    total = jnp.zeros_like(index)
    for edge in range(step, top, step):
        total += (index >= edge).astype(I32)
    return total


def plane_ids(index, zh):
    return index + 48 * count(index, 48, 192) + 48 * zh


def planes_of(orient, row):
    return (((row - HALF) * (orient - NORIENT // 2)) >> 11) + HALF


def power(n):
    total = jnp.ones(n.shape, F32)
    for bit in range(7):
        total *= jnp.where((n >> bit) & 1 == 1, 2.0 ** (2**bit), 1.0)
    return total


def pack(tiles):
    peak = jnp.maximum(jnp.maximum(jnp.abs(tiles[0]), jnp.abs(tiles[1])), jnp.abs(tiles[2]))
    peak = jnp.maximum(jnp.max(peak, axis=1, keepdims=True), 1e-30)
    level = jnp.ceil(jnp.log(peak) * (1.0 / math.log(2.0)) + 0.01)
    level = jnp.clip(level, -100.0, 20.0).astype(I32) + 101
    gain = power(121 - level)
    q0, q1, q2 = (jnp.floor(tile * gain + 0.5).astype(I32) for tile in tiles)
    flag = (level >> (iota(tiles[0].shape, 1) & 31)) & 1
    return (q0 << 11) | ((q2 >> 10) & 2047), (q1 << 11) | ((q2 & 1023) << 1) | flag


def unpack(one, two):
    lane = iota(one.shape, 1)
    flag = jnp.where(lane < 8, (two & 1) << (lane & 7), 0).astype(F32)
    level = jnp.sum(flag, axis=1, keepdims=True).astype(I32)
    gain = power(level) * 2.0**-121
    third = ((one & 2047) << 10) | ((two >> 1) & 1023)
    return [v.astype(F32) * gain for v in (one >> 11, two >> 11, (third << 11) >> 11)]


def whole(tab, part):
    return jnp.concatenate([tab[part, n] for n in range(3)], axis=1)


def kernel(
    img_in, vol_in, orient_in, prior_in, noise_in, tab_in, small, cols,
    out,
    meta, pics, vol, tab, strip, strips, a, volb, voll, xd, vbd, vld, md, tt, wt,
    exh, exl, ezh, ezl, eyh, eyl, rt, puts, shares, sc, parts, sums, w, mh, ml, lines, g, r, d, other, total,
    load, spread_send, spread_recv, own, post_send, post_recv,
    plane_send, plane_recv, swap_send, swap_recv, out_send, out_recv,
):
    img = lax.axis_index("img")
    slab = lax.axis_index("slab")
    zl, x, zh = img // 8, slab // 2, slab % 2
    q, core, yc = img // 2, img % 2, img % 8
    z = zh * 4 + zl
    me = q * 8 + slab

    loads = [
        pltpu.make_async_copy(src, dst, load.at[n])
        for n, (src, dst) in enumerate(((vol_in, vol), (img_in, pics), (tab_in, tab)))
    ]
    for copy in loads:
        copy.start()

    barrier = pltpu.get_barrier_semaphore()
    for turn in (2, 6, 1, 7, 0):
        to_z = (z + turn) % 8

        def greet(k, carry, to_z=to_z):
            pl.semaphore_signal(
                barrier,
                inc=1,
                device_id={"img": to_z % 4 * 8 + (yc + k) % 8, "slab": 2 * x + to_z // 4},
                device_id_type=pl.DeviceIdType.MESH,
            )
            return carry

        lax.fori_loop(1 if turn == 0 else 0, 8, greet, 0)
    for k in range(1, 4):
        pl.semaphore_signal(
            barrier,
            inc=1,
            device_id={"img": img, "slab": 2 * ((x + k) % 4) + zh},
            device_id_type=pl.DeviceIdType.MESH,
        )

    entry, item = iota((8, 128), 0), iota((8, 128), 1)
    facts = jnp.zeros((8, 128), F32)
    for n in range(8):
        for m, ref in enumerate((orient_in, prior_in, noise_in)):
            here = jnp.logical_and(entry == n, item == m)
            facts = jnp.where(here, ref[n].astype(F32), facts)
    meta[...] = facts

    loads[0].wait()
    for c in range(2):

        def cast(j, carry, c=c):
            volb[c, j], voll[c, j] = halves(vol[c, j])
            return carry

        lax.fori_loop(0, 12, cast, 0)
    loads[1].wait()

    def widen(n, carry):
        for c in range(2):
            for t in range(3):
                strip[n, c, t] = pics[n, c, :, 128 * t : 128 * t + 128].astype(F32)
        return carry

    lax.fori_loop(0, 8, widen, 0)

    def sort_images(j, carry):
        def gather(n, inner):
            for c in range(2):
                for t in range(3):
                    strips[c, t, pl.ds(n, 32, stride=8), :] = strip[
                        n, c, t, pl.ds(3 * x + j, 32, stride=12), :
                    ]
            return inner

        lax.fori_loop(0, 8, gather, 0)
        for c in range(2):
            rows = jnp.concatenate([strips[c, t] for t in range(3)], axis=1)
            a[j, :, c] = rows.reshape(32, 8, L).astype(BF16)
        return carry

    pl.semaphore_wait(barrier, 42)

    def send_map(src, dst, n):
        for k in range(1, 4):
            to = (x + k) % 4
            remote(
                src.at[:, pl.ds(3 * to, 3)], dst.at[x],
                spread_send.at[n], spread_recv.at[n], img, 2 * to + zh,
            ).start()

    def send_images(j, carry):
        for turn in (2, 6, 1, 7, 0):
            to_z = (z + turn) % 8

            def spread(k, inner, turn=turn, to_z=to_z):
                to = (to_z % 4) * 8 + (yc + k) % 8
                to_slab = 2 * x + to_z // 4
                if turn in (2, 6):
                    c = 0 if turn == 2 else 1
                    src, dst = a.at[j, to, c], xd.at[j, img, c]
                else:
                    src, dst = a.at[j, to], xd.at[j, img]
                remote(src, dst, spread_send.at[j], spread_recv.at[j], to, to_slab).start()
                return inner

            lax.fori_loop(1 if turn == 0 else 0, 8, spread, 0)
        pltpu.make_async_copy(a.at[j, img], xd.at[j, img], own.at[j]).start()
        return carry

    send_map(volb, vbd, 3)
    for turn in (2, 1, 7, 0):
        to_z = (z + turn) % 8

        def send_meta(k, carry, to_z=to_z):
            to = (to_z % 4) * 8 + (yc + k) % 8
            remote(
                meta, md.at[img], spread_send.at[5], spread_recv.at[5], to, 2 * x + to_z // 4
            ).start()
            return carry

        lax.fori_loop(1 if turn == 0 else 0, 8, send_meta, 0)
    def next_images(j, carry):
        return send_images(j, sort_images(j, carry))

    lax.fori_loop(0, 3, next_images, 0)
    mine = [
        pltpu.make_async_copy(src, dst, own.at[3 + n])
        for n, (src, dst) in enumerate(
            (
                (volb.at[:, pl.ds(3 * x, 3)], vbd.at[x]),
                (voll.at[:, pl.ds(3 * x, 3)], vld.at[x]),
                (meta, md.at[img]),
            )
        )
    ]
    for copy in mine:
        copy.start()

    loads[2].wait()
    cell = iota((256, 3 * GRID), 0)
    step = iota((256, 3 * GRID), 1) & 15
    in_b = jnp.where((cell & 15) == step, 1.0, 0.0).astype(BF16)
    in_a = jnp.where((cell >> 4) == step, 1.0, 0.0).astype(BF16)

    def parts_of(first, size):
        return jnp.concatenate([small[n, first : first + size] for n in range(3)], axis=0)

    def stacked(a):
        high, middle = halves(a)
        low = (a - high.astype(F32) - middle.astype(F32)).astype(BF16)
        return jnp.concatenate([high, middle, low], axis=0)

    col_c, col_s = dot(in_b, parts_of(0, GRID)), dot(in_b, parts_of(GRID, GRID))
    row_ids = iota((L, 128), 0)
    at_rows = jnp.where(row_ids == 12 * img + 3 * x + iota((L, 128), 1), 1.0, 0.0).astype(BF16)
    here = dot(small[0], at_rows) + dot(small[1], at_rows) + dot(small[2], at_rows)
    row_c = dot(in_a, stacked(here[:GRID]))
    row_s = dot(in_a, stacked(here[GRID : 2 * GRID]))
    for j in range(3):
        rc, rs = row_c[:, j : j + 1], row_s[:, j : j + 1]
        wt[j, :, :L] = col_c * rc - col_s * rs
        wt[j, :, L:] = col_s * rc + col_c * rs

    drain(md.at[pl.ds(0, 31)], spread_recv.at[5])
    mine[2].wait()
    values = md[...].reshape(256, 128)
    orient = values[:, 0:1].astype(I32)
    prior = values[:, 1:2].astype(I32)
    values_t = values.T
    orient_row = values_t[0:1, :].astype(I32)
    ids = iota((256, 3 * PRIOR), 1) & 7
    in_cols = jnp.where((prior & 7) == ids, 1.0, 0.0).astype(BF16)
    in_rows = jnp.where((prior >> 3) == ids, 1.0, 0.0).astype(BF16)
    turn_c, turn_s = (dot(in_cols, parts_of(2 * GRID + PRIOR * n, PRIOR)) for n in range(2))
    row_turn_c, row_turn_s = (
        dot(in_rows, stacked(here[2 * GRID + PRIOR * n : 2 * GRID + PRIOR * n + PRIOR]))
        for n in range(2)
    )
    for j in range(3):
        rc, rs = row_turn_c[:, j : j + 1], row_turn_s[:, j : j + 1]
        tt[j, 0] = turn_c * rc - turn_s * rs
        tt[j, 1] = turn_c * rs + turn_s * rc

    drain(vbd.at[pl.ds(0, 3)], spread_recv.at[3])
    mine[0].wait()
    send_map(voll, vld, 4)
    first = 12 * img + 3 * x
    zid_row = plane_ids(iota((1, 192), 1), zh)
    zid_col = plane_ids(iota((192, 1), 0), zh)

    def picture(j, c):
        return xd[j, :, c].astype(F32).reshape(256, L)

    sc[...] = jnp.zeros_like(sc)

    def score(j, carry):
        drain(xd.at[j, pl.ds(0, 31)], spread_recv.at[j])
        pltpu.make_async_copy(xd.at[j, 0], xd.at[j, 0], own.at[j]).wait()
        pick = jnp.where(planes_of(orient, first + j) == zid_row, 1.0, 0.0).astype(BF16)
        sr, si = (
            dot(pick, jnp.concatenate([vbd[b, c, j] for b in range(4)], axis=0))
            for c in range(2)
        )
        xr, xi = picture(j, 0), picture(j, 1)
        tr, ti = tt[j, 0], tt[j, 1]
        rr, ii, ri, ir = xr * tr, xi * ti, xr * ti, xi * tr
        tr, ti = rr - ii, ri + ir
        tt[j, 0] = rr + ii
        tt[j, 1] = ir - ri
        lhs = jnp.concatenate([sr * tr + si * ti, si * tr - sr * ti], axis=1)
        sc[...] += dot_full(lhs, wt[j], NT).reshape(32, 8, 256)
        return carry

    lax.fori_loop(0, 3, score, 0)

    layer = yc * 4 + x

    def send_parts(k, carry):
        to = (layer + k) % 32
        remote(
            sc.at[to], parts.at[layer], post_send.at[0], post_recv.at[0],
            zl * 8 + to // 4, 2 * (to % 4) + zh,
        ).start()
        return carry

    lax.fori_loop(1, 32, send_parts, 0)
    parts[layer] = sc[layer]

    lane = iota((256, 192), 1)
    same = ((iota((256, 192), 0) ^ lane) & 15) == 0
    for j in range(3):
        wave_of = jnp.where((lane & 16) == 0, row_c[:, j : j + 1], row_s[:, j : j + 1])
        rt[j] = jnp.where(same, wave_of, 0.0)
    for k in range(3):
        cx, sx = (
            jnp.concatenate([tab[p, t, pl.ds(k, 128, stride=3), :] for t in range(3)], axis=1)
            for p in range(2)
        )
        for n, (left, right) in enumerate(((cx, -sx), (sx, cx))):
            for side, value in enumerate((left, right)):
                high, low = halves(value)
                exh[k, 128 * n : 128 * n + 128, L * side : L * side + L] = high
                exl[k, 128 * n : 128 * n + 128, L * side : L * side + L] = low

    for j in range(3):
        hit = jnp.where(planes_of(orient_row, first + j) == zid_col, 1.0, 0.0).astype(F32)
        puts[j] = hit.astype(BF16)
        share = 1.0 / (jnp.sum(hit, axis=1, keepdims=True) + 1.0)
        shares[j] = jnp.broadcast_to(share, (192, L))

    drain(parts.at[pl.ds(0, 31)], post_recv.at[0])
    sums[z] = jnp.sum(parts[...], axis=0)

    def send_sums(k, carry):
        to = (z + k) % 8
        remote(
            sums.at[z], sums.at[z], post_send.at[1], post_recv.at[1],
            to % 4 * 8 + yc, 2 * x + to // 4,
        ).start()
        return carry

    lax.fori_loop(1, 8, send_sums, 0)
    ct, st = whole(tab, 0), whole(tab, 1)
    lane = iota((L, 2 * L), 1)
    spot = lane % L
    is_re = jnp.logical_or(spot < 128, jnp.logical_and(spot >= 128, spot < 192))
    local = jnp.where(spot < 192, spot, jnp.where(spot < 256, spot - 64, spot - 256))
    kz = local + 48 * count(local, 48, 192) + 48 * (lane >= L).astype(I32)
    pick_z = jnp.where(iota((L, 2 * L), 0) == kz, 1.0, 0.0).astype(BF16)
    cth, ctl = halves(ct)
    sth, stl = halves(st)
    re_z = is_re[:1]
    for dst, c_part, s_part in ((ezh, cth, sth), (ezl, ctl, stl)):
        cz, sz = dot(c_part, pick_z), dot(s_part, pick_z)
        dst[:L] = jnp.where(re_z, cz, -sz).astype(BF16)
        dst[L:] = jnp.where(re_z, sz, cz).astype(BF16)
    drain(sums.at[pl.ds(0, 7)], post_recv.at[1])
    logits = jnp.sum(sums[...], axis=0) / (2.0 * md[layer][:, 2:3])
    expo = jnp.exp(logits - jnp.max(logits, axis=1, keepdims=True))
    w[layer] = expo / jnp.sum(expo, axis=1, keepdims=True)

    def send_weights(k, carry):
        to = (layer + k) % 32
        remote(
            w.at[layer], w.at[layer], post_send.at[2], post_recv.at[2],
            zl * 8 + to // 4, 2 * (to % 4) + zh,
        ).start()
        return carry

    lax.fori_loop(1, 32, send_weights, 0)
    lane = iota((L, L), 1)
    local = jnp.where(lane < 192, lane, lane - 192)
    ky = local + 12 * count(local, 12, 192) + 12 * core
    pick_y = jnp.where(iota((L, L), 0) == ky, 1.0, 0.0).astype(BF16)
    re_y = (lane < 192)[:1]
    for dst, c_part, s_part in ((eyh, cth, sth), (eyl, ctl, stl)):
        dst[...] = jnp.where(re_y, dot(c_part, pick_y), -dot(s_part, pick_y)).astype(BF16)
    drain(vld.at[pl.ds(0, 3)], spread_recv.at[4])
    mine[1].wait()
    drain(w.at[pl.ds(0, 31)], post_recv.at[2])

    def merge(j, carry):
        rows = dot_full(w[...].reshape(256, 256), rt[j])
        high, middle = halves(rows)
        low = (rows - high.astype(F32) - middle.astype(F32)).astype(BF16)
        group = iota((256, 192), 1) >> 5
        use_middle = jnp.logical_or(group == 2, group == 3)
        rows = jnp.where(use_middle, middle.astype(F32), high.astype(F32))
        rows = jnp.where(group == 5, low.astype(F32), rows).astype(BF16)
        f = dot(rows, cols[...])
        fr, fi = f[:, :L], f[:, L:]
        xr, xi = tt[j, 0], tt[j, 1]
        for c, part in enumerate((xr * fr + xi * fi, xi * fr - xr * fi)):
            back = dot(puts[j], part.astype(BF16))
            rows = jnp.concatenate(
                [vbd[b, c, j].astype(F32) + vld[b, c, j].astype(F32) for b in range(4)], axis=0
            )
            high, low = halves((back + rows) * shares[j])
            mh[j, :, L * c : L * c + L] = high
            ml[j, :, L * c : L * c + L] = low
        return carry

    lax.fori_loop(0, 3, merge, 0)

    for k in range(3):

        def x_lines(j, carry, k=k):
            gx = dot_split(exh[k], exl[k], mh[j], ml[j], NT)
            re, im = gx[:128], gx[128:]
            tiles = (
                re[:, :128],
                jnp.concatenate([re[:, 128:], im[:, 128:]], axis=1),
                im[:, :128],
            )
            for t in range(3):
                lines[t, pl.ds(j, 128, stride=3), :] = tiles[t]
            return carry

        lax.fori_loop(0, 3, x_lines, 0)
        g[k, 0], g[k, 1] = pack([lines[t] for t in range(3)])
        land = r.at[k, pl.ds(2 * zh, 2), pl.ds(3 * (4 * q + x), 3)]

        def send_lines(n, carry, k=k, land=land):
            to = (me + n) % 128
            remote(
                g.at[k, :, pl.ds(3 * to, 3)], land,
                plane_send.at[k], plane_recv.at[k], 2 * (to // 8) + core, to % 8,
            ).start()
            return carry

        lax.fori_loop(1, 128, send_lines, 0)
        pltpu.make_async_copy(g.at[k, :, pl.ds(3 * me, 3)], land, own.at[6 + k]).start()

    to = 2 * q + slab // 4

    def deliver(k, across):
        place = out.at[3 * (slab % 4) + k]
        for half in range(2):
            n = 2 * half + (1 - zh if across else zh)
            here = jnp.logical_and(to == img, 4 * core + n == slab)

            @pl.when(here)
            def _(n=n):
                pltpu.make_async_copy(total.at[k, n], place, out_recv).start()

            @pl.when(jnp.logical_not(here))
            def _(n=n):
                remote(
                    total.at[k, n], place, out_send.at[n], out_recv, to, 4 * core + n
                ).start()

    for k in range(3):
        pltpu.make_async_copy(
            g.at[k, :, pl.ds(0, 3)], g.at[k, :, pl.ds(0, 3)], own.at[6 + k]
        ).wait()
        if k == 2:
            drain(g.at[k, :, pl.ds(0, 381)], plane_send.at[k])
            deliver(0, True)
            deliver(1, True)
            deliver(0, False)
            deliver(1, False)
        drain(g.at[k, :, pl.ds(0, 381)], plane_recv.at[k])
        columns = unpack(r[k, 0], r[k, 1]) + unpack(r[k, 2], r[k, 3])
        th, tl = halves(jnp.concatenate(columns, axis=1))
        u = dot_split(th, tl, ezh[...], ezl[...], NT)
        uh, ul = halves(jnp.concatenate([u[:, :L], u[:, L:]], axis=0))
        theirs, ours = pl.ds(192 * (1 - core), 192), pl.ds(192 * core, 192)
        d[k] = dot_split(eyh[theirs], eyl[theirs], uh, ul, NN).reshape(4, 48, L)
        swap = remote(
            d.at[k], other.at[k], swap_send.at[k], swap_recv.at[k], 2 * q + 1 - core, slab
        )
        swap.start()
        done = dot_split(eyh[ours], eyl[ours], uh, ul, NN)
        swap.wait()
        done = (done + other[k].reshape(192, L)) * SCALE
        words = pack([done[:, :128], done[:, 128:256], done[:, 256:]])
        for n in range(2):
            total[k, :, n] = words[n].reshape(4, 48, 128)
        if k == 2:
            deliver(2, True)
            deliver(2, False)

    for j in range(3):
        drain(a.at[j, pl.ds(0, 31)], spread_send.at[j])
    drain(vbd.at[pl.ds(0, 3)], spread_send.at[3])
    drain(vld.at[pl.ds(0, 3)], spread_send.at[4])
    drain(md.at[pl.ds(0, 31)], spread_send.at[5])
    drain(parts.at[pl.ds(0, 31)], post_send.at[0])
    drain(sums.at[pl.ds(0, 7)], post_send.at[1])
    drain(w.at[pl.ds(0, 31)], post_send.at[2])
    for k in range(2):
        drain(g.at[k, :, pl.ds(0, 381)], plane_send.at[k])
    for n in range(4):
        here = jnp.logical_and(to == img, 4 * core + n == slab)

        @pl.when(jnp.logical_not(here))
        def _(n=n):
            drain(total.at[:, n], out_send.at[n])

    drain(out, out_recv)


def open_kernel(words, out):
    for n in range(4):
        one, two = (words[3 * n : 3 * n + 3, m].reshape(144, 128) for m in range(2))
        value = jnp.concatenate(unpack(one, two), axis=1)
        out[3 * n : 3 * n + 3] = value.reshape(3, 48, L)


ANY = pl.BlockSpec(memory_space=pl.ANY)
VMEM = pl.BlockSpec(memory_space=pltpu.VMEM)
DMA = pltpu.SemaphoreType.DMA


def per_device(images, volume, orient, prior_shift, noise_var):
    tab, small, cols = make_tables()
    vol = jnp.transpose(volume, (0, 2, 1, 3))
    buf = pltpu.VMEM
    scratch = [
        buf((8, 128), F32),
        buf((8, 2, L, L), BF16),
        buf((2, 12, 48, L), F32),
        buf((2, 3, L, 128), F32),
        buf((8, 2, 3, L, 128), F32),
        buf((2, 3, 256, 128), F32),
        buf((3, 32, 2, 8, L), BF16),
        buf((2, 12, 48, L), BF16),
        buf((2, 12, 48, L), BF16),
        buf((3, 32, 2, 8, L), BF16),
        buf((4, 2, 3, 48, L), BF16),
        buf((4, 2, 3, 48, L), BF16),
        buf((32, 8, 128), F32),
        buf((3, 2, 256, L), F32),
        buf((3, 256, 2 * L), F32),
        buf((3, 256, 2 * L), BF16),
        buf((3, 256, 2 * L), BF16),
        buf((2 * L, 2 * L), BF16),
        buf((2 * L, 2 * L), BF16),
        buf((L, L), BF16),
        buf((L, L), BF16),
        buf((3, 256, 192), F32),
        buf((3, 192, 256), BF16),
        buf((3, 192, L), F32),
        buf((32, 8, 256), F32),
        buf((32, 8, 256), F32),
        buf((8, 8, 256), F32),
        buf((32, 8, 256), F32),
        buf((3, 192, 2 * L), BF16),
        buf((3, 192, 2 * L), BF16),
        buf((3, L, 128), F32),
        buf((3, 2, L, 128), I32),
        buf((3, 4, 192, 128), I32),
        buf((3, 4, 48, L), F32),
        buf((3, 4, 48, L), F32),
        buf((3, 4, 2, 48, 128), I32),
        DMA((3,)),
        DMA((6,)),
        DMA((6,)),
        DMA((9,)),
        DMA((3,)),
        DMA((3,)),
        DMA((3,)),
        DMA((3,)),
        DMA((3,)),
        DMA((3,)),
        DMA((4,)),
        DMA(()),
    ]
    smem = pl.BlockSpec(memory_space=pltpu.SMEM)
    words = pl.pallas_call(
        kernel,
        out_shape=jax.ShapeDtypeStruct((12, 2, 48, 128), I32),
        in_specs=[ANY, ANY, smem, smem, smem, ANY, VMEM, VMEM],
        out_specs=ANY,
        scratch_shapes=scratch,
        compiler_params=pltpu.CompilerParams(
            vmem_limit_bytes=VLIM, has_side_effects=True, collective_id=0
        ),
        name="step",
    )(images, vol, orient, prior_shift, noise_var, tab, small, cols)
    return pl.pallas_call(
        open_kernel,
        out_shape=jax.ShapeDtypeStruct((12, 48, L), F32),
        in_specs=[VMEM],
        out_specs=VMEM,
        name="open",
    )(words)


def solution(mesh):
    return jax.shard_map(
        per_device,
        mesh=mesh,
        in_specs=(
            P("img", None, None, None),
            P(None, "slab", "img", None),
            P("img"),
            P("img"),
            P("img"),
        ),
        out_specs=P("img", "slab", None),
        check_vma=False,
    )
```
